32 devices in a mesh: dp: 2 (over y), group: 4 (over x, core), tensor: 4 (over z).
Axes of the slice: x: 2, y: 2, z: 4, core: 2. Of those that a mesh axis runs over, the one named last changes fastest.
Arguments:
- inputs: bfloat16 [16384, 1024], P(('dp', 'group', 'tensor')), may hold values from -6 to 6
- segments: int32 [8, 2048], P(('dp', 'group')), may hold values from 0 to 15, never falling along the last dimension, each value on 1 to 1024 neighbouring positions
- gain_attn: float32 [1024], replicated, may hold values from 0.25 to 1.75
- w_query: bfloat16 [1024, 1024], P(None, 'tensor'), may hold values from -0.046875 to 0.046875
- w_key: bfloat16 [1024, 1024], P(None, 'tensor'), may hold values from -0.1875 to 0.1875
- w_value: bfloat16 [1024, 1024], P(None, 'tensor'), may hold values from -0.1875 to 0.1875
- w_out: bfloat16 [1024, 1024], P('tensor'), may hold values from -0.75 to 0.75
- bias_table: float32 [32, 16], P(None, 'tensor'), may hold values from -3 to 3
- gain_ffn: float32 [1024], replicated, may hold values from 0.25 to 1.75
- w_in: bfloat16 [1024, 4096], P(None, 'tensor'), may hold values from -0.1875 to 0.1875
- w_back: bfloat16 [4096, 1024], P('tensor'), may hold values from -0.09375 to 0.09375
- cotangent: bfloat16 [16384, 1024], P(('dp', 'group', 'tensor')), may hold values from -6 to 6
Outputs:
- output: float32 [16384, 1024], P(('dp', 'group', 'tensor'))
- grad_inputs: float32 [16384, 1024], P(('dp', 'group', 'tensor'))
- grad_gain_attn: float32 [1024], replicated
- grad_w_query: float32 [1024, 1024], P('dp', 'tensor')
- grad_w_key: float32 [1024, 1024], P('dp', 'tensor')
- grad_w_value: float32 [1024, 1024], P('dp', 'tensor')
- grad_w_out: float32 [1024, 1024], P('tensor', 'dp')
- grad_bias_table: float32 [32, 16], P('dp', 'tensor')
- grad_gain_ffn: float32 [1024], replicated
- grad_w_in: float32 [1024, 4096], P('dp', 'tensor')
- grad_w_back: float32 [4096, 1024], P('tensor', 'dp')
The draws below stay inside these ranges and needn't reach their ends.
Inputs may be any that keep to these rules, and one draw needn't show every extreme that they name: `segments`: in each packed sequence the document numbers never fall; a document covers at most 1024 positions, and some document covers exactly that many.
All inputs are finite; a program needn't handle non-finite values.
Results may differ from the reference program's by a relative error of at most 0.02.
Values may be sent and summed in bfloat16 or wider, within the bound.
No kernel may reach another device: no remote copies, remote signals or barrier semaphores. Data moves between devices by JAX's collectives and lax.ppermute only.
A program may use at most 192 MiB of HBM per device.

```python
import math
import jax
import jax.numpy as jnp
import numpy as np
from jax import lax

D = 1024
HEADS = 16
HEAD = 64
FF = 4096
BUCKETS = 32
SEQ_LEN = 2048
BLK = 512
NSEQ = 8
TOKENS = 16384


def draw_cotangent(key, part):
    position = jnp.arange(TOKENS, dtype=jnp.float32) / max(TOKENS - 1, 1)
    entries = jnp.clip(jax.random.normal(key, (TOKENS, D), jnp.float32), -2.5, 2.5)
    row_scale = 1.0 + 1.4 * position
    return (entries * row_scale[:, None]).astype(jnp.bfloat16)


def steps_of(own_key, dims, cuts, least, top_value):
    factor_of = 1.0
    for dim, blocks in cuts:
        steps = jax.random.uniform(jax.random.fold_in(jax.random.fold_in(own_key, 6), dim), (blocks,), jnp.float32, least / len(cuts), top_value / len(cuts))
        factor_of = factor_of * jnp.repeat(jnp.exp(steps), dims[dim] // blocks).reshape((-1,) + (1,) * (len(dims) - 1 - dim))
    return factor_of


def split_up(count, total, limit, slope):
    loads = [(1 << 20) // math.isqrt(grade ** slope) + 1 for grade in range(2, count + 1)]
    spare, holding = total - limit - (count - 1), [1] * (count - 1)
    while spare > 0:
        candidates = [i for i in range(count - 1) if holding[i] < limit]
        pool, budget = sum([loads[i] for i in candidates]), spare
        for i in candidates:
            extra = min(limit - holding[i], max(1, budget * loads[i] // pool), spare)
            holding[i] = holding[i] + extra
            spare = spare - extra
    return np.array([limit] + holding)


def ragged(key, number_of, total, limit, lean):
    if number_of == 2:
        one = jax.random.randint(key, (), max(1, total - limit), min(limit, total - 1) + 1)
        return jnp.stack([one, total - one])
    lengths = jnp.asarray(split_up(number_of, total, limit, lean), jnp.int32)
    twos = (number_of - 1) // 2
    donor, taker = lengths[1:1 + 2 * twos:2], lengths[2:2 + 2 * twos:2]
    margin = jnp.minimum(donor - 1, limit - taker)
    moved = jax.random.randint(jax.random.fold_in(key, 1), (twos,), 0, 1 << 20) % (margin + 1)
    lengths = lengths.at[1:1 + 2 * twos:2].set(donor - moved).at[2:2 + 2 * twos:2].set(taker + moved)
    return lengths[jax.random.permutation(jax.random.fold_in(key, 2), number_of)]


def bell_draw(own_key, shape, spread, bound, cuts=(), kind=jnp.bfloat16):
    gain = steps_of(own_key, shape, cuts, -0.22, 0.18) if cuts else 1.0
    values = jax.random.normal(own_key, shape, jnp.float32) * spread * gain
    return jnp.minimum(jnp.maximum(values, -bound), bound).astype(kind)


def setup_inputs(seed: int = 0) -> dict:
    key_list = jax.random.split(jax.random.key(seed), 13)
    return {
        "inputs": bell_draw(key_list[0], (TOKENS, D), 1.0, 6.0, ((0, 32),)),
        "segments": jax.vmap(lambda own: jnp.searchsorted(jnp.cumsum(ragged(own, max(SEQ_LEN // 128, 4), SEQ_LEN, SEQ_LEN // 2, 2)), jnp.arange(SEQ_LEN), side="right"))(jax.random.split(key_list[1], NSEQ)).reshape((NSEQ, SEQ_LEN)).astype(jnp.int32),
        "gain_attn": jnp.clip(1.0 + 0.15 * jax.random.normal(key_list[2], (D,), jnp.float32), 0.25, 1.75),
        "w_query": bell_draw(key_list[3], (D, HEADS * HEAD), (16 * D) ** -0.5, 0.046875, ((1, 4),)),
        "w_key": bell_draw(key_list[4], (D, HEADS * HEAD), D ** -0.5, 0.1875, ((1, 4),)),
        "w_value": bell_draw(key_list[5], (D, HEADS * HEAD), D ** -0.5, 0.1875, ((1, 4),)),
        "w_out": bell_draw(key_list[6], (HEADS * HEAD, D), (HEADS * HEAD // 16) ** -0.5, 0.75, ((0, 4),)),
        "bias_table": bell_draw(key_list[7], (BUCKETS, HEADS), 1.0, 3.0, ((1, 4),), jnp.float32),
        "gain_ffn": jnp.clip(1.0 + 0.15 * jax.random.normal(key_list[8], (D,), jnp.float32), 0.25, 1.75),
        "w_in": bell_draw(key_list[9], (D, FF), D ** -0.5, 0.1875, ((1, 4),)),
        "w_back": bell_draw(key_list[10], (FF, D), FF ** -0.5, 0.09375, ((0, 4),)),
        "cotangent": draw_cotangent(jax.random.fold_in(key_list[12], 71), 0),
    }


@jax.custom_vjp
def low(v):
    return lax.optimization_barrier(v.astype(jnp.bfloat16)).astype(jnp.float32)

@jax.custom_vjp
def low_back(v):
    return v

def low_keep(v):
    return (low(v), None)

def low_pass(kept, grad):
    return (grad,)

def back_keep(v):
    return (v, None)

def back_low(kept, grad):
    return (low(grad),)
low.defvjp(low_keep, low_pass)
low_back.defvjp(back_keep, back_low)
EPSILON = 1e-06
MASKED = -1e+30
reach_marks = (12, 16, 23, 32, 46, 64, 91)

def bucket_of(offset):
    offset = offset.astype(jnp.int32)
    distance = jnp.abs(offset).astype(jnp.int32)
    far_bucket = jnp.full(offset.shape, 8, jnp.int32)
    for threshold in reach_marks:
        far_bucket = far_bucket + (distance >= threshold).astype(jnp.int32)
    near_far = jnp.where(distance < 8, distance, far_bucket).astype(jnp.int32)
    return (16 * (offset > 0).astype(jnp.int32) + near_far).astype(jnp.int32)

def normalize(stream, gain_row):
    inv_scale = lax.rsqrt(lax.optimization_barrier(jnp.mean(stream * stream, axis=-1, keepdims=True)) + EPSILON)
    return stream * inv_scale * gain_row

def product(left_side, right_side):
    return jnp.dot(left_side, right_side, precision=lax.Precision.HIGHEST, preferred_element_type=jnp.float32)

def attention(queries, all_keys, values, segment_row, bias_table):
    positions = jnp.arange(SEQ_LEN, dtype=jnp.int32)

    def block_rows(query_start):
        query_start = query_start.astype(jnp.int32)
        query_block = lax.dynamic_slice_in_dim(queries, query_start, BLK, 0)
        query_segs = lax.dynamic_slice_in_dim(segment_row, query_start, BLK, 0)
        offset = positions[None, :] - (query_start + jnp.arange(BLK, dtype=jnp.int32))[:, None]
        bias_full = jnp.transpose(bias_table[bucket_of(offset)], (2, 0, 1))
        raw_scores = low_back(jnp.einsum('qhd,khd->hqk', query_block, all_keys, precision=lax.Precision.HIGHEST))
        scores = raw_scores + bias_full
        allowed = (query_segs[:, None] == segment_row[None, :])[None]
        masked_fill = jnp.full(scores.shape, MASKED, scores.dtype)
        zero_fill = jnp.zeros(scores.shape, scores.dtype)
        top = lax.optimization_barrier(jnp.max(jnp.where(allowed, scores, masked_fill), axis=-1, keepdims=True))
        exp_terms = jnp.where(allowed, jnp.exp(jnp.where(allowed, scores - top, zero_fill)), zero_fill)
        probs_low = low(exp_terms / lax.optimization_barrier(jnp.sum(exp_terms, axis=-1, keepdims=True)))
        return jnp.einsum('hqk,khd->qhd', probs_low, values, precision=lax.Precision.HIGHEST)
    starts = jnp.arange(SEQ_LEN // BLK, dtype=jnp.int32) * BLK
    return lax.map(jax.checkpoint(block_rows), starts).reshape(SEQ_LEN, HEADS, HEAD)

def layer(stream, segment_row, gain_attn, w_query, w_key, w_value, w_out, bias_table, gain_ffn, w_in, w_back):
    normed = low(normalize(stream, gain_attn))
    queries = low(low_back(product(normed, w_query))).reshape(SEQ_LEN, HEADS, HEAD)
    all_keys = low(low_back(product(normed, w_key))).reshape(SEQ_LEN, HEADS, HEAD)
    values = low(low_back(product(normed, w_value))).reshape(SEQ_LEN, HEADS, HEAD)
    context = attention(queries, all_keys, values, segment_row, bias_table).reshape(SEQ_LEN, HEADS * HEAD)
    context = low(low_back(context))
    hidden = stream + low_back(product(context, w_out))
    normed_ffn = low(normalize(hidden, gain_ffn))
    inner_pre = low_back(product(normed_ffn, w_in))
    active = low(jax.nn.gelu(inner_pre, approximate=True))
    return hidden + low_back(product(active, w_back))

def reference(inputs, segments, gain_attn, w_query, w_key, w_value, w_out, bias_table, gain_ffn, w_in, w_back, cotangent):
    params = tuple((weight_arg.astype(jnp.float32) for weight_arg in (gain_attn, w_query, w_key, w_value, w_out, bias_table, gain_ffn, w_in, w_back)))
    stream_all = inputs.astype(jnp.float32).reshape(NSEQ, SEQ_LEN, D)
    cot_all = cotangent.astype(jnp.float32).reshape(NSEQ, SEQ_LEN, D)
    segment_all = segments.astype(jnp.int32)

    def per_sequence(totals, seq_items):
        stream, segment_row, cot_rows = seq_items

        def layer_of(stream_in, *weight_args):
            return layer(stream_in, segment_row, *weight_args)
        result, pullback = jax.vjp(layer_of, stream, *params)
        pulled = pullback(cot_rows)
        totals = tuple((total_part + new_part for total_part, new_part in zip(totals, pulled[1:])))
        return (totals, (result, pulled[0]))
    zero_grads = tuple((jnp.zeros(weight_arg.shape, jnp.float32) for weight_arg in params))
    totals, (results, grad_stream) = lax.scan(per_sequence, zero_grads, (stream_all, segment_all, cot_all))
    return (results.reshape(TOKENS, D), grad_stream.reshape(TOKENS, D), totals[0], totals[1], totals[2], totals[3], totals[4], totals[5], totals[6], totals[7], totals[8])
```

```python
import functools
import math

import jax
import jax.numpy as jnp
from jax import lax
from jax.experimental import pallas as pl
from jax.experimental.pallas import tpu as pltpu
from jax.sharding import PartitionSpec as P

EPSILON = 1e-06

LOG2E = math.log2(math.e)
MASKED = -1e30
TILE = 256
VROWS = 80
reach_marks = (12, 16, 23, 32, 46, 64, 91)


def bucket_of(offset):
    distance = jnp.abs(offset)
    far_bucket = jnp.full(offset.shape, 8, jnp.int32)
    for threshold in reach_marks:
        far_bucket = far_bucket + (distance >= threshold).astype(jnp.int32)
    return 16 * (offset > 0).astype(jnp.int32) + jnp.where(distance < 8, distance, far_bucket)


def bias_tiles_kernel(heads, table_ref, tile_ref):
    T = TILE
    for d in range(3):
        t = lax.broadcasted_iota(jnp.int32, (8, 2 * T), 1)
        t = jnp.where(t < T, t, t - 2 * T)
        bucket = bucket_of((d - 1) * T - t)
        for h in range(heads):
            row = jnp.zeros((8, 2 * T), jnp.float32)
            for b in range(32):
                row = jnp.where(bucket == b, table_ref[b, h] * LOG2E, row)
            wide = jnp.broadcast_to(row[0:1], (T, 2 * T))
            rolled = pltpu.roll(wide, 0, 1, stride=1, stride_axis=0)
            tile_ref[h * 3 + d] = rolled[:, :T]


def bias_tiles(bias_table):
    heads = bias_table.shape[1]
    return pl.pallas_call(
        functools.partial(bias_tiles_kernel, heads),
        out_shape=jax.ShapeDtypeStruct((heads * 3, TILE, TILE), jnp.float32),
        in_specs=[pl.BlockSpec(memory_space=pltpu.SMEM)],
        out_specs=pl.BlockSpec(memory_space=pltpu.VMEM),
        name="bias_tiles",
    )(bias_table)


def block_loops(i, lo, hi, far, near):
    lax.fori_loop(lo, i - 1, lambda j, _: far(j, 0) or 0, 0)
    lax.fori_loop(jnp.maximum(lo, i - 1), jnp.minimum(hi, i + 1) + 1, lambda j, _: near(j) or 0, 0)
    lax.fori_loop(i + 2, hi + 1, lambda j, _: far(j, 1) or 0, 0)


def attn_fwd_kernel(heads, lo_ref, hi_ref, table_ref, qx_ref, kx_ref, vt_ref, tile_ref, o_ref, lse_ref, m_ref, acc_ref):
    T = TILE
    i = pl.program_id(0)
    lo, hi = lo_ref[i], hi_ref[i]
    m_ref[...] = jnp.full(m_ref.shape, MASKED, jnp.float32)
    acc_ref[...] = jnp.zeros(acc_ref.shape, jnp.float32)

    def tile(j, bias_of):
        start = pl.multiple_of(j * T, T)
        for h in range(heads):
            k = kx_ref[pl.ds(start, T), h * 128:(h + 1) * 128]
            s = jnp.dot(k, qx_ref[h * 128:(h + 1) * 128, :], preferred_element_type=jnp.float32)
            s = s + bias_of(h)
            m_old = m_ref[h:h + 1, :]
            m_new = jnp.maximum(m_old, jnp.max(s, axis=0, keepdims=True))
            p = jnp.exp2(s - m_new).astype(jnp.bfloat16)
            alpha = jnp.exp2(m_old - m_new)
            m_ref[h:h + 1, :] = m_new
            rows = slice(h * VROWS, (h + 1) * VROWS)
            acc_ref[rows, :] = acc_ref[rows, :] * alpha + jnp.dot(
                vt_ref[rows, pl.ds(start, T)], p, preferred_element_type=jnp.float32)

    def far(j, side):
        tile(j, lambda h: table_ref[16 * side + 15, h] * LOG2E)

    def near(j):
        tile(j, lambda h: tile_ref[h * 3 + j - i + 1])

    block_loops(i, lo, hi, far, near)
    for h in range(heads):
        total = acc_ref[h * VROWS + 64:h * VROWS + 65, :]
        o_ref[h * 64:(h + 1) * 64, :] = (acc_ref[h * VROWS:h * VROWS + 64, :] / total).astype(jnp.bfloat16)
        lse_ref[h:h + 1, :] = m_ref[h:h + 1, :] + jnp.log2(total)


def attn_fwd(lo, hi, bias_table, qx, kx, vt, tiles):
    heads = bias_table.shape[1]
    S = kx.shape[0]
    T = TILE
    smem = pl.BlockSpec(memory_space=pltpu.SMEM)
    full = lambda shape: pl.BlockSpec(shape, lambda i: (0,) * len(shape), pipeline_mode=pl.Buffered(1))
    return pl.pallas_call(
        functools.partial(attn_fwd_kernel, heads),
        grid=(S // T,),
        out_shape=(jax.ShapeDtypeStruct((heads * 64, S), jnp.bfloat16), jax.ShapeDtypeStruct((8, S), jnp.float32)),
        in_specs=[smem, smem, smem, pl.BlockSpec((heads * 128, T), lambda i: (0, i)), full(kx.shape), full(vt.shape), full(tiles.shape)],
        out_specs=(pl.BlockSpec((heads * 64, T), lambda i: (0, i)), pl.BlockSpec((8, T), lambda i: (0, i))),
        scratch_shapes=[pltpu.VMEM((8, T), jnp.float32), pltpu.VMEM((heads * VROWS, T), jnp.float32)],
        compiler_params=pltpu.CompilerParams(dimension_semantics=("arbitrary",), vmem_limit_bytes=48 << 20),
        name="attn_fwd",
    )(lo, hi, bias_table, qx, kx, vt, tiles)


def attn_bwd_kernel(heads, lo_ref, hi_ref, table_ref, qx_ref, kx_ref, vx_ref, kt_ref, dot_ref, ot_ref, lse_ref, tile_ref,
                    dq_ref, dk_ref, dv_ref, diag_ref, d_ref, dqacc_ref, bacc_ref, far_ref, dk_acc, dv_acc):
    T = TILE
    j = pl.program_id(0)
    last = pl.num_programs(0) - 1
    lo, hi = lo_ref[j], hi_ref[j]
    NT = (((1,), (1,)), ((), ()))

    @pl.when(j == 0)
    def _():
        dqacc_ref[...] = jnp.zeros(dqacc_ref.shape, jnp.float32)
        bacc_ref[...] = jnp.zeros(bacc_ref.shape, jnp.float32)
        far_ref[...] = jnp.zeros(far_ref.shape, jnp.float32)
        for h in range(heads):
            rows = slice(h * 64, (h + 1) * 64)
            d_ref[h:h + 1, :] = jnp.sum(dot_ref[rows, :].astype(jnp.float32) * ot_ref[rows, :].astype(jnp.float32), axis=0, keepdims=True)

    dk_acc[...] = jnp.zeros(dk_acc.shape, jnp.float32)
    dv_acc[...] = jnp.zeros(dv_acc.shape, jnp.float32)

    def tile(i, bias_of, sums):
        cols = pl.ds(pl.multiple_of(i * T, T), T)
        for h in range(heads):
            rows = slice(h * 64, (h + 1) * 64)
            q = qx_ref[h * 128:(h + 1) * 128, cols]
            do = dot_ref[rows, cols]
            s = jnp.dot(kx_ref[:, h * 128:(h + 1) * 128], q, preferred_element_type=jnp.float32)
            p = jnp.exp2(s + bias_of(h, lse_ref[h:h + 1, cols]))
            dp = jnp.dot(vx_ref[:, h * 128:h * 128 + 64], do, preferred_element_type=jnp.float32)
            ds = p * (dp - d_ref[h:h + 1, cols])
            sums(h, ds)
            pb = p.astype(jnp.bfloat16)
            db = ds.astype(jnp.bfloat16)
            dv_acc[h] += lax.dot_general(pb, do, NT, preferred_element_type=jnp.float32)
            dk_acc[h] += lax.dot_general(db, q[:64], NT, preferred_element_type=jnp.float32)
            dqacc_ref[rows, cols] += jnp.dot(kt_ref[rows, :], db, preferred_element_type=jnp.float32)

    def far(i, later):
        side = 1 - later

        def bias_of(h, lse):
            return table_ref[16 * side + 15, h] * LOG2E - lse

        def sums(h, ds):
            far_ref[h * 2 + side] += jnp.sum(ds.reshape(T // 8, 8, T), axis=0)
        tile(i, bias_of, sums)

    def near(i):
        def bias_of(h, lse):
            return tile_ref[h * 3 + j - i + 1] - lse

        def sums(h, ds):
            bacc_ref[h * 3 + j - i + 1] += ds
        tile(i, bias_of, sums)

    block_loops(j, lo, hi, far, near)
    for h in range(0, heads, 2):
        dk_ref[:, h * 64:(h + 2) * 64] = (jnp.concatenate((dk_acc[h], dk_acc[h + 1]), axis=1) * (1.0 / LOG2E)).astype(jnp.bfloat16)
        dv_ref[:, h * 64:(h + 2) * 64] = jnp.concatenate((dv_acc[h], dv_acc[h + 1]), axis=1).astype(jnp.bfloat16)

    @pl.when(j == last)
    def _():
        dq_ref[...] = dqacc_ref[...].astype(jnp.bfloat16)
        zero = jnp.zeros((8, T), jnp.float32)
        sub = lax.broadcasted_iota(jnp.int32, (8, 2 * T), 0)
        for n in range(heads * 3):
            total = jnp.concatenate((bacc_ref[n, 0:8, :], zero), axis=1)
            for g in range(1, T // 8):
                rows = jnp.concatenate((bacc_ref[n, 8 * g:8 * g + 8, :], zero), axis=1)
                total = total + pltpu.roll(rows, 2 * T - 8 * g, 1)
            for bit in (1, 2, 4):
                total = jnp.where((sub & bit) != 0, pltpu.roll(total, 2 * T - bit, 1), total)
            diag_ref[n:n + 1, :] = jnp.sum(total, axis=0, keepdims=True)
        for n in range(heads * 2):
            diag_ref[heads * 3 + n:heads * 3 + n + 1, 0:T] = jnp.sum(far_ref[n], axis=0, keepdims=True)
            diag_ref[heads * 3 + n:heads * 3 + n + 1, T:] = jnp.zeros((1, T), jnp.float32)


def attn_bwd(lo, hi, bias_table, qx, kx, vx, kt, dot, ot, lse, tiles):
    heads = bias_table.shape[1]
    S = kx.shape[0]
    T = TILE
    smem = pl.BlockSpec(memory_space=pltpu.SMEM)
    full = lambda shape: pl.BlockSpec(shape, lambda i: (0,) * len(shape), pipeline_mode=pl.Buffered(1))
    rows = lambda n: pl.BlockSpec((T, n), lambda i: (i, 0))
    HC = heads * 64
    return pl.pallas_call(
        functools.partial(attn_bwd_kernel, heads),
        grid=(S // T,),
        out_shape=(jax.ShapeDtypeStruct((HC, S), jnp.bfloat16), jax.ShapeDtypeStruct((S, HC), jnp.bfloat16),
                   jax.ShapeDtypeStruct((S, HC), jnp.bfloat16), jax.ShapeDtypeStruct((heads * 5, 2 * T), jnp.float32)),
        in_specs=[smem, smem, smem, full(qx.shape), rows(heads * 128), rows(heads * 128), pl.BlockSpec((HC, T), lambda i: (0, i)),
                  full(dot.shape), full(ot.shape), full(lse.shape), full(tiles.shape)],
        out_specs=(full((HC, S)), rows(HC), rows(HC), full((heads * 5, 2 * T))),
        scratch_shapes=[pltpu.VMEM((8, S), jnp.float32), pltpu.VMEM((HC, S), jnp.float32),
                        pltpu.VMEM((heads * 3, T, T), jnp.float32), pltpu.VMEM((heads * 2, 8, T), jnp.float32),
                        pltpu.VMEM((heads, T, 64), jnp.float32), pltpu.VMEM((heads, T, 64), jnp.float32)],
        compiler_params=pltpu.CompilerParams(dimension_semantics=("arbitrary",), vmem_limit_bytes=56 << 20),
        name="attn_bwd",
    )(lo, hi, bias_table, qx, kx, vx, kt, dot, ot, lse, tiles)


def table_grad(diag, heads):
    T = TILE
    t = jnp.arange(2 * T, dtype=jnp.int32)
    t = jnp.where(t < T, t, t - 2 * T)
    d = jnp.arange(3, dtype=jnp.int32)
    bucket = bucket_of((d[:, None] - 1) * T - t[None, :])
    onehot = (bucket[:, :, None] == jnp.arange(32, dtype=jnp.int32)).astype(jnp.float32)
    near = jnp.einsum("hdt,dtb->bh", diag[:heads * 3].reshape(heads, 3, 2 * T), onehot, precision=lax.Precision.HIGHEST)
    far = jnp.sum(diag[heads * 3:].reshape(heads, 2, 2 * T), axis=2)
    ids = jnp.arange(32, dtype=jnp.int32)[:, None]
    return near + jnp.where(ids == 15, far[None, :, 0], 0.0) + jnp.where(ids == 31, far[None, :, 1], 0.0)


def block_bounds(segment_row):
    S = segment_row.shape[0]
    blocks = segment_row.reshape(S // TILE, TILE)
    first, final = blocks[:, 0], blocks[:, TILE - 1]
    lo = jnp.sum((segment_row[None, :] < first[:, None]).astype(jnp.int32), axis=1) // TILE
    hi = (jnp.sum((segment_row[None, :] <= final[:, None]).astype(jnp.int32), axis=1) - 1) // TILE
    return lo, hi


def pad_heads(w, heads, width):
    D = w.shape[0]
    return jnp.pad(w.reshape(D, heads, 64), ((0, 0), (0, 0), (0, width - 64))).reshape(D, heads * width)


def operands(segment_row):
    S = segment_row.shape[0]
    row = jnp.arange(128, dtype=jnp.int32)
    same = segment_row[None, :] == (row[:, None] - 64)
    inside = (row >= 64) & (row < 80)
    qext = jnp.where(inside[:, None] & same, 1.0, 0.0)
    kext = jnp.where(inside[None, :] & ~same.T, MASKED, 0.0)
    vext = jnp.where(jnp.arange(VROWS) == 64, 1.0, 0.0)[:, None]
    return qext, kext, vext


def project(normed, w_query, w_key, w_value, ext, heads):
    qext, kext, vext = ext
    TN = (((0,), (1,)), ((), ()))
    f32 = jnp.float32
    qx = lax.dot_general(pad_heads(w_query, heads, 128), normed, TN, preferred_element_type=f32) * LOG2E
    qx = (qx + jnp.tile(qext, (heads, 1))).astype(jnp.bfloat16)
    kx = jnp.dot(normed, pad_heads(w_key, heads, 128), preferred_element_type=f32)
    kx = (kx + jnp.tile(kext, (1, heads))).astype(jnp.bfloat16)
    vt = lax.dot_general(pad_heads(w_value, heads, VROWS), normed, TN, preferred_element_type=f32)
    vt = (vt + jnp.tile(vext, (heads, 1))).astype(jnp.bfloat16)
    vx = jnp.dot(normed, pad_heads(w_value, heads, 128), preferred_element_type=f32).astype(jnp.bfloat16)
    kt = lax.dot_general(w_key, normed, TN, preferred_element_type=f32).astype(jnp.bfloat16)
    return qx, kx, vt, vx, kt


def over_rows(left_side, right_side):
    return lax.dot_general(
        left_side, right_side, (((0,), (0,)), ((), ())), preferred_element_type=jnp.float32
    )


def against(left_side, right_side):
    return lax.dot_general(
        left_side, right_side, (((1,), (1,)), ((), ())), preferred_element_type=jnp.float32
    )


def norm_back(grad_normed, unit_rows, inv_scale, gain_row):
    scaled = grad_normed * gain_row
    return inv_scale * (scaled - unit_rows * jnp.mean(scaled * unit_rows, axis=-1, keepdims=True))


def smooth_gate(values_in):
    return jax.nn.gelu(values_in, approximate=True)


def on_device(
    inputs,
    segments,
    gain_attn,
    w_query,
    w_key,
    w_value,
    w_out,
    bias_table,
    gain_ffn,
    w_in,
    w_back,
    cotangent,
):
    head_cols = w_query.shape[1]
    heads_here = bias_table.shape[1]
    segment_row = segments.reshape(-1)
    lo, hi = block_bounds(segment_row)
    tiles = bias_tiles(bias_table)
    stream = inputs.astype(jnp.float32)
    inv_attn = lax.rsqrt(jnp.mean(stream * stream, axis=-1, keepdims=True) + EPSILON)
    unit_attn = stream * inv_attn
    normed = lax.all_gather(
        (unit_attn * gain_attn).astype(jnp.bfloat16), "tensor", axis=0, tiled=True
    )
    w_joint = jnp.concatenate((w_query, w_key, w_value), axis=1)
    qx, kx, vt, vx, kt = project(normed, w_query, w_key, w_value, operands(segment_row), heads_here)
    ctx_t, lse = attn_fwd(lo, hi, bias_table, qx, kx, vt, tiles)
    context_low = ctx_t.T
    hidden = stream + lax.psum_scatter(
        jnp.dot(context_low, w_out, preferred_element_type=jnp.float32).astype(jnp.bfloat16),
        "tensor",
        scatter_dimension=0,
        tiled=True,
    ).astype(jnp.float32)
    inv_ffn = lax.rsqrt(jnp.mean(hidden * hidden, axis=-1, keepdims=True) + EPSILON)
    unit_ffn = hidden * inv_ffn
    normed_ffn = lax.all_gather(
        (unit_ffn * gain_ffn).astype(jnp.bfloat16), "tensor", axis=0, tiled=True
    )
    inner_pre = jnp.dot(normed_ffn, w_in, preferred_element_type=jnp.float32)
    gated, gate_pull = jax.vjp(smooth_gate, inner_pre)
    active = gated.astype(jnp.bfloat16)
    output = hidden + lax.psum_scatter(
        jnp.dot(active, w_back, preferred_element_type=jnp.float32).astype(jnp.bfloat16),
        "tensor",
        scatter_dimension=0,
        tiled=True,
    ).astype(jnp.float32)
    grad_out_full = lax.all_gather(cotangent, "tensor", axis=0, tiled=True)
    grad_w_back = over_rows(active, grad_out_full)
    grad_inner = gate_pull(against(grad_out_full, w_back))[0].astype(jnp.bfloat16)
    grad_w_in = over_rows(normed_ffn, grad_inner)
    grad_normed_ffn = lax.psum_scatter(
        against(grad_inner, w_in).astype(jnp.bfloat16), "tensor", scatter_dimension=0, tiled=True
    ).astype(jnp.float32)
    gain_ffn_part = jnp.sum(grad_normed_ffn * unit_ffn, axis=0)
    grad_hidden = cotangent.astype(jnp.float32) + norm_back(
        grad_normed_ffn, unit_ffn, inv_ffn, gain_ffn
    )
    grad_hidden_full = lax.all_gather(
        grad_hidden.astype(jnp.bfloat16), "tensor", axis=0, tiled=True
    )
    grad_w_out = over_rows(context_low, grad_hidden_full)
    grad_ctx_t = against(w_out, grad_hidden_full).astype(jnp.bfloat16)
    dq_t, grad_keys, grad_values, diag = attn_bwd(
        lo, hi, bias_table, qx, kx, vx, kt, grad_ctx_t, ctx_t, lse, tiles
    )
    grad_table = table_grad(diag, heads_here)
    grad_joint = jnp.concatenate((dq_t.T, grad_keys, grad_values), axis=1)
    grad_w_joint = over_rows(normed, grad_joint)
    grad_normed = lax.psum_scatter(
        against(grad_joint, w_joint).astype(jnp.bfloat16), "tensor", scatter_dimension=0, tiled=True
    ).astype(jnp.float32)
    gain_attn_part = jnp.sum(grad_normed * unit_attn, axis=0)
    grad_inputs = grad_hidden + norm_back(grad_normed, unit_attn, inv_attn, gain_attn)
    weight_grads = (
        grad_w_joint[:, :head_cols],
        grad_w_joint[:, head_cols : 2 * head_cols],
        grad_w_joint[:, 2 * head_cols :],
        grad_w_out,
        grad_table,
        grad_w_in,
        grad_w_back,
    )
    scattered = (
        lax.psum_scatter(
            weight_grads[0].astype(jnp.bfloat16), "dp", scatter_dimension=0, tiled=True
        ).astype(jnp.float32),
        lax.psum_scatter(
            weight_grads[1].astype(jnp.bfloat16), "dp", scatter_dimension=0, tiled=True
        ).astype(jnp.float32),
        lax.psum_scatter(
            weight_grads[2].astype(jnp.bfloat16), "dp", scatter_dimension=0, tiled=True
        ).astype(jnp.float32),
        lax.psum_scatter(
            weight_grads[3].astype(jnp.bfloat16), "dp", scatter_dimension=1, tiled=True
        ).astype(jnp.float32),
        lax.psum_scatter(
            weight_grads[4].astype(jnp.bfloat16), "dp", scatter_dimension=0, tiled=True
        ).astype(jnp.float32),
        lax.psum_scatter(
            weight_grads[5].astype(jnp.bfloat16), "dp", scatter_dimension=0, tiled=True
        ).astype(jnp.float32),
        lax.psum_scatter(
            weight_grads[6].astype(jnp.bfloat16), "dp", scatter_dimension=1, tiled=True
        ).astype(jnp.float32),
    )
    summed = (
        lax.psum(scattered[0].astype(jnp.bfloat16), "group").astype(jnp.float32),
        lax.psum(scattered[1].astype(jnp.bfloat16), "group").astype(jnp.float32),
        lax.psum(scattered[2].astype(jnp.bfloat16), "group").astype(jnp.float32),
        lax.psum(scattered[3].astype(jnp.bfloat16), "group").astype(jnp.float32),
        lax.psum(scattered[4].astype(jnp.bfloat16), "group").astype(jnp.float32),
        lax.psum(scattered[5].astype(jnp.bfloat16), "group").astype(jnp.float32),
        lax.psum(scattered[6].astype(jnp.bfloat16), "group").astype(jnp.float32),
    )
    gain_grads = lax.psum((gain_attn_part, gain_ffn_part), ("dp", "group", "tensor"))
    return (
        output,
        grad_inputs,
        gain_grads[0],
        summed[0],
        summed[1],
        summed[2],
        summed[3],
        summed[4],
        gain_grads[1],
        summed[5],
        summed[6],
    )


def solution(mesh):
    return jax.shard_map(
        on_device,
        mesh=mesh,
        in_specs=(
            P(("dp", "group", "tensor"), None),
            P(("dp", "group"), None),
            P(),
            P(None, "tensor"),
            P(None, "tensor"),
            P(None, "tensor"),
            P("tensor", None),
            P(None, "tensor"),
            P(),
            P(None, "tensor"),
            P("tensor", None),
            P(("dp", "group", "tensor"), None),
        ),
        out_specs=(
            P(("dp", "group", "tensor"), None),
            P(("dp", "group", "tensor"), None),
            P(),
            P("dp", "tensor"),
            P("dp", "tensor"),
            P("dp", "tensor"),
            P("tensor", "dp"),
            P("dp", "tensor"),
            P(),
            P("dp", "tensor"),
            P("tensor", "dp"),
        ),
        check_vma=False,
    )
```

```python
import functools
import math

import jax
import jax.numpy as jnp
from jax import lax
from jax.experimental import pallas as pl
from jax.experimental.pallas import tpu as pltpu
from jax.sharding import PartitionSpec as P

EPSILON = 1e-06

LOG2E = math.log2(math.e)
MASKED = -1e30
TILE = 256
VROWS = 80
PAIR = 2
TN = (((0,), (1,)), ((), ()))
reach_marks = (12, 16, 23, 32, 46, 64, 91)


def bucket_of(offset):
    distance = jnp.abs(offset)
    far_bucket = jnp.full(offset.shape, 8, jnp.int32)
    for threshold in reach_marks:
        far_bucket = far_bucket + (distance >= threshold).astype(jnp.int32)
    return 16 * (offset > 0).astype(jnp.int32) + jnp.where(distance < 8, distance, far_bucket)


def bias_tiles_kernel(heads, table_ref, tile_ref):
    T = TILE
    for d in range(3):
        t = lax.broadcasted_iota(jnp.int32, (8, 2 * T), 1)
        t = jnp.where(t < T, t, t - 2 * T)
        bucket = bucket_of((d - 1) * T - t)
        for h in range(heads):
            row = jnp.zeros((8, 2 * T), jnp.float32)
            for b in range(32):
                row = jnp.where(bucket == b, table_ref[b, h] * LOG2E, row)
            wide = jnp.broadcast_to(row[0:1], (T, 2 * T))
            rolled = pltpu.roll(wide, 0, 1, stride=1, stride_axis=0)
            tile_ref[h * 3 + d] = rolled[:, :T]


def bias_tiles(bias_table):
    heads = bias_table.shape[1]
    return pl.pallas_call(
        functools.partial(bias_tiles_kernel, heads),
        out_shape=jax.ShapeDtypeStruct((heads * 3, TILE, TILE), jnp.float32),
        in_specs=[pl.BlockSpec(memory_space=pltpu.SMEM)],
        out_specs=pl.BlockSpec(memory_space=pltpu.VMEM),
        name="bias_tiles",
    )(bias_table)


def block_loops(i, lo, hi, far, near):
    lax.fori_loop(lo, i - 1, lambda j, _: far(j, 0) or 0, 0)
    lax.fori_loop(jnp.maximum(lo, i - 1), jnp.minimum(hi, i + 1) + 1, lambda j, _: near(j) or 0, 0)
    lax.fori_loop(i + 2, hi + 1, lambda j, _: far(j, 1) or 0, 0)


def attn_fwd_kernel(heads, first, lo_ref, hi_ref, table_ref, qx_ref, kx_ref, vt_ref, tile_ref, o_ref, lse_ref, m_ref, acc_ref):
    T = TILE
    i = pl.program_id(0)
    lo, hi = lo_ref[i], hi_ref[i]
    m_ref[...] = jnp.full(m_ref.shape, MASKED, jnp.float32)
    acc_ref[...] = jnp.zeros(acc_ref.shape, jnp.float32)

    def tile(j, bias_of):
        start = pl.multiple_of(j * T, T)
        for h in range(heads):
            k = kx_ref[pl.ds(start, T), h * 128:(h + 1) * 128]
            s = jnp.dot(k, qx_ref[h * 128:(h + 1) * 128, :], preferred_element_type=jnp.float32)
            s = s + bias_of(h)
            m_old = m_ref[h:h + 1, :]
            m_new = jnp.maximum(m_old, jnp.max(s, axis=0, keepdims=True))
            p = jnp.exp2(s - m_new).astype(jnp.bfloat16)
            alpha = jnp.exp2(m_old - m_new)
            m_ref[h:h + 1, :] = m_new
            rows = slice(h * VROWS, (h + 1) * VROWS)
            acc_ref[rows, :] = acc_ref[rows, :] * alpha + jnp.dot(
                vt_ref[rows, pl.ds(start, T)], p, preferred_element_type=jnp.float32)

    def far(j, side):
        tile(j, lambda h: table_ref[16 * side + 15, first + h] * LOG2E)

    def near(j):
        tile(j, lambda h: tile_ref[h * 3 + j - i + 1])

    block_loops(i, lo, hi, far, near)
    for h in range(heads):
        total = acc_ref[h * VROWS + 64:h * VROWS + 65, :]
        o_ref[h * 64:(h + 1) * 64, :] = (acc_ref[h * VROWS:h * VROWS + 64, :] / total).astype(jnp.bfloat16)
        lse_ref[h:h + 1, :] = m_ref[h:h + 1, :] + jnp.log2(total)


def attn_cost(seq_len, heads, micros):
    return pl.CostEstimate(flops=int(micros * 1e9), transcendentals=0, bytes_accessed=seq_len * heads * 2048)


def attn_fwd(pair, lo, hi, bias_table, qx, kx, vt, tiles):
    heads = PAIR
    T = TILE
    S = lo.shape[0] * T
    smem = pl.BlockSpec(memory_space=pltpu.SMEM)
    once = lambda shape, index: pl.BlockSpec(shape, lambda i: index, pipeline_mode=pl.Buffered(1))
    return pl.pallas_call(
        functools.partial(attn_fwd_kernel, heads, pair * heads),
        grid=(S // T,),
        out_shape=(jax.ShapeDtypeStruct((heads * 64, S), jnp.bfloat16), jax.ShapeDtypeStruct((8, S), jnp.float32)),
        in_specs=[smem, smem, smem, pl.BlockSpec((heads * 128, T), lambda i: (pair, i)), once((S, heads * 128), (0, pair)),
                  once((heads * VROWS, S), (pair, 0)), once((heads * 3, T, T), (pair, 0, 0))],
        out_specs=(pl.BlockSpec((heads * 64, T), lambda i: (0, i)), pl.BlockSpec((8, T), lambda i: (0, i))),
        scratch_shapes=[pltpu.VMEM((8, T), jnp.float32), pltpu.VMEM((heads * VROWS, T), jnp.float32)],
        compiler_params=pltpu.CompilerParams(dimension_semantics=("arbitrary",), vmem_limit_bytes=24 << 20),
        cost_estimate=attn_cost(S, heads, 22),
        name="attn_fwd",
    )(lo, hi, bias_table, qx, kx, vt, tiles)


def attn_bwd_kernel(heads, first, lo_ref, hi_ref, table_ref, qx_ref, kx_ref, vx_ref, kt_ref, dot_ref, ot_ref, lse_ref, tile_ref,
                    grad_ref, diag_ref, d_ref, dqacc_ref, bacc_ref, far_ref, dk_acc, dv_acc):
    T = TILE
    j = pl.program_id(0)
    last = pl.num_programs(0) - 1
    lo, hi = lo_ref[j], hi_ref[j]
    NT = (((1,), (1,)), ((), ()))

    @pl.when(j == 0)
    def _():
        dqacc_ref[...] = jnp.zeros(dqacc_ref.shape, jnp.float32)
        bacc_ref[...] = jnp.zeros(bacc_ref.shape, jnp.float32)
        far_ref[...] = jnp.zeros(far_ref.shape, jnp.float32)
        for h in range(heads):
            rows = slice(h * 64, (h + 1) * 64)
            d_ref[h:h + 1, :] = jnp.sum(dot_ref[rows, :].astype(jnp.float32) * ot_ref[rows, :].astype(jnp.float32), axis=0, keepdims=True)

    dk_acc[...] = jnp.zeros(dk_acc.shape, jnp.float32)
    dv_acc[...] = jnp.zeros(dv_acc.shape, jnp.float32)

    def tile(i, bias_of, sums):
        cols = pl.ds(pl.multiple_of(i * T, T), T)
        for h in range(heads):
            rows = slice(h * 64, (h + 1) * 64)
            q = qx_ref[h * 128:(h + 1) * 128, cols]
            do = dot_ref[rows, cols]
            s = jnp.dot(kx_ref[:, h * 128:(h + 1) * 128], q, preferred_element_type=jnp.float32)
            p = jnp.exp2(s + bias_of(h, lse_ref[h:h + 1, cols]))
            dp = jnp.dot(vx_ref[:, h * 128:h * 128 + 64], do, preferred_element_type=jnp.float32)
            ds = p * (dp - d_ref[h:h + 1, cols])
            sums(h, ds)
            pb = p.astype(jnp.bfloat16)
            db = ds.astype(jnp.bfloat16)
            dv_acc[h] += lax.dot_general(pb, do, NT, preferred_element_type=jnp.float32)
            dk_acc[h] += lax.dot_general(db, q[:64], NT, preferred_element_type=jnp.float32)
            dqacc_ref[rows, cols] += jnp.dot(kt_ref[rows, :], db, preferred_element_type=jnp.float32)

    def far(i, later):
        side = 1 - later

        def bias_of(h, lse):
            return table_ref[16 * side + 15, first + h] * LOG2E - lse

        def sums(h, ds):
            far_ref[h * 2 + side] += jnp.sum(ds.reshape(T // 8, 8, T), axis=0)
        tile(i, bias_of, sums)

    def near(i):
        def bias_of(h, lse):
            return tile_ref[h * 3 + j - i + 1] - lse

        def sums(h, ds):
            bacc_ref[h * 3 + j - i + 1] += ds
        tile(i, bias_of, sums)

    block_loops(j, lo, hi, far, near)
    HC = heads * 64
    block = pl.ds(pl.multiple_of(j * T, T), T)
    grad_ref[block, HC:2 * HC] = (jnp.concatenate([dk_acc[h] for h in range(heads)], axis=1) * (1.0 / LOG2E)).astype(jnp.bfloat16)
    grad_ref[block, 2 * HC:] = jnp.concatenate([dv_acc[h] for h in range(heads)], axis=1).astype(jnp.bfloat16)

    @pl.when(j == last)
    def _():
        for n in range(dqacc_ref.shape[1] // T):
            grad_ref[n * T:(n + 1) * T, 0:HC] = dqacc_ref[:, n * T:(n + 1) * T].T.astype(jnp.bfloat16)
        zero = jnp.zeros((8, T), jnp.float32)
        sub = lax.broadcasted_iota(jnp.int32, (8, 2 * T), 0)
        for n in range(heads * 3):
            total = jnp.concatenate((bacc_ref[n, 0:8, :], zero), axis=1)
            for g in range(1, T // 8):
                rows = jnp.concatenate((bacc_ref[n, 8 * g:8 * g + 8, :], zero), axis=1)
                total = total + pltpu.roll(rows, 2 * T - 8 * g, 1)
            for bit in (1, 2, 4):
                total = jnp.where((sub & bit) != 0, pltpu.roll(total, 2 * T - bit, 1), total)
            diag_ref[n:n + 1, :] = jnp.sum(total, axis=0, keepdims=True)
        for n in range(heads * 2):
            diag_ref[heads * 3 + n:heads * 3 + n + 1, 0:T] = jnp.sum(far_ref[n], axis=0, keepdims=True)
            diag_ref[heads * 3 + n:heads * 3 + n + 1, T:] = jnp.zeros((1, T), jnp.float32)


def attn_bwd(pair, lo, hi, bias_table, qx, kx, vx, kt, dot, ot, lse, tiles):
    heads = PAIR
    T = TILE
    S = lo.shape[0] * T
    smem = pl.BlockSpec(memory_space=pltpu.SMEM)
    once = lambda shape, index: pl.BlockSpec(shape, lambda i: index, pipeline_mode=pl.Buffered(1))
    rows = lambda n: pl.BlockSpec((T, n), lambda i: (i, pair))
    HC = heads * 64
    return pl.pallas_call(
        functools.partial(attn_bwd_kernel, heads, pair * heads),
        grid=(S // T,),
        out_shape=(jax.ShapeDtypeStruct((S, 3 * HC), jnp.bfloat16), jax.ShapeDtypeStruct((heads * 5, 2 * T), jnp.float32)),
        in_specs=[smem, smem, smem, once((heads * 128, S), (pair, 0)), rows(heads * 128), rows(heads * 128),
                  pl.BlockSpec((HC, T), lambda i: (pair, i)), once((HC, S), (pair, 0)), once((HC, S), (0, 0)), once((8, S), (0, 0)),
                  once((heads * 3, T, T), (pair, 0, 0))],
        out_specs=(once((S, 3 * HC), (0, 0)), once((heads * 5, 2 * T), (0, 0))),
        scratch_shapes=[pltpu.VMEM((8, S), jnp.float32), pltpu.VMEM((HC, S), jnp.float32),
                        pltpu.VMEM((heads * 3, T, T), jnp.float32), pltpu.VMEM((heads * 2, 8, T), jnp.float32),
                        pltpu.VMEM((heads, T, 64), jnp.float32), pltpu.VMEM((heads, T, 64), jnp.float32)],
        compiler_params=pltpu.CompilerParams(dimension_semantics=("arbitrary",), vmem_limit_bytes=32 << 20),
        cost_estimate=attn_cost(S, heads, 24),
        name="attn_bwd",
    )(lo, hi, bias_table, qx, kx, vx, kt, dot, ot, lse, tiles)


def table_grad(diag, heads):
    T = TILE
    t = jnp.arange(2 * T, dtype=jnp.int32)
    t = jnp.where(t < T, t, t - 2 * T)
    d = jnp.arange(3, dtype=jnp.int32)
    bucket = bucket_of((d[:, None] - 1) * T - t[None, :])
    onehot = (bucket[:, :, None] == jnp.arange(32, dtype=jnp.int32)).astype(jnp.float32)
    near = jnp.einsum("hdt,dtb->bh", diag[:heads * 3].reshape(heads, 3, 2 * T), onehot, precision=lax.Precision.HIGHEST)
    far = jnp.sum(diag[heads * 3:].reshape(heads, 2, 2 * T), axis=2)
    ids = jnp.arange(32, dtype=jnp.int32)[:, None]
    return near + jnp.where(ids == 15, far[None, :, 0], 0.0) + jnp.where(ids == 31, far[None, :, 1], 0.0)


def block_bounds(segment_row):
    S = segment_row.shape[0]
    blocks = segment_row.reshape(S // TILE, TILE)
    first, final = blocks[:, 0], blocks[:, TILE - 1]
    lo = jnp.sum((segment_row[None, :] < first[:, None]).astype(jnp.int32), axis=1) // TILE
    hi = (jnp.sum((segment_row[None, :] <= final[:, None]).astype(jnp.int32), axis=1) - 1) // TILE
    return lo, hi


def pad_heads(w, heads, width):
    D = w.shape[0]
    return jnp.pad(w.reshape(D, heads, 64), ((0, 0), (0, 0), (0, width - 64))).reshape(D, heads * width)


def operands(segment_row):
    S = segment_row.shape[0]
    row = jnp.arange(128, dtype=jnp.int32)
    same = segment_row[None, :] == (row[:, None] - 64)
    inside = (row >= 64) & (row < 80)
    qext = jnp.where(inside[:, None] & same, 1.0, 0.0)
    kext = jnp.where(inside[None, :] & ~same.T, MASKED, 0.0)
    vext = jnp.where(jnp.arange(VROWS) == 64, 1.0, 0.0)[:, None]
    return qext, kext, vext


def padded_weights(w_query, w_key, w_value, heads):
    return pad_heads(w_query, heads, 128), pad_heads(w_key, heads, 128), pad_heads(w_value, heads, VROWS)


def project(normed, weights, ext, heads):
    (qext, kext, vext), (wq, wk, wv) = ext, weights
    f32 = jnp.float32
    qx = lax.dot_general(wq, normed, TN, preferred_element_type=f32) * LOG2E
    qx = (qx + jnp.tile(qext, (heads, 1))).astype(jnp.bfloat16)
    kx = jnp.dot(normed, wk, preferred_element_type=f32)
    kx = (kx + jnp.tile(kext, (1, heads))).astype(jnp.bfloat16)
    vt = lax.dot_general(wv, normed, TN, preferred_element_type=f32)
    vt = (vt + jnp.tile(vext, (heads, 1))).astype(jnp.bfloat16)
    return qx, kx, vt


def project_back(normed, w_vx, w_key):
    vx = jnp.dot(normed, w_vx, preferred_element_type=jnp.float32).astype(jnp.bfloat16)
    kt = lax.dot_general(w_key, normed, TN, preferred_element_type=jnp.float32).astype(jnp.bfloat16)
    return vx, kt


CHUNK = 256
ROOT = math.sqrt(2 / math.pi)


def ffn_kernel(parts, per_part, in_sent, back_sent, n_ref, c_ref, *refs):
    in_refs, back_refs = refs[:parts], refs[parts:2 * parts]
    out_ref, out_mate_ref, norm_ref, norm_mate_ref = refs[2 * parts:2 * parts + 4]
    gin_refs, gback_refs = refs[2 * parts + 4:2 * parts + 6], refs[2 * parts + 6:2 * parts + 8]
    w_in, w_back, out_acc, norm_acc = refs[2 * parts + 8:]
    step = pl.program_id(0)
    f32, bf16 = jnp.float32, jnp.bfloat16
    NT = (((1,), (1,)), ((), ()))
    TN = (((0,), (0,)), ((), ()))

    @pl.when(step == 0)
    def _():
        out_acc[...] = jnp.zeros(out_acc.shape, f32)
        norm_acc[...] = jnp.zeros(norm_acc.shape, f32)

    for q in range(parts):
        @pl.when(step // per_part == q)
        def _():
            w_in[...] = in_refs[q][...]
            w_back[...] = back_refs[q][...]

    rows = n_ref.shape[0]
    inner = lax.dot_general(n_ref[...], w_in[...], NT, preferred_element_type=f32)
    cube = inner * inner * 0.044715
    th = jnp.tanh(ROOT * inner * (1.0 + cube))
    half = 0.5 * (1.0 + th)
    active = (inner * half).astype(bf16)
    slope = half + (0.5 * ROOT) * inner * (1.0 - th * th) * (1.0 + 3.0 * cube)
    grad = (lax.dot_general(c_ref[...], w_back[...], NT, preferred_element_type=f32) * slope).astype(bf16)
    norm_acc[...] += jnp.dot(grad, w_in[...], preferred_element_type=f32)
    out_acc[...] += jnp.dot(active, w_back[...], preferred_element_type=f32)
    gin = lax.dot_general(grad, n_ref[...], TN, preferred_element_type=f32).astype(bf16)
    gback = lax.dot_general(active, c_ref[...], TN, preferred_element_type=f32).astype(bf16)
    part = step // per_part
    for grad_refs, value, sent in ((gin_refs, gin, in_sent), (gback_refs, gback, back_sent)):
        leaves = functools.reduce(jnp.logical_or, [part == q for q in sent], False)

        @pl.when(leaves)
        def _():
            grad_refs[1][...] = value

        @pl.when(jnp.logical_not(leaves))
        def _():
            grad_refs[0][...] = value

    @pl.when(step == pl.num_programs(0) - 1)
    def _():
        own = out_ref.shape[0]
        out_ref[...] = out_acc[:own, :]
        out_mate_ref[...] = out_acc[own:, :].astype(bf16)
        norm_ref[...] = norm_acc[:own, :]
        norm_mate_ref[...] = norm_acc[own:, :].astype(bf16)


def ffn(normed, cot, in_parts, back_parts, in_sent, back_sent):
    parts = len(in_parts)
    units, width = in_parts[0].shape
    rows = normed.shape[0]
    chunk = min(CHUNK, units)
    per_part = units // chunk
    once = lambda shape: pl.BlockSpec(shape, lambda i: (0, 0), pipeline_mode=pl.Buffered(1))
    piece = lambda q: pl.BlockSpec((chunk, width), lambda i: (jnp.clip(i - q * per_part, 0, per_part - 1), 0))
    weights = [piece(q) for q in range(parts)]
    sums = [jax.ShapeDtypeStruct((rows // 2, width), kind) for kind in (jnp.float32, jnp.bfloat16)]
    grads, grad_specs = [], []
    for sent in (in_sent, back_sent):
        for members in ([q for q in range(parts) if q not in sent], list(sent)):
            steps = [q * per_part + n for q in members for n in range(per_part)]
            index = lambda i, ups=tuple(steps[1:]): (sum([(i >= up).astype(jnp.int32) for up in ups], jnp.int32(0)), 0)
            grads.append(jax.ShapeDtypeStruct((len(members) * units, width), jnp.bfloat16))
            grad_specs.append(pl.BlockSpec((chunk, width), index))
    return pl.pallas_call(
        functools.partial(ffn_kernel, parts, per_part, in_sent, back_sent),
        grid=(parts * per_part,),
        out_shape=sums * 2 + grads,
        in_specs=[once((rows, width)), once((rows, width))] + weights * 2,
        out_specs=[once((rows // 2, width))] * 4 + grad_specs,
        scratch_shapes=[pltpu.VMEM((chunk, width), jnp.bfloat16)] * 2 + [pltpu.VMEM((rows, width), jnp.float32)] * 2,
        compiler_params=pltpu.CompilerParams(dimension_semantics=("arbitrary",), vmem_limit_bytes=56 << 20),
        cost_estimate=pl.CostEstimate(flops=int(35e9), transcendentals=0, bytes_accessed=16 << 20),
        name="ffn",
    )(normed, cot, *in_parts, *back_parts)


def over_rows(left_side, right_side):
    return lax.dot_general(
        left_side, right_side, (((0,), (0,)), ((), ())), preferred_element_type=jnp.float32
    )


def against(left_side, right_side):
    return lax.dot_general(
        left_side, right_side, (((1,), (1,)), ((), ())), preferred_element_type=jnp.float32
    )


def matmul(left_side, right_side):
    return jnp.dot(left_side, right_side, preferred_element_type=jnp.float32)


def norm_back(grad_normed, unit_rows, inv_scale, gain_row):
    scaled = grad_normed * gain_row
    return inv_scale * (scaled - unit_rows * jnp.mean(scaled * unit_rows, axis=-1, keepdims=True))


def low(values_in):
    return values_in.astype(jnp.bfloat16)


def wide(values_in):
    return values_in.astype(jnp.float32)


def bits_of(size):
    return [1 << n for n in range(size.bit_length() - 1)]


def tie(*values):
    return lax.optimization_barrier(values)


def finish(steps):
    for step in steps:
        last = step
    return last


def send_or_none(steps, value):
    try:
        return steps.send(value)
    except StopIteration:
        return None


class Slice:
    def __init__(self, mesh):
        self.dp, self.group, self.tensor = (mesh.shape[name] for name in ("dp", "group", "tensor"))

    def swap(self, array, axis, mask):
        size = getattr(self, axis)
        return lax.ppermute(array, axis, [(i, i ^ mask) for i in range(size)])

    def pair_swap(self, array):
        return self.swap(array, "group", 1)

    def row_steps(self):
        return [("group", 2 * bit) for bit in bits_of(self.group // 2)]

    def col_steps(self):
        return [("dp", bit) for bit in bits_of(self.dp)]

    def spread(self, block):
        have = {(0, 0): block}
        size = self.dp * self.group
        for col in range(self.dp):
            for row in range(self.group // 2):
                mask = col * self.group + 2 * row
                if mask:
                    have[col, row] = lax.ppermute(block, ("dp", "group"), [(i, i ^ mask) for i in range(size)])
        return have

    def collect_order(self, rows_first):
        steps = self.row_steps() + self.col_steps() if rows_first else self.col_steps() + self.row_steps()
        return list(reversed(steps))

    def sent_first(self, keys, rows_first):
        return self.sent_first_of(keys, self.collect_order(rows_first)[0])

    def collect(self, keys, kept, sent, rows_first):
        order = self.collect_order(rows_first)
        leaves = self.sent_first(keys, rows_first)
        keys = [key for n, key in enumerate(keys) if n not in leaves]
        units = kept.shape[0] // len(keys)
        for n, (axis, mask) in enumerate(order):
            other = yield self.swap(sent, axis, mask)
            total = low(wide(kept) + wide(other))
            if n + 1 < len(order):
                leaves = self.sent_first_of(keys, order[n + 1])
                block = lambda k: total[k * units:(k + 1) * units]
                pick = lambda ks: block(ks[0]) if len(ks) == 1 else jnp.concatenate([block(k) for k in ks], axis=0)
                kept, sent = pick([k for k in range(len(keys)) if k not in leaves]), pick(list(leaves))
                keys = [key for k, key in enumerate(keys) if k not in leaves]
        yield total

    def sent_first_of(self, keys, step):
        axis, mask = step
        return tuple(n for n, (col, row) in enumerate(keys) if (row & mask // 2 if axis == "group" else col & mask))

    def slot(self):
        rows = self.group // 2
        group = lax.axis_index("group")
        return (group % 2) * (self.dp * rows) + lax.axis_index("dp") * rows + group // 2

    def slot_gather(self, block):
        for axis, mask in self.row_steps() + self.col_steps() + [("group", 1)]:
            upper = (lax.axis_index(axis) // mask) % 2 == 1
            other = self.swap(block, axis, mask)
            yield other
            block = jnp.concatenate((jnp.where(upper, other, block), jnp.where(upper, block, other)), axis=2)
        yield block.reshape(block.shape[0], -1, block.shape[3])

    def plane_sum(self, grad, others):
        mine = lax.axis_index("dp")
        for axis, mask in reversed(self.col_steps()):
            half = grad.shape[0] // 2
            bit = (mine // mask) % 2
            keep = lax.dynamic_slice_in_dim(grad, bit * half, half, 0)
            send = lax.dynamic_slice_in_dim(grad, (1 - bit) * half, half, 0)
            other = self.swap(send, axis, mask)
            grad = low(wide(keep) + wide(other))
        for axis, mask in self.row_steps() + [("group", 1)]:
            other = self.swap(grad, axis, mask)
            if axis == "group" and mask == 2:
                other, others = tie(other, others)
            grad = low(wide(grad) + wide(other))
        return grad[0], others

    def small_sum(self, vector, axes):
        for axis in axes:
            for mask in bits_of(getattr(self, axis)):
                vector = vector + self.swap(vector, axis, mask)
        return vector

    def col_exchange(self, blocks):
        mine = lax.axis_index("dp")
        for axis, mask in reversed(self.col_steps()):
            half = blocks.shape[3] // 2
            upper = (mine // mask) % 2 == 1
            low_half, high_half = blocks[..., :half], blocks[..., half:]
            keep = jnp.where(upper, high_half, low_half)
            other = self.swap(jnp.where(upper, low_half, high_half), axis, mask)
            pair = jnp.where(upper, jnp.stack((other, keep), axis=1), jnp.stack((keep, other), axis=1))
            blocks = pair.reshape((pair.shape[0], -1) + pair.shape[3:])
        if self.dp > 2:
            count, bits = blocks.shape[0], self.dp.bit_length() - 1
            split = blocks.reshape((count,) + (2,) * bits + blocks.shape[2:])
            split = split.transpose((0,) + tuple(range(bits, 0, -1)) + (bits + 1, bits + 2))
            blocks = split.reshape(blocks.shape)
        return blocks

    def group_gather(self, block):
        block = block[None]
        for mask in reversed(bits_of(self.group)):
            upper = (lax.axis_index("group") // mask) % 2 == 1
            other = self.swap(block, "group", mask)
            block = jnp.where(upper, jnp.stack((other, block), axis=1), jnp.stack((block, other), axis=1))
            block = block.reshape((-1,) + block.shape[2:])
        return block

    def col_exchange_rows(self, rows):
        return self.col_exchange(rows[None, None])[0]


def on_device(
    sl,
    inputs,
    segments,
    gain_attn,
    w_query,
    w_key,
    w_value,
    w_out,
    bias_table,
    gain_ffn,
    w_in,
    w_back,
    cotangent,
):
    heads_here = bias_table.shape[1]
    width = inputs.shape[1]
    pairs = heads_here // PAIR
    cols = PAIR * 64
    dp_index, group_index = lax.axis_index("dp"), lax.axis_index("group")
    segment_row = segments.reshape(-1)
    lo, hi = block_bounds(segment_row)
    tiles = bias_tiles(bias_table)

    stream = wide(inputs)
    inv_attn = lax.rsqrt(jnp.mean(stream * stream, axis=-1, keepdims=True) + EPSILON)
    unit_attn = stream * inv_attn
    rows = stream.shape[0]
    units_g = w_back.shape[0] // sl.group
    units = units_g // sl.dp
    start = group_index * units_g + dp_index * units
    plane = sl.dp * sl.group
    slot = sl.slot()
    qkv = [jnp.concatenate([w[:, k * cols:(k + 1) * cols] for w in (w_query, w_key, w_value)], axis=1) for k in range(pairs)]
    n_out, n_qkv = cols // plane, 3 * cols // plane
    own_in = [lax.dynamic_slice_in_dim(w_in, start, units, 1).T]
    own_out = [lax.dynamic_slice_in_dim(w_out, k * cols + slot * n_out, n_out, 0) for k in range(pairs)]
    own_in, own_out = jnp.concatenate(own_in + own_out, axis=0), None
    own_back = lax.dynamic_slice_in_dim(w_back, start, units, 0)
    own_qkv = jnp.concatenate([lax.dynamic_slice_in_dim(qkv[k], slot * n_qkv, n_qkv, 1).T for k in range(pairs)], axis=0)
    cot_pair = jnp.concatenate((cotangent, sl.pair_swap(cotangent)), axis=0)
    prep = (tiles, padded_weights(w_query, w_key, w_value, heads_here), operands(segment_row), cot_pair, pad_heads(w_value, heads_here, 128))
    by_pair = lambda block, rows: block.reshape(sl.tensor, pairs, rows, width).transpose(1, 0, 2, 3)
    in_z = lax.all_gather(own_in, "tensor", axis=0, tiled=False)
    own_normed, in_z = tie(low(unit_attn * gain_attn), in_z)
    normed = lax.all_gather(own_normed, "tensor", axis=0, tiled=True)
    in_parts = sl.spread(in_z[:, :units].reshape(-1, width))
    out_full = finish(sl.slot_gather(by_pair(in_z[:, units:], n_out)))
    own_back = jnp.concatenate((own_back, own_qkv), axis=0)
    own_back, normed, prep, in_parts, qkv, out_full = tie(own_back, normed, prep, in_parts, qkv, out_full)
    tiles, padded, ext, cot_pair, w_vx = prep
    back_z = lax.all_gather(own_back, "tensor", axis=0, tiled=False)

    qx, kx, vt = project(normed, padded, ext, heads_here)
    ctx_t, lse, ctx_got = [], [], []
    for k in range(pairs):
        lo_k = lo
        if k > 0:
            lo_k, back_z, ctx_t[-1] = tie(lo, back_z, ctx_t[-1])
        ctx, total = attn_fwd(k, lo_k, hi, bias_table, qx, kx, vt, tiles)
        ctx_t.append(ctx)
        lse.append(total)
        ctx_got.append(lax.all_to_all(ctx, "tensor", split_axis=1, concat_axis=0, tiled=True))
    back_z, qkv_z = back_z[:, :units].reshape(-1, width), back_z[:, units:]
    back_parts = sl.spread(back_z)
    vx, kt = project_back(normed, w_vx, w_key)
    ctx_rows, vx, kt, back_parts, ctx_t[-1] = tie(ctx_got, vx, kt, back_parts, ctx_t[-1])
    hidden = stream
    for k in range(pairs):
        hidden = hidden + over_rows(ctx_rows[k], out_full[k])
    inv_ffn = lax.rsqrt(jnp.mean(hidden * hidden, axis=-1, keepdims=True) + EPSILON)
    unit_ffn = hidden * inv_ffn

    normed_ffn, qkv_z = tie(low(unit_ffn * gain_ffn), qkv_z)
    qkv_all = lax.all_gather(qkv_z, ("dp", "group"), axis=0, tiled=False)
    normed_pair = jnp.concatenate((normed_ffn, sl.pair_swap(normed_ffn)), axis=0)
    keys = sorted(in_parts)
    results = ffn(
        normed_pair, cot_pair, [in_parts[key] for key in keys], [back_parts[key] for key in keys],
        sl.sent_first(keys, True), sl.sent_first(keys, False),
    )
    out_own, out_mate, normed_own, normed_mate = results[:4]
    in_steps, back_steps = sl.collect(keys, *results[4:6], True), sl.collect(keys, *results[6:8], False)
    normed_own, qkv_all = tie(normed_own, qkv_all)
    grad_normed_ffn = normed_own + wide(sl.pair_swap(normed_mate))
    output = hidden + out_own + wide(sl.pair_swap(out_mate))

    gain_ffn_part = jnp.sum(grad_normed_ffn * unit_ffn, axis=0)
    grad_hidden = wide(cotangent) + norm_back(grad_normed_ffn, unit_ffn, inv_ffn, gain_ffn)
    grad_hidden_low = low(grad_hidden)
    grad_ctx = low(against(out_full.reshape(-1, width), grad_hidden_low)).reshape(pairs, sl.tensor, cols, rows)
    grad_ctx = grad_ctx.transpose(1, 0, 2, 3).reshape(sl.tensor, -1, rows)
    grad_hidden_late, grad_ctx = tie(grad_hidden_low, grad_ctx)
    grad_ctx_t = lax.all_to_all(grad_ctx, "tensor", split_axis=0, concat_axis=2, tiled=True)[0]

    grad_w_out = jnp.stack([low(matmul(ctx_rows[k], grad_hidden_late)) for k in range(pairs)])
    grad_w_out = grad_w_out.reshape(pairs, sl.tensor, cols, width).transpose(1, 0, 2, 3)
    grad_w_out = grad_w_out.reshape(sl.tensor, sl.group, -1, width)

    def out_scatter(grad):
        for mask in bits_of(sl.group):
            grad = grad.reshape((sl.tensor, -1, 2) + grad.shape[2:])
            bit = (group_index // mask) % 2
            keep = lax.dynamic_index_in_dim(grad, bit, 2, keepdims=False)
            other = sl.swap(lax.dynamic_index_in_dim(grad, 1 - bit, 2, keepdims=False), "group", mask)
            other = yield other
            grad = low(wide(keep) + wide(other))
        grad = grad[:, 0]
        for axis, mask in reversed(sl.col_steps()):
            n = grad.shape[1] // 2
            bit = (dp_index // mask) % 2
            keep = lax.dynamic_slice_in_dim(grad, bit * n, n, 1)
            other = sl.swap(lax.dynamic_slice_in_dim(grad, (1 - bit) * n, n, 1), axis, mask)
            other = yield other
            grad = low(wide(keep) + wide(other))
        yield grad

    out_steps = out_scatter(grad_w_out)
    first, grad_ctx_t = tie((next(in_steps), next(back_steps), out_steps.send(next(out_steps))), grad_ctx_t)
    second = [steps.send(other) for steps, other in zip((in_steps, back_steps, out_steps), first)]
    tables, grad_parts, grad_rows = [], [], []
    for k in range(pairs):
        lo_k = lo
        if k == pairs - 1:
            own_sums = []
            if k > 0:
                second, grad_parts[-1] = tie(second, grad_parts[-1])
            for steps, last in zip((in_steps, back_steps, out_steps), second):
                for other in iter(lambda: send_or_none(steps, last), None):
                    last = other
                own_sums.append(last)
            own_sums = jnp.concatenate([part.reshape(sl.tensor, -1, width) for part in own_sums], axis=1)
            lo_k, own_sums = tie(lo, own_sums)
            own_rows = own_sums.shape[1]
            summed = lax.psum_scatter(own_sums.reshape(-1, width), "tensor", scatter_dimension=0, tiled=True)
        grads, diag = attn_bwd(k, lo_k, hi, bias_table, qx, kx, vx, kt, grad_ctx_t, ctx_t[k], lse[k], tiles)
        grad_parts.append(grads)
        if k > 0:
            grads, diag, grad_rows[k - 1] = tie(grads, diag, grad_rows[k - 1])
        grad_rows.append(lax.all_to_all(grads, "tensor", split_axis=0, concat_axis=1, tiled=True))
        tables.append(table_grad(diag, PAIR))

    summed = sl.col_exchange_rows(summed)
    grad_parts = tie(*grad_parts)
    gain_dot, grad_w_qkv = 0.0, []
    for k in range(pairs):
        grad_w = over_rows(normed, grad_parts[k])
        gain_dot = gain_dot + jnp.sum(grad_w * wide(qkv[k]), axis=1)
        grad_w_qkv.append(low(grad_w))

    columns = pairs * 3 * cols
    small = jnp.concatenate([gain_dot / gain_attn, gain_ffn_part] + [table.T.reshape(-1) for table in tables])
    small_rows = -(-small.shape[0] // columns)
    small = low(jnp.pad(small, (0, small_rows * columns - small.shape[0]))).reshape(1, small_rows, columns)
    grad_w_qkv = jnp.concatenate(grad_w_qkv, axis=1).reshape(sl.dp, -1, columns)
    grad_w_qkv = jnp.concatenate((grad_w_qkv, jnp.tile(small, (sl.dp, 1, 1))), axis=1)
    grad_w_qkv, (grad_rows, summed) = sl.plane_sum(grad_w_qkv, (grad_rows, summed))
    small = grad_w_qkv[-small_rows:].reshape(-1)
    grad_w_qkv = wide(grad_w_qkv[:-small_rows])
    gain_grads = sl.small_sum(wide(small[:2 * width]), ("tensor",))
    table_rows = bias_table.shape[0] // sl.dp
    grad_table = wide(small[2 * width:2 * width + bias_table.size]).reshape(heads_here, -1)
    grad_table = lax.dynamic_slice_in_dim(grad_table, dp_index * table_rows, table_rows, 1).T

    everything = sl.group_gather(summed)
    cuts = [0, units, 2 * units, own_rows]
    pick = lambda n: wide(everything[:, :, cuts[n]:cuts[n + 1]].reshape(-1, width // sl.dp))
    grad_w_in, grad_w_back, grad_w_out = pick(0).T, pick(1), pick(2)
    qkv_all = qkv_all.reshape(sl.dp, sl.group // 2, 2, sl.tensor, pairs, n_qkv, width).transpose(4, 3, 2, 0, 1, 5, 6)
    qkv_full = qkv_all.reshape(pairs, -1, width)
    grad_normed = 0.0
    for k in range(pairs):
        grad_normed = grad_normed + matmul(grad_rows[k], qkv_full[k])
    grad_inputs = grad_hidden + norm_back(grad_normed, unit_attn, inv_attn, gain_attn)
    grad_w_query, grad_w_key, grad_w_value = (
        jnp.concatenate([grad_w_qkv[:, (3 * k + n) * cols:(3 * k + n + 1) * cols] for k in range(pairs)], axis=1) for n in range(3)
    )
    return (
        output,
        grad_inputs,
        gain_grads[:width],
        grad_w_query,
        grad_w_key,
        grad_w_value,
        grad_w_out,
        grad_table,
        gain_grads[width:],
        grad_w_in,
        grad_w_back,
    )


def solution(mesh):
    return jax.shard_map(
        functools.partial(on_device, Slice(mesh)),
        mesh=mesh,
        in_specs=(
            P(("dp", "group", "tensor"), None),
            P(("dp", "group"), None),
            P(),
            P(None, "tensor"),
            P(None, "tensor"),
            P(None, "tensor"),
            P("tensor", None),
            P(None, "tensor"),
            P(),
            P(None, "tensor"),
            P("tensor", None),
            P(("dp", "group", "tensor"), None),
        ),
        out_specs=(
            P(("dp", "group", "tensor"), None),
            P(("dp", "group", "tensor"), None),
            P(),
            P("dp", "tensor"),
            P("dp", "tensor"),
            P("dp", "tensor"),
            P("tensor", "dp"),
            P("dp", "tensor"),
            P(),
            P("dp", "tensor"),
            P("tensor", "dp"),
        ),
        check_vma=False,
    )
```

```python
import functools
import math

import jax
import jax.numpy as jnp
from jax import lax
from jax.experimental import pallas as pl
from jax.experimental.pallas import tpu as pltpu
from jax.sharding import PartitionSpec as P

EPSILON = 1e-06

LOG2E = math.log2(math.e)
MASKED = -1e30
TILE = 256
VROWS = 80
PAIR = 2
TN = (((0,), (1,)), ((), ()))
reach_marks = (12, 16, 23, 32, 46, 64, 91)


def bucket_of(offset):
    distance = jnp.abs(offset)
    far_bucket = jnp.full(offset.shape, 8, jnp.int32)
    for threshold in reach_marks:
        far_bucket = far_bucket + (distance >= threshold).astype(jnp.int32)
    return 16 * (offset > 0).astype(jnp.int32) + jnp.where(distance < 8, distance, far_bucket)


def bias_tiles_kernel(heads, table_ref, tile_ref):
    T = TILE
    for d in range(3):
        t = lax.broadcasted_iota(jnp.int32, (8, 2 * T), 1)
        t = jnp.where(t < T, t, t - 2 * T)
        bucket = bucket_of((d - 1) * T - t)
        for h in range(heads):
            row = jnp.zeros((8, 2 * T), jnp.float32)
            for b in range(32):
                row = jnp.where(bucket == b, table_ref[b, h] * LOG2E, row)
            wide = jnp.broadcast_to(row[0:1], (T, 2 * T))
            rolled = pltpu.roll(wide, 0, 1, stride=1, stride_axis=0)
            tile_ref[h * 3 + d] = rolled[:, :T]


def bias_tiles(bias_table):
    heads = bias_table.shape[1]
    return pl.pallas_call(
        functools.partial(bias_tiles_kernel, heads),
        out_shape=jax.ShapeDtypeStruct((heads * 3, TILE, TILE), jnp.float32),
        in_specs=[pl.BlockSpec(memory_space=pltpu.SMEM)],
        out_specs=pl.BlockSpec(memory_space=pltpu.VMEM),
        name="bias_tiles",
    )(bias_table)


def block_loops(i, lo, hi, far, near):
    lax.fori_loop(lo, i - 1, lambda j, _: far(j, 0) or 0, 0)
    lax.fori_loop(jnp.maximum(lo, i - 1), jnp.minimum(hi, i + 1) + 1, lambda j, _: near(j) or 0, 0)
    lax.fori_loop(i + 2, hi + 1, lambda j, _: far(j, 1) or 0, 0)


def attn_fwd_kernel(heads, first, lo_ref, hi_ref, table_ref, qx_ref, kx_ref, vt_ref, tile_ref, o_ref, lse_ref, m_ref, acc_ref, s_ref):
    T = TILE
    i = pl.program_id(0)
    lo, hi = lo_ref[i], hi_ref[i]
    m_ref[...] = jnp.full(m_ref.shape, MASKED, jnp.float32)
    acc_ref[...] = jnp.zeros(acc_ref.shape, jnp.float32)

    def scores(j, bias_of):
        start = pl.multiple_of(j * T, T)
        for h in range(heads):
            k = kx_ref[pl.ds(start, T), h * 128:(h + 1) * 128]
            s = jnp.dot(k, qx_ref[h * 128:(h + 1) * 128, :], preferred_element_type=jnp.float32)
            s = s + bias_of(h)
            s_ref[j - lo, h] = s
            m_ref[h] = jnp.maximum(m_ref[h], jnp.max(s.reshape(T // 8, 8, T), axis=0))

    def far(j, side):
        scores(j, lambda h: table_ref[16 * side + 15, first + h] * LOG2E)

    def near(j):
        scores(j, lambda h: tile_ref[h * 3 + j - i + 1])

    block_loops(i, lo, hi, far, near)
    tops = [jnp.max(m_ref[h], axis=0, keepdims=True) for h in range(heads)]

    def values(j, _):
        start = pl.multiple_of(j * T, T)
        for h in range(heads):
            p = jnp.exp2(s_ref[j - lo, h] - tops[h]).astype(jnp.bfloat16)
            rows = slice(h * VROWS, (h + 1) * VROWS)
            acc_ref[rows, :] += jnp.dot(vt_ref[rows, pl.ds(start, T)], p, preferred_element_type=jnp.float32)
        return 0

    lax.fori_loop(lo, hi + 1, values, 0)
    for h in range(heads):
        total = acc_ref[h * VROWS + 64:h * VROWS + 65, :]
        o_ref[h * 64:(h + 1) * 64, :] = (acc_ref[h * VROWS:h * VROWS + 64, :] / total).astype(jnp.bfloat16)
        lse_ref[h:h + 1, :] = tops[h] + jnp.log2(total)


def attn_cost(seq_len, heads, micros):
    return pl.CostEstimate(flops=int(micros * 1e9), transcendentals=0, bytes_accessed=seq_len * heads * 2048)


def attn_fwd(lo, hi, bias_table, qx, kx, vt, tiles):
    heads = bias_table.shape[1]
    T = TILE
    S = lo.shape[0] * T
    smem = pl.BlockSpec(memory_space=pltpu.SMEM)
    once = lambda shape, index: pl.BlockSpec(shape, lambda i: index, pipeline_mode=pl.Buffered(1))
    return pl.pallas_call(
        functools.partial(attn_fwd_kernel, heads, 0),
        grid=(S // T,),
        out_shape=(jax.ShapeDtypeStruct((heads * 64, S), jnp.bfloat16), jax.ShapeDtypeStruct((8, S), jnp.float32)),
        in_specs=[smem, smem, smem, pl.BlockSpec((heads * 128, T), lambda i: (0, i)), once((S, heads * 128), (0, 0)),
                  once((heads * VROWS, S), (0, 0)), once((heads * 3, T, T), (0, 0, 0))],
        out_specs=(pl.BlockSpec((heads * 64, T), lambda i: (0, i)), pl.BlockSpec((8, T), lambda i: (0, i))),
        scratch_shapes=[pltpu.VMEM((heads, 8, T), jnp.float32), pltpu.VMEM((heads * VROWS, T), jnp.float32),
                        pltpu.VMEM((S // T, heads, T, T), jnp.float32)],
        compiler_params=pltpu.CompilerParams(dimension_semantics=("arbitrary",), vmem_limit_bytes=24 << 20),
        cost_estimate=attn_cost(S, heads, 25),
        name="attn_fwd",
    )(lo, hi, bias_table, qx, kx, vt, tiles)


def attn_bwd_kernel(heads, first, lo_ref, hi_ref, table_ref, qx_ref, kx_ref, vx_ref, kt_ref, dot_ref, ot_ref, lse_ref, tile_ref,
                    grad_ref, diag_ref, d_ref, dqacc_ref, bacc_ref, far_ref, dk_acc, dv_acc):
    T = TILE
    j = pl.program_id(0)
    last = pl.num_programs(0) - 1
    lo, hi = lo_ref[j], hi_ref[j]
    NT = (((1,), (1,)), ((), ()))

    @pl.when(j == 0)
    def _():
        dqacc_ref[...] = jnp.zeros(dqacc_ref.shape, jnp.float32)
        bacc_ref[...] = jnp.zeros(bacc_ref.shape, jnp.float32)
        far_ref[...] = jnp.zeros(far_ref.shape, jnp.float32)
        for h in range(heads):
            rows = slice(h * 64, (h + 1) * 64)
            d_ref[h:h + 1, :] = jnp.sum(dot_ref[rows, :].astype(jnp.float32) * ot_ref[rows, :].astype(jnp.float32), axis=0, keepdims=True)

    dk_acc[...] = jnp.zeros(dk_acc.shape, jnp.float32)
    dv_acc[...] = jnp.zeros(dv_acc.shape, jnp.float32)

    def tile(i, bias_of, sums):
        cols = pl.ds(pl.multiple_of(i * T, T), T)
        for h in range(heads):
            rows = slice(h * 64, (h + 1) * 64)
            q = qx_ref[h * 128:(h + 1) * 128, cols]
            do = dot_ref[rows, cols]
            s = jnp.dot(kx_ref[:, h * 128:(h + 1) * 128], q, preferred_element_type=jnp.float32)
            p = jnp.exp2(s + bias_of(h, lse_ref[first + h:first + h + 1, cols]))
            dp = jnp.dot(vx_ref[:, h * 128:h * 128 + 64], do, preferred_element_type=jnp.float32)
            ds = p * (dp - d_ref[h:h + 1, cols])
            sums(h, ds)
            pb = p.astype(jnp.bfloat16)
            db = ds.astype(jnp.bfloat16)
            dv_acc[h] += lax.dot_general(pb, do, NT, preferred_element_type=jnp.float32)
            dk_acc[h] += lax.dot_general(db, q[:64], NT, preferred_element_type=jnp.float32)
            dqacc_ref[rows, cols] += jnp.dot(kt_ref[rows, :], db, preferred_element_type=jnp.float32)

    def far(i, later):
        side = 1 - later

        def bias_of(h, lse):
            return table_ref[16 * side + 15, first + h] * LOG2E - lse

        def sums(h, ds):
            far_ref[h * 2 + side] += jnp.sum(ds.reshape(T // 8, 8, T), axis=0)
        tile(i, bias_of, sums)

    def near(i):
        def bias_of(h, lse):
            return tile_ref[h * 3 + j - i + 1] - lse

        def sums(h, ds):
            bacc_ref[h * 3 + j - i + 1] += ds
        tile(i, bias_of, sums)

    block_loops(j, lo, hi, far, near)
    HC = heads * 64
    block = pl.ds(pl.multiple_of(j * T, T), T)
    grad_ref[block, HC:2 * HC] = (jnp.concatenate([dk_acc[h] for h in range(heads)], axis=1) * (1.0 / LOG2E)).astype(jnp.bfloat16)
    grad_ref[block, 2 * HC:] = jnp.concatenate([dv_acc[h] for h in range(heads)], axis=1).astype(jnp.bfloat16)

    @pl.when(j == last)
    def _():
        for n in range(dqacc_ref.shape[1] // T):
            grad_ref[n * T:(n + 1) * T, 0:HC] = dqacc_ref[:, n * T:(n + 1) * T].T.astype(jnp.bfloat16)
        zero = jnp.zeros((8, T), jnp.float32)
        sub = lax.broadcasted_iota(jnp.int32, (8, 2 * T), 0)
        for n in range(heads * 3):
            total = jnp.concatenate((bacc_ref[n, 0:8, :], zero), axis=1)
            for g in range(1, T // 8):
                rows = jnp.concatenate((bacc_ref[n, 8 * g:8 * g + 8, :], zero), axis=1)
                total = total + pltpu.roll(rows, 2 * T - 8 * g, 1)
            for bit in (1, 2, 4):
                total = jnp.where((sub & bit) != 0, pltpu.roll(total, 2 * T - bit, 1), total)
            diag_ref[n:n + 1, :] = jnp.sum(total, axis=0, keepdims=True)
        for n in range(heads * 2):
            diag_ref[heads * 3 + n:heads * 3 + n + 1, 0:T] = jnp.sum(far_ref[n], axis=0, keepdims=True)
            diag_ref[heads * 3 + n:heads * 3 + n + 1, T:] = jnp.zeros((1, T), jnp.float32)


def attn_bwd(pair, lo, hi, bias_table, qx, kx, vx, kt, dot, ot, lse, tiles):
    heads = PAIR
    T = TILE
    S = lo.shape[0] * T
    smem = pl.BlockSpec(memory_space=pltpu.SMEM)
    once = lambda shape, index: pl.BlockSpec(shape, lambda i: index, pipeline_mode=pl.Buffered(1))
    rows = lambda n: pl.BlockSpec((T, n), lambda i: (i, pair))
    HC = heads * 64
    return pl.pallas_call(
        functools.partial(attn_bwd_kernel, heads, pair * heads),
        grid=(S // T,),
        out_shape=(jax.ShapeDtypeStruct((S, 3 * HC), jnp.bfloat16), jax.ShapeDtypeStruct((heads * 5, 2 * T), jnp.float32)),
        in_specs=[smem, smem, smem, once((heads * 128, S), (pair, 0)), rows(heads * 128), rows(heads * 128),
                  pl.BlockSpec((HC, T), lambda i: (pair, i)), once((HC, S), (pair, 0)), once((HC, S), (pair, 0)), once((8, S), (0, 0)),
                  once((heads * 3, T, T), (pair, 0, 0))],
        out_specs=(once((S, 3 * HC), (0, 0)), once((heads * 5, 2 * T), (0, 0))),
        scratch_shapes=[pltpu.VMEM((8, S), jnp.float32), pltpu.VMEM((HC, S), jnp.float32),
                        pltpu.VMEM((heads * 3, T, T), jnp.float32), pltpu.VMEM((heads * 2, 8, T), jnp.float32),
                        pltpu.VMEM((heads, T, 64), jnp.float32), pltpu.VMEM((heads, T, 64), jnp.float32)],
        compiler_params=pltpu.CompilerParams(dimension_semantics=("arbitrary",), vmem_limit_bytes=60 << 20),
        cost_estimate=attn_cost(S, heads, 24),
        name="attn_bwd",
    )(lo, hi, bias_table, qx, kx, vx, kt, dot, ot, lse, tiles)


def table_grad(diag, heads):
    T = TILE
    t = jnp.arange(2 * T, dtype=jnp.int32)
    t = jnp.where(t < T, t, t - 2 * T)
    d = jnp.arange(3, dtype=jnp.int32)
    bucket = bucket_of((d[:, None] - 1) * T - t[None, :])
    onehot = (bucket[:, :, None] == jnp.arange(32, dtype=jnp.int32)).astype(jnp.float32)
    near = jnp.einsum("hdt,dtb->bh", diag[:heads * 3].reshape(heads, 3, 2 * T), onehot, precision=lax.Precision.HIGHEST)
    far = jnp.sum(diag[heads * 3:].reshape(heads, 2, 2 * T), axis=2)
    ids = jnp.arange(32, dtype=jnp.int32)[:, None]
    return near + jnp.where(ids == 15, far[None, :, 0], 0.0) + jnp.where(ids == 31, far[None, :, 1], 0.0)


def block_bounds(segment_row):
    S = segment_row.shape[0]
    blocks = segment_row.reshape(S // TILE, TILE)
    first, final = blocks[:, 0], blocks[:, TILE - 1]
    lo = jnp.sum((segment_row[None, :] < first[:, None]).astype(jnp.int32), axis=1) // TILE
    hi = (jnp.sum((segment_row[None, :] <= final[:, None]).astype(jnp.int32), axis=1) - 1) // TILE
    return lo, hi


def pad_heads(w, heads, width):
    D = w.shape[0]
    return jnp.pad(w.reshape(D, heads, 64), ((0, 0), (0, 0), (0, width - 64))).reshape(D, heads * width)


def operands(segment_row):
    S = segment_row.shape[0]
    row = jnp.arange(128, dtype=jnp.int32)
    same = segment_row[None, :] == (row[:, None] - 64)
    inside = (row >= 64) & (row < 80)
    qext = jnp.where(inside[:, None] & same, 1.0, 0.0)
    kext = jnp.where(inside[None, :] & ~same.T, MASKED, 0.0)
    vext = jnp.where(jnp.arange(VROWS) == 64, 1.0, 0.0)[:, None]
    return qext, kext, vext


def padded_weights(w_query, w_key, w_value, heads):
    return pad_heads(w_query, heads, 128), pad_heads(w_key, heads, 128), pad_heads(w_value, heads, VROWS)


def project(normed, weights, ext, heads):
    (qext, kext, vext), (wq, wk, wv) = ext, weights
    f32 = jnp.float32
    qx = lax.dot_general(wq, normed, TN, preferred_element_type=f32) * LOG2E
    qx = (qx + jnp.tile(qext, (heads, 1))).astype(jnp.bfloat16)
    kx = jnp.dot(normed, wk, preferred_element_type=f32)
    kx = (kx + jnp.tile(kext, (1, heads))).astype(jnp.bfloat16)
    vt = lax.dot_general(wv, normed, TN, preferred_element_type=f32)
    vt = (vt + jnp.tile(vext, (heads, 1))).astype(jnp.bfloat16)
    return qx, kx, vt


def project_back(normed, w_vx, w_key):
    vx = jnp.dot(normed, w_vx, preferred_element_type=jnp.float32).astype(jnp.bfloat16)
    kt = lax.dot_general(w_key, normed, TN, preferred_element_type=jnp.float32).astype(jnp.bfloat16)
    return vx, kt


CHUNK = 256
ROOT = math.sqrt(2 / math.pi)


def ffn_kernel(parts, per_part, in_sent, back_sent, n_ref, c_ref, *refs):
    in_refs, back_refs = refs[:parts], refs[parts:2 * parts]
    out_ref, out_mate_ref, norm_ref, norm_mate_ref = refs[2 * parts:2 * parts + 4]
    gin_refs, gback_refs = refs[2 * parts + 4:2 * parts + 6], refs[2 * parts + 6:2 * parts + 8]
    w_in, w_back, out_acc, norm_acc = refs[2 * parts + 8:]
    step = pl.program_id(0)
    f32, bf16 = jnp.float32, jnp.bfloat16
    NT = (((1,), (1,)), ((), ()))
    TN = (((0,), (0,)), ((), ()))

    @pl.when(step == 0)
    def _():
        out_acc[...] = jnp.zeros(out_acc.shape, f32)
        norm_acc[...] = jnp.zeros(norm_acc.shape, f32)

    for q in range(parts):
        @pl.when(step // per_part == q)
        def _():
            w_in[...] = in_refs[q][...]
            w_back[...] = back_refs[q][...]

    rows = n_ref.shape[0]
    inner = lax.dot_general(n_ref[...], w_in[...], NT, preferred_element_type=f32)
    cube = inner * inner * 0.044715
    th = jnp.tanh(ROOT * inner * (1.0 + cube))
    half = 0.5 * (1.0 + th)
    active = (inner * half).astype(bf16)
    slope = half + (0.5 * ROOT) * inner * (1.0 - th * th) * (1.0 + 3.0 * cube)
    grad = (lax.dot_general(c_ref[...], w_back[...], NT, preferred_element_type=f32) * slope).astype(bf16)
    norm_acc[...] += jnp.dot(grad, w_in[...], preferred_element_type=f32)
    out_acc[...] += jnp.dot(active, w_back[...], preferred_element_type=f32)
    gin = lax.dot_general(grad, n_ref[...], TN, preferred_element_type=f32).astype(bf16)
    gback = lax.dot_general(active, c_ref[...], TN, preferred_element_type=f32).astype(bf16)
    part = step // per_part
    for grad_refs, value, sent in ((gin_refs, gin, in_sent), (gback_refs, gback, back_sent)):
        leaves = functools.reduce(jnp.logical_or, [part == q for q in sent], False)

        @pl.when(leaves)
        def _():
            grad_refs[1][...] = value

        @pl.when(jnp.logical_not(leaves))
        def _():
            grad_refs[0][...] = value

    @pl.when(step == pl.num_programs(0) - 1)
    def _():
        own = out_ref.shape[0]
        out_ref[...] = out_acc[:own, :]
        out_mate_ref[...] = out_acc[own:, :].astype(bf16)
        norm_ref[...] = norm_acc[:own, :]
        norm_mate_ref[...] = norm_acc[own:, :].astype(bf16)


def ffn(normed, cot, in_parts, back_parts, in_sent, back_sent):
    parts = len(in_parts)
    units, width = in_parts[0].shape
    rows = normed.shape[0]
    chunk = min(CHUNK, units)
    per_part = units // chunk
    once = lambda shape: pl.BlockSpec(shape, lambda i: (0, 0), pipeline_mode=pl.Buffered(1))
    piece = lambda q: pl.BlockSpec((chunk, width), lambda i: (jnp.clip(i - q * per_part, 0, per_part - 1), 0))
    weights = [piece(q) for q in range(parts)]
    sums = [jax.ShapeDtypeStruct((rows // 2, width), kind) for kind in (jnp.float32, jnp.bfloat16)]
    grads, grad_specs = [], []
    for sent in (in_sent, back_sent):
        for members in ([q for q in range(parts) if q not in sent], list(sent)):
            steps = [q * per_part + n for q in members for n in range(per_part)]
            index = lambda i, ups=tuple(steps[1:]): (sum([(i >= up).astype(jnp.int32) for up in ups], jnp.int32(0)), 0)
            grads.append(jax.ShapeDtypeStruct((len(members) * units, width), jnp.bfloat16))
            grad_specs.append(pl.BlockSpec((chunk, width), index))
    return pl.pallas_call(
        functools.partial(ffn_kernel, parts, per_part, in_sent, back_sent),
        grid=(parts * per_part,),
        out_shape=sums * 2 + grads,
        in_specs=[once((rows, width)), once((rows, width))] + weights * 2,
        out_specs=[once((rows // 2, width))] * 4 + grad_specs,
        scratch_shapes=[pltpu.VMEM((chunk, width), jnp.bfloat16)] * 2 + [pltpu.VMEM((rows, width), jnp.float32)] * 2,
        compiler_params=pltpu.CompilerParams(dimension_semantics=("arbitrary",), vmem_limit_bytes=60 << 20),
        cost_estimate=pl.CostEstimate(flops=int(35e9), transcendentals=0, bytes_accessed=16 << 20),
        name="ffn",
    )(normed, cot, *in_parts, *back_parts)


def over_rows(left_side, right_side):
    return lax.dot_general(
        left_side, right_side, (((0,), (0,)), ((), ())), preferred_element_type=jnp.float32
    )


def against(left_side, right_side):
    return lax.dot_general(
        left_side, right_side, (((1,), (1,)), ((), ())), preferred_element_type=jnp.float32
    )


def matmul(left_side, right_side):
    return jnp.dot(left_side, right_side, preferred_element_type=jnp.float32)


def norm_back(grad_normed, unit_rows, inv_scale, gain_row):
    scaled = grad_normed * gain_row
    return inv_scale * (scaled - unit_rows * jnp.mean(scaled * unit_rows, axis=-1, keepdims=True))


def low(values_in):
    return values_in.astype(jnp.bfloat16)


def wide(values_in):
    return values_in.astype(jnp.float32)


def bits_of(size):
    return [1 << n for n in range(size.bit_length() - 1)]


def tie(*values):
    return lax.optimization_barrier(values)


def finish(steps):
    for step in steps:
        last = step
    return last


def send_or_none(steps, value):
    try:
        return steps.send(value)
    except StopIteration:
        return None


class Slice:
    def __init__(self, mesh):
        self.dp, self.group, self.tensor = (mesh.shape[name] for name in ("dp", "group", "tensor"))

    def swap(self, array, axis, mask):
        size = getattr(self, axis)
        return lax.ppermute(array, axis, [(i, i ^ mask) for i in range(size)])

    def pair_swap(self, array):
        return self.swap(array, "group", 1)

    def row_steps(self):
        return [("group", 2 * bit) for bit in bits_of(self.group // 2)]

    def col_steps(self):
        return [("dp", bit) for bit in bits_of(self.dp)]

    def spread(self, block):
        have = {(0, 0): block}
        size = self.dp * self.group
        for col in range(self.dp):
            for row in range(self.group // 2):
                mask = col * self.group + 2 * row
                if mask:
                    have[col, row] = lax.ppermute(block, ("dp", "group"), [(i, i ^ mask) for i in range(size)])
        return have

    def collect_order(self, rows_first):
        steps = self.row_steps() + self.col_steps() if rows_first else self.col_steps() + self.row_steps()
        return list(reversed(steps))

    def sent_first(self, keys, rows_first):
        return self.sent_first_of(keys, self.collect_order(rows_first)[0])

    def collect(self, keys, kept, sent, rows_first):
        order = self.collect_order(rows_first)
        leaves = self.sent_first(keys, rows_first)
        keys = [key for n, key in enumerate(keys) if n not in leaves]
        units = kept.shape[0] // len(keys)
        for n, (axis, mask) in enumerate(order):
            other = yield self.swap(sent, axis, mask)
            total = low(wide(kept) + wide(other))
            if n + 1 < len(order):
                leaves = self.sent_first_of(keys, order[n + 1])
                block = lambda k: total[k * units:(k + 1) * units]
                pick = lambda ks: block(ks[0]) if len(ks) == 1 else jnp.concatenate([block(k) for k in ks], axis=0)
                kept, sent = pick([k for k in range(len(keys)) if k not in leaves]), pick(list(leaves))
                keys = [key for k, key in enumerate(keys) if k not in leaves]
        yield total

    def sent_first_of(self, keys, step):
        axis, mask = step
        return tuple(n for n, (col, row) in enumerate(keys) if (row & mask // 2 if axis == "group" else col & mask))

    def slot(self):
        rows = self.group // 2
        group = lax.axis_index("group")
        return (group % 2) * (self.dp * rows) + lax.axis_index("dp") * rows + group // 2

    def slot_gather(self, block):
        for axis, mask in self.row_steps() + self.col_steps() + [("group", 1)]:
            upper = (lax.axis_index(axis) // mask) % 2 == 1
            other = self.swap(block, axis, mask)
            yield other
            block = jnp.concatenate((jnp.where(upper, other, block), jnp.where(upper, block, other)), axis=2)
        yield block.reshape(block.shape[0], -1, block.shape[3])

    def plane_sum(self, grad, others):
        mine = lax.axis_index("dp")
        for axis, mask in reversed(self.col_steps()):
            half = grad.shape[0] // 2
            bit = (mine // mask) % 2
            keep = lax.dynamic_slice_in_dim(grad, bit * half, half, 0)
            send = lax.dynamic_slice_in_dim(grad, (1 - bit) * half, half, 0)
            other = self.swap(send, axis, mask)
            grad = low(wide(keep) + wide(other))
        for axis, mask in self.row_steps() + [("group", 1)]:
            other = self.swap(grad, axis, mask)
            if axis == "group" and mask == 2:
                other, others = tie(other, others)
            grad = low(wide(grad) + wide(other))
        return grad[0], others

    def small_sum(self, vector, axes):
        for axis in axes:
            for mask in bits_of(getattr(self, axis)):
                vector = vector + self.swap(vector, axis, mask)
        return vector

    def col_exchange(self, blocks):
        mine = lax.axis_index("dp")
        for axis, mask in reversed(self.col_steps()):
            half = blocks.shape[3] // 2
            upper = (mine // mask) % 2 == 1
            low_half, high_half = blocks[..., :half], blocks[..., half:]
            keep = jnp.where(upper, high_half, low_half)
            other = self.swap(jnp.where(upper, low_half, high_half), axis, mask)
            pair = jnp.where(upper, jnp.stack((other, keep), axis=1), jnp.stack((keep, other), axis=1))
            blocks = pair.reshape((pair.shape[0], -1) + pair.shape[3:])
        if self.dp > 2:
            count, bits = blocks.shape[0], self.dp.bit_length() - 1
            split = blocks.reshape((count,) + (2,) * bits + blocks.shape[2:])
            split = split.transpose((0,) + tuple(range(bits, 0, -1)) + (bits + 1, bits + 2))
            blocks = split.reshape(blocks.shape)
        return blocks

    def group_gather(self, block):
        block = block[None]
        for mask in reversed(bits_of(self.group)):
            upper = (lax.axis_index("group") // mask) % 2 == 1
            other = self.swap(block, "group", mask)
            block = jnp.where(upper, jnp.stack((other, block), axis=1), jnp.stack((block, other), axis=1))
            block = block.reshape((-1,) + block.shape[2:])
        return block

    def col_exchange_rows(self, rows):
        return self.col_exchange(rows[None, None])[0]


def on_device(
    sl,
    inputs,
    segments,
    gain_attn,
    w_query,
    w_key,
    w_value,
    w_out,
    bias_table,
    gain_ffn,
    w_in,
    w_back,
    cotangent,
):
    heads_here = bias_table.shape[1]
    width = inputs.shape[1]
    pairs = heads_here // PAIR
    cols = PAIR * 64
    dp_index, group_index = lax.axis_index("dp"), lax.axis_index("group")
    segment_row = segments.reshape(-1)
    lo, hi = block_bounds(segment_row)
    tiles = bias_tiles(bias_table)

    stream = wide(inputs)
    inv_attn = lax.rsqrt(jnp.mean(stream * stream, axis=-1, keepdims=True) + EPSILON)
    unit_attn = stream * inv_attn
    rows = stream.shape[0]
    units_g = w_back.shape[0] // sl.group
    units = units_g // sl.dp
    start = group_index * units_g + dp_index * units
    plane = sl.dp * sl.group
    slot = sl.slot()
    qkv = [jnp.concatenate([w[:, k * cols:(k + 1) * cols] for w in (w_query, w_key, w_value)], axis=1) for k in range(pairs)]
    n_out, n_qkv = w_out.shape[0] // plane, 3 * cols // plane
    own_in = [lax.dynamic_slice_in_dim(w_in, start, units, 1).T]
    own_in.append(lax.dynamic_slice_in_dim(w_out, slot * n_out, n_out, 0))
    own_in = jnp.concatenate(own_in, axis=0)
    own_back = lax.dynamic_slice_in_dim(w_back, start, units, 0)
    own_qkv = jnp.concatenate([lax.dynamic_slice_in_dim(qkv[k], slot * n_qkv, n_qkv, 1).T for k in range(pairs)], axis=0)
    cot_pair = jnp.concatenate((cotangent, sl.pair_swap(cotangent)), axis=0)
    prep = (tiles, padded_weights(w_query, w_key, w_value, heads_here), operands(segment_row), cot_pair, pad_heads(w_value, heads_here, 128))
    by_pair = lambda block, rows: block.reshape(sl.tensor, pairs, rows, width).transpose(1, 0, 2, 3)
    in_z = lax.all_gather(own_in, "tensor", axis=0, tiled=False)
    own_normed, in_z = tie(low(unit_attn * gain_attn), in_z)
    normed = lax.all_gather(own_normed, "tensor", axis=0, tiled=True)
    in_parts = sl.spread(in_z[:, :units].reshape(-1, width))
    out_full = finish(sl.slot_gather(in_z[:, units:][None]))[0]
    own_back = jnp.concatenate((own_back, own_qkv), axis=0)
    own_back, normed, prep, in_parts, qkv, out_full = tie(own_back, normed, prep, in_parts, qkv, out_full)
    tiles, padded, ext, cot_pair, w_vx = prep
    back_z = lax.all_gather(own_back, "tensor", axis=0, tiled=False)

    qx, kx, vt = project(normed, padded, ext, heads_here)
    ctx_t, lse = attn_fwd(lo, hi, bias_table, qx, kx, vt, tiles)
    back_z, ctx_t = tie(back_z, ctx_t)
    ctx_rows = lax.all_to_all(ctx_t, "tensor", split_axis=1, concat_axis=0, tiled=True)
    back_z, qkv_z = back_z[:, :units].reshape(-1, width), back_z[:, units:]
    back_parts = sl.spread(back_z)
    vx, kt = project_back(normed, w_vx, w_key)
    ctx_rows, vx, kt = tie(ctx_rows, vx, kt)
    hidden = stream + over_rows(ctx_rows, out_full)
    inv_ffn = lax.rsqrt(jnp.mean(hidden * hidden, axis=-1, keepdims=True) + EPSILON)
    unit_ffn = hidden * inv_ffn

    normed_ffn, qkv_z, back_parts = tie(low(unit_ffn * gain_ffn), qkv_z, back_parts)
    qkv_all = lax.all_gather(qkv_z, ("dp", "group"), axis=0, tiled=False)
    normed_pair = jnp.concatenate((normed_ffn, sl.pair_swap(normed_ffn)), axis=0)
    keys = sorted(in_parts)
    results = ffn(
        normed_pair, cot_pair, [in_parts[key] for key in keys], [back_parts[key] for key in keys],
        sl.sent_first(keys, True), sl.sent_first(keys, False),
    )
    out_own, out_mate, normed_own, normed_mate = results[:4]
    in_steps, back_steps = sl.collect(keys, *results[4:6], True), sl.collect(keys, *results[6:8], False)
    normed_own, qkv_all = tie(normed_own, qkv_all)
    grad_normed_ffn = normed_own + wide(sl.pair_swap(normed_mate))
    output = hidden + out_own + wide(sl.pair_swap(out_mate))

    gain_ffn_part = jnp.sum(grad_normed_ffn * unit_ffn, axis=0)
    grad_hidden = wide(cotangent) + norm_back(grad_normed_ffn, unit_ffn, inv_ffn, gain_ffn)
    grad_hidden_low = low(grad_hidden)
    grad_ctx = low(against(out_full, grad_hidden_low))
    grad_hidden_late, grad_ctx = tie(grad_hidden_low, grad_ctx)
    grad_ctx_t = lax.all_to_all(grad_ctx, "tensor", split_axis=0, concat_axis=1, tiled=True)

    grad_w_out = low(matmul(ctx_rows, grad_hidden_late)).reshape(sl.tensor, sl.group, -1, width)

    def out_scatter(grad):
        for mask in bits_of(sl.group):
            grad = grad.reshape((sl.tensor, -1, 2) + grad.shape[2:])
            bit = (group_index // mask) % 2
            keep = lax.dynamic_index_in_dim(grad, bit, 2, keepdims=False)
            other = sl.swap(lax.dynamic_index_in_dim(grad, 1 - bit, 2, keepdims=False), "group", mask)
            other = yield other
            grad = low(wide(keep) + wide(other))
        grad = grad[:, 0]
        for axis, mask in reversed(sl.col_steps()):
            n = grad.shape[1] // 2
            bit = (dp_index // mask) % 2
            keep = lax.dynamic_slice_in_dim(grad, bit * n, n, 1)
            other = sl.swap(lax.dynamic_slice_in_dim(grad, (1 - bit) * n, n, 1), axis, mask)
            other = yield other
            grad = low(wide(keep) + wide(other))
        yield grad

    out_steps = out_scatter(grad_w_out)
    first, grad_ctx_t = tie((next(in_steps), next(back_steps), next(out_steps)), grad_ctx_t)
    second = [steps.send(other) for steps, other in zip((in_steps, back_steps, out_steps), first)]
    tables, grad_parts, grad_rows = [], [], []
    for k in range(pairs):
        lo_k = lo
        if k == pairs - 1:
            own_sums = []
            if k > 0:
                second, grad_parts[-1] = tie(second, grad_parts[-1])
            for steps, last in zip((in_steps, back_steps, out_steps), second):
                for other in iter(lambda: send_or_none(steps, last), None):
                    last = other
                own_sums.append(last)
            own_sums = jnp.concatenate([part.reshape(sl.tensor, -1, width) for part in own_sums], axis=1)
            lo_k, own_sums = tie(lo, own_sums)
            own_rows = own_sums.shape[1]
            summed = lax.psum_scatter(own_sums.reshape(-1, width), "tensor", scatter_dimension=0, tiled=True)
        grads, diag = attn_bwd(k, lo_k, hi, bias_table, qx, kx, vx, kt, grad_ctx_t, ctx_t, lse, tiles)
        grad_parts.append(grads)
        if k > 0:
            grads, diag, grad_rows[k - 1] = tie(grads, diag, grad_rows[k - 1])
        grad_rows.append(lax.all_to_all(grads, "tensor", split_axis=0, concat_axis=1, tiled=True))
        tables.append(table_grad(diag, PAIR))

    summed = sl.col_exchange_rows(summed)
    grad_parts = tie(*grad_parts)
    gain_dot, grad_w_qkv = 0.0, []
    for k in range(pairs):
        grad_w = over_rows(normed, grad_parts[k])
        gain_dot = gain_dot + jnp.sum(grad_w * wide(qkv[k]), axis=1)
        grad_w_qkv.append(low(grad_w))

    columns = pairs * 3 * cols
    small = jnp.concatenate([gain_dot / gain_attn, gain_ffn_part] + [table.T.reshape(-1) for table in tables])
    small_rows = -(-small.shape[0] // columns)
    small = low(jnp.pad(small, (0, small_rows * columns - small.shape[0]))).reshape(1, small_rows, columns)
    grad_w_qkv = jnp.concatenate(grad_w_qkv, axis=1).reshape(sl.dp, -1, columns)
    grad_w_qkv = jnp.concatenate((grad_w_qkv, jnp.tile(small, (sl.dp, 1, 1))), axis=1)
    grad_w_qkv, (grad_rows, summed) = sl.plane_sum(grad_w_qkv, (grad_rows, summed))
    small = grad_w_qkv[-small_rows:].reshape(-1)
    grad_w_qkv = wide(grad_w_qkv[:-small_rows])
    gain_grads = sl.small_sum(wide(small[:2 * width]), ("tensor",))
    table_rows = bias_table.shape[0] // sl.dp
    grad_table = wide(small[2 * width:2 * width + bias_table.size]).reshape(heads_here, -1)
    grad_table = lax.dynamic_slice_in_dim(grad_table, dp_index * table_rows, table_rows, 1).T

    everything = sl.group_gather(summed)
    cuts = [0, units, 2 * units, own_rows]
    pick = lambda n: wide(everything[:, :, cuts[n]:cuts[n + 1]].reshape(-1, width // sl.dp))
    grad_w_in, grad_w_back, grad_w_out = pick(0).T, pick(1), pick(2)
    qkv_all = qkv_all.reshape(sl.dp, sl.group // 2, 2, sl.tensor, pairs, n_qkv, width).transpose(4, 3, 2, 0, 1, 5, 6)
    qkv_full = qkv_all.reshape(pairs, -1, width)
    grad_normed = 0.0
    for k in range(pairs):
        grad_normed = grad_normed + matmul(grad_rows[k], qkv_full[k])
    grad_inputs = grad_hidden + norm_back(grad_normed, unit_attn, inv_attn, gain_attn)
    grad_w_query, grad_w_key, grad_w_value = (
        jnp.concatenate([grad_w_qkv[:, (3 * k + n) * cols:(3 * k + n + 1) * cols] for k in range(pairs)], axis=1) for n in range(3)
    )
    return (
        output,
        grad_inputs,
        gain_grads[:width],
        grad_w_query,
        grad_w_key,
        grad_w_value,
        grad_w_out,
        grad_table,
        gain_grads[width:],
        grad_w_in,
        grad_w_back,
    )


def solution(mesh):
    return jax.shard_map(
        functools.partial(on_device, Slice(mesh)),
        mesh=mesh,
        in_specs=(
            P(("dp", "group", "tensor"), None),
            P(("dp", "group"), None),
            P(),
            P(None, "tensor"),
            P(None, "tensor"),
            P(None, "tensor"),
            P("tensor", None),
            P(None, "tensor"),
            P(),
            P(None, "tensor"),
            P("tensor", None),
            P(("dp", "group", "tensor"), None),
        ),
        out_specs=(
            P(("dp", "group", "tensor"), None),
            P(("dp", "group", "tensor"), None),
            P(),
            P("dp", "tensor"),
            P("dp", "tensor"),
            P("dp", "tensor"),
            P("tensor", "dp"),
            P("dp", "tensor"),
            P(),
            P("dp", "tensor"),
            P("tensor", "dp"),
        ),
        check_vma=False,
    )
```

```python
import functools
import math

import jax
import jax.numpy as jnp
from jax import lax
from jax.experimental import pallas as pl
from jax.experimental.pallas import tpu as pltpu
from jax.sharding import PartitionSpec as P

EPSILON = 1e-06

LOG2E = math.log2(math.e)
MASKED = -1e30
TILE = 256
VROWS = 80
PAIR = 2
TN = (((0,), (1,)), ((), ()))
reach_marks = (12, 16, 23, 32, 46, 64, 91)


def bucket_of(offset):
    distance = jnp.abs(offset)
    far_bucket = jnp.full(offset.shape, 8, jnp.int32)
    for threshold in reach_marks:
        far_bucket = far_bucket + (distance >= threshold).astype(jnp.int32)
    return 16 * (offset > 0).astype(jnp.int32) + jnp.where(distance < 8, distance, far_bucket)


def bias_tiles_kernel(heads, table_ref, tile_ref):
    T = TILE
    for d in range(3):
        t = lax.broadcasted_iota(jnp.int32, (8, 2 * T), 1)
        t = jnp.where(t < T, t, t - 2 * T)
        bucket = bucket_of((d - 1) * T - t)
        for h in range(heads):
            row = jnp.zeros((8, 2 * T), jnp.float32)
            for b in range(32):
                row = jnp.where(bucket == b, table_ref[b, h] * LOG2E, row)
            wide = jnp.broadcast_to(row[0:1], (T, 2 * T))
            rolled = pltpu.roll(wide, 0, 1, stride=1, stride_axis=0)
            tile_ref[h * 3 + d] = rolled[:, :T]


def bias_tiles(bias_table):
    heads = bias_table.shape[1]
    return pl.pallas_call(
        functools.partial(bias_tiles_kernel, heads),
        out_shape=jax.ShapeDtypeStruct((heads * 3, TILE, TILE), jnp.float32),
        in_specs=[pl.BlockSpec(memory_space=pltpu.SMEM)],
        out_specs=pl.BlockSpec(memory_space=pltpu.VMEM),
        name="bias_tiles",
    )(bias_table)


def block_loops(i, lo, hi, far, near):
    lax.fori_loop(lo, i - 1, lambda j, _: far(j, 0) or 0, 0)
    lax.fori_loop(jnp.maximum(lo, i - 1), jnp.minimum(hi, i + 1) + 1, lambda j, _: near(j) or 0, 0)
    lax.fori_loop(i + 2, hi + 1, lambda j, _: far(j, 1) or 0, 0)


def attn_fwd_kernel(heads, first, lo_ref, hi_ref, table_ref, qx_ref, kx_ref, vt_ref, tile_ref, o_ref, lse_ref, m_ref, acc_ref, s_ref):
    T = TILE
    i = pl.program_id(0)
    lo, hi = lo_ref[i], hi_ref[i]
    m_ref[...] = jnp.full(m_ref.shape, MASKED, jnp.float32)
    acc_ref[...] = jnp.zeros(acc_ref.shape, jnp.float32)

    def scores(j, bias_of):
        start = pl.multiple_of(j * T, T)
        for h in range(heads):
            k = kx_ref[pl.ds(start, T), h * 128:(h + 1) * 128]
            s = jnp.dot(k, qx_ref[h * 128:(h + 1) * 128, :], preferred_element_type=jnp.float32)
            s = s + bias_of(h)
            s_ref[j - lo, h] = s
            m_ref[h] = jnp.maximum(m_ref[h], jnp.max(s.reshape(T // 8, 8, T), axis=0))

    def far(j, side):
        scores(j, lambda h: table_ref[16 * side + 15, first + h] * LOG2E)

    def near(j):
        scores(j, lambda h: tile_ref[h * 3 + j - i + 1])

    block_loops(i, lo, hi, far, near)
    tops = [jnp.max(m_ref[h], axis=0, keepdims=True) for h in range(heads)]

    def values(j, _):
        start = pl.multiple_of(j * T, T)
        for h in range(heads):
            p = jnp.exp2(s_ref[j - lo, h] - tops[h]).astype(jnp.bfloat16)
            rows = slice(h * VROWS, (h + 1) * VROWS)
            acc_ref[rows, :] += jnp.dot(vt_ref[rows, pl.ds(start, T)], p, preferred_element_type=jnp.float32)
        return 0

    lax.fori_loop(lo, hi + 1, values, 0)
    for h in range(heads):
        total = acc_ref[h * VROWS + 64:h * VROWS + 65, :]
        o_ref[h * 64:(h + 1) * 64, :] = (acc_ref[h * VROWS:h * VROWS + 64, :] / total).astype(jnp.bfloat16)
        lse_ref[h:h + 1, :] = tops[h] + jnp.log2(total)


def attn_cost(seq_len, heads, micros):
    return pl.CostEstimate(flops=int(micros * 1e9), transcendentals=0, bytes_accessed=seq_len * heads * 2048)


def attn_fwd(lo, hi, bias_table, qx, kx, vt, tiles):
    heads = bias_table.shape[1]
    T = TILE
    S = lo.shape[0] * T
    smem = pl.BlockSpec(memory_space=pltpu.SMEM)
    once = lambda shape, index: pl.BlockSpec(shape, lambda i: index, pipeline_mode=pl.Buffered(1))
    return pl.pallas_call(
        functools.partial(attn_fwd_kernel, heads, 0),
        grid=(S // T,),
        out_shape=(jax.ShapeDtypeStruct((heads * 64, S), jnp.bfloat16), jax.ShapeDtypeStruct((8, S), jnp.float32)),
        in_specs=[smem, smem, smem, pl.BlockSpec((heads * 128, T), lambda i: (0, i)), once((S, heads * 128), (0, 0)),
                  once((heads * VROWS, S), (0, 0)), once((heads * 3, T, T), (0, 0, 0))],
        out_specs=(pl.BlockSpec((heads * 64, T), lambda i: (0, i)), pl.BlockSpec((8, T), lambda i: (0, i))),
        scratch_shapes=[pltpu.VMEM((heads, 8, T), jnp.float32), pltpu.VMEM((heads * VROWS, T), jnp.float32),
                        pltpu.VMEM((S // T, heads, T, T), jnp.float32)],
        compiler_params=pltpu.CompilerParams(dimension_semantics=("arbitrary",), vmem_limit_bytes=24 << 20),
        cost_estimate=attn_cost(S, heads, 25),
        name="attn_fwd",
    )(lo, hi, bias_table, qx, kx, vt, tiles)


def attn_bwd_kernel(heads, first, lo_ref, hi_ref, table_ref, qx_ref, kx_ref, vx_ref, kt_ref, dot_ref, ot_ref, lse_ref, tile_ref,
                    grad_ref, diag_ref, d_ref, dqacc_ref, bacc_ref, far_ref, dk_acc, dv_acc):
    T = TILE
    j = pl.program_id(0)
    last = pl.num_programs(0) - 1
    lo, hi = lo_ref[j], hi_ref[j]
    NT = (((1,), (1,)), ((), ()))

    @pl.when(j == 0)
    def _():
        dqacc_ref[...] = jnp.zeros(dqacc_ref.shape, jnp.float32)
        bacc_ref[...] = jnp.zeros(bacc_ref.shape, jnp.float32)
        far_ref[...] = jnp.zeros(far_ref.shape, jnp.float32)
        for h in range(heads):
            rows = slice(h * 64, (h + 1) * 64)
            d_ref[h:h + 1, :] = jnp.sum(dot_ref[rows, :].astype(jnp.float32) * ot_ref[rows, :].astype(jnp.float32), axis=0, keepdims=True)

    dk_acc[...] = jnp.zeros(dk_acc.shape, jnp.float32)
    dv_acc[...] = jnp.zeros(dv_acc.shape, jnp.float32)

    def tile(i, bias_of, sums):
        cols = pl.ds(pl.multiple_of(i * T, T), T)
        for h in range(heads):
            rows = slice(h * 64, (h + 1) * 64)
            q = qx_ref[h * 128:(h + 1) * 128, cols]
            do = dot_ref[rows, cols]
            s = jnp.dot(kx_ref[:, h * 128:(h + 1) * 128], q, preferred_element_type=jnp.float32)
            p = jnp.exp2(s + bias_of(h, lse_ref[first + h:first + h + 1, cols]))
            dp = jnp.dot(vx_ref[:, h * 128:h * 128 + 64], do, preferred_element_type=jnp.float32)
            ds = p * (dp - d_ref[h:h + 1, cols])
            sums(h, ds)
            pb = p.astype(jnp.bfloat16)
            db = ds.astype(jnp.bfloat16)
            dv_acc[h] += lax.dot_general(pb, do, NT, preferred_element_type=jnp.float32)
            dk_acc[h] += lax.dot_general(db, q[:64], NT, preferred_element_type=jnp.float32)
            dqacc_ref[rows, cols] += jnp.dot(kt_ref[rows, :], db, preferred_element_type=jnp.float32)

    def far(i, later):
        side = 1 - later

        def bias_of(h, lse):
            return table_ref[16 * side + 15, first + h] * LOG2E - lse

        def sums(h, ds):
            far_ref[h * 2 + side] += jnp.sum(ds.reshape(T // 8, 8, T), axis=0)
        tile(i, bias_of, sums)

    def near(i):
        def bias_of(h, lse):
            return tile_ref[h * 3 + j - i + 1] - lse

        def sums(h, ds):
            bacc_ref[h * 3 + j - i + 1] += ds
        tile(i, bias_of, sums)

    block_loops(j, lo, hi, far, near)
    HC = heads * 64
    block = pl.ds(pl.multiple_of(j * T, T), T)
    grad_ref[block, HC:2 * HC] = (jnp.concatenate([dk_acc[h] for h in range(heads)], axis=1) * (1.0 / LOG2E)).astype(jnp.bfloat16)
    grad_ref[block, 2 * HC:] = jnp.concatenate([dv_acc[h] for h in range(heads)], axis=1).astype(jnp.bfloat16)

    @pl.when(j == last)
    def _():
        for n in range(dqacc_ref.shape[1] // T):
            grad_ref[n * T:(n + 1) * T, 0:HC] = dqacc_ref[:, n * T:(n + 1) * T].T.astype(jnp.bfloat16)
        zero = jnp.zeros((8, T), jnp.float32)
        sub = lax.broadcasted_iota(jnp.int32, (8, 2 * T), 0)
        for n in range(heads * 3):
            total = jnp.concatenate((bacc_ref[n, 0:8, :], zero), axis=1)
            for g in range(1, T // 8):
                rows = jnp.concatenate((bacc_ref[n, 8 * g:8 * g + 8, :], zero), axis=1)
                total = total + pltpu.roll(rows, 2 * T - 8 * g, 1)
            for bit in (1, 2, 4):
                total = jnp.where((sub & bit) != 0, pltpu.roll(total, 2 * T - bit, 1), total)
            diag_ref[n:n + 1, :] = jnp.sum(total, axis=0, keepdims=True)
        for n in range(heads * 2):
            diag_ref[heads * 3 + n:heads * 3 + n + 1, 0:T] = jnp.sum(far_ref[n], axis=0, keepdims=True)
            diag_ref[heads * 3 + n:heads * 3 + n + 1, T:] = jnp.zeros((1, T), jnp.float32)


def attn_bwd(pair, lo, hi, bias_table, qx, kx, vx, kt, dot, ot, lse, tiles):
    heads = PAIR
    T = TILE
    S = lo.shape[0] * T
    smem = pl.BlockSpec(memory_space=pltpu.SMEM)
    once = lambda shape, index: pl.BlockSpec(shape, lambda i: index, pipeline_mode=pl.Buffered(1))
    rows = lambda n: pl.BlockSpec((T, n), lambda i: (i, pair))
    HC = heads * 64
    return pl.pallas_call(
        functools.partial(attn_bwd_kernel, heads, pair * heads),
        grid=(S // T,),
        out_shape=(jax.ShapeDtypeStruct((S, 3 * HC), jnp.bfloat16), jax.ShapeDtypeStruct((heads * 5, 2 * T), jnp.float32)),
        in_specs=[smem, smem, smem, once((heads * 128, S), (pair, 0)), rows(heads * 128), rows(heads * 128),
                  pl.BlockSpec((HC, T), lambda i: (pair, i)), once((HC, S), (pair, 0)), once((HC, S), (pair, 0)), once((8, S), (0, 0)),
                  once((heads * 3, T, T), (pair, 0, 0))],
        out_specs=(once((S, 3 * HC), (0, 0)), once((heads * 5, 2 * T), (0, 0))),
        scratch_shapes=[pltpu.VMEM((8, S), jnp.float32), pltpu.VMEM((HC, S), jnp.float32),
                        pltpu.VMEM((heads * 3, T, T), jnp.float32), pltpu.VMEM((heads * 2, 8, T), jnp.float32),
                        pltpu.VMEM((heads, T, 64), jnp.float32), pltpu.VMEM((heads, T, 64), jnp.float32)],
        compiler_params=pltpu.CompilerParams(dimension_semantics=("arbitrary",), vmem_limit_bytes=60 << 20),
        cost_estimate=attn_cost(S, heads, 24),
        name="attn_bwd",
    )(lo, hi, bias_table, qx, kx, vx, kt, dot, ot, lse, tiles)


def table_grad(diag, heads):
    T = TILE
    t = jnp.arange(2 * T, dtype=jnp.int32)
    t = jnp.where(t < T, t, t - 2 * T)
    d = jnp.arange(3, dtype=jnp.int32)
    bucket = bucket_of((d[:, None] - 1) * T - t[None, :])
    onehot = (bucket[:, :, None] == jnp.arange(32, dtype=jnp.int32)).astype(jnp.float32)
    near = jnp.einsum("hdt,dtb->bh", diag[:heads * 3].reshape(heads, 3, 2 * T), onehot, precision=lax.Precision.HIGHEST)
    far = jnp.sum(diag[heads * 3:].reshape(heads, 2, 2 * T), axis=2)
    ids = jnp.arange(32, dtype=jnp.int32)[:, None]
    return near + jnp.where(ids == 15, far[None, :, 0], 0.0) + jnp.where(ids == 31, far[None, :, 1], 0.0)


def block_bounds(segment_row):
    S = segment_row.shape[0]
    blocks = segment_row.reshape(S // TILE, TILE)
    first, final = blocks[:, 0], blocks[:, TILE - 1]
    lo = jnp.sum((segment_row[None, :] < first[:, None]).astype(jnp.int32), axis=1) // TILE
    hi = (jnp.sum((segment_row[None, :] <= final[:, None]).astype(jnp.int32), axis=1) - 1) // TILE
    return lo, hi


def pad_heads(w, heads, width):
    D = w.shape[0]
    return jnp.pad(w.reshape(D, heads, 64), ((0, 0), (0, 0), (0, width - 64))).reshape(D, heads * width)


def operands(segment_row):
    S = segment_row.shape[0]
    row = jnp.arange(128, dtype=jnp.int32)
    same = segment_row[None, :] == (row[:, None] - 64)
    inside = (row >= 64) & (row < 80)
    qext = jnp.where(inside[:, None] & same, 1.0, 0.0)
    kext = jnp.where(inside[None, :] & ~same.T, MASKED, 0.0)
    vext = jnp.where(jnp.arange(VROWS) == 64, 1.0, 0.0)[:, None]
    return qext, kext, vext


def padded_weights(w_query, w_key, w_value, heads):
    return pad_heads(w_query, heads, 128), pad_heads(w_key, heads, 128), pad_heads(w_value, heads, VROWS)


def project(normed, weights, ext, heads):
    (qext, kext, vext), (wq, wk, wv) = ext, weights
    f32 = jnp.float32
    qx = lax.dot_general(wq, normed, TN, preferred_element_type=f32) * LOG2E
    qx = (qx + jnp.tile(qext, (heads, 1))).astype(jnp.bfloat16)
    kx = jnp.dot(normed, wk, preferred_element_type=f32)
    kx = (kx + jnp.tile(kext, (1, heads))).astype(jnp.bfloat16)
    vt = lax.dot_general(wv, normed, TN, preferred_element_type=f32)
    vt = (vt + jnp.tile(vext, (heads, 1))).astype(jnp.bfloat16)
    return qx, kx, vt


def project_back(normed, w_vx, w_key):
    vx = jnp.dot(normed, w_vx, preferred_element_type=jnp.float32).astype(jnp.bfloat16)
    kt = lax.dot_general(w_key, normed, TN, preferred_element_type=jnp.float32).astype(jnp.bfloat16)
    return vx, kt


CHUNK = 256
ROOT = math.sqrt(2 / math.pi)


def ffn_kernel(parts, per_part, in_sent, back_sent, n_ref, c_ref, *refs):
    in_refs, back_refs = refs[:parts], refs[parts:2 * parts]
    out_ref, out_mate_ref, norm_ref, norm_mate_ref = refs[2 * parts:2 * parts + 4]
    gin_refs, gback_refs = refs[2 * parts + 4:2 * parts + 6], refs[2 * parts + 6:2 * parts + 8]
    w_in, w_back, out_acc, norm_acc = refs[2 * parts + 8:]
    step = pl.program_id(0)
    f32, bf16 = jnp.float32, jnp.bfloat16
    NT = (((1,), (1,)), ((), ()))
    TN = (((0,), (0,)), ((), ()))

    @pl.when(step == 0)
    def _():
        out_acc[...] = jnp.zeros(out_acc.shape, f32)
        norm_acc[...] = jnp.zeros(norm_acc.shape, f32)

    for q in range(parts):
        @pl.when(step // per_part == q)
        def _():
            w_in[...] = in_refs[q][...]
            w_back[...] = back_refs[q][...]

    rows = n_ref.shape[0]
    inner = lax.dot_general(n_ref[...], w_in[...], NT, preferred_element_type=f32)
    cube = inner * inner * 0.044715
    th = jnp.tanh(ROOT * inner * (1.0 + cube))
    half = 0.5 * (1.0 + th)
    active = (inner * half).astype(bf16)
    slope = half + (0.5 * ROOT) * inner * (1.0 - th * th) * (1.0 + 3.0 * cube)
    grad = (lax.dot_general(c_ref[...], w_back[...], NT, preferred_element_type=f32) * slope).astype(bf16)
    norm_acc[...] += jnp.dot(grad, w_in[...], preferred_element_type=f32)
    out_acc[...] += jnp.dot(active, w_back[...], preferred_element_type=f32)
    gin = lax.dot_general(grad, n_ref[...], TN, preferred_element_type=f32).astype(bf16)
    gback = lax.dot_general(active, c_ref[...], TN, preferred_element_type=f32).astype(bf16)
    part = step // per_part
    for grad_refs, value, sent in ((gin_refs, gin, in_sent), (gback_refs, gback, back_sent)):
        leaves = functools.reduce(jnp.logical_or, [part == q for q in sent], False)

        @pl.when(leaves)
        def _():
            grad_refs[1][...] = value

        @pl.when(jnp.logical_not(leaves))
        def _():
            grad_refs[0][...] = value

    @pl.when(step == pl.num_programs(0) - 1)
    def _():
        own = out_ref.shape[0]
        out_ref[...] = out_acc[:own, :]
        out_mate_ref[...] = out_acc[own:, :].astype(bf16)
        norm_ref[...] = norm_acc[:own, :]
        norm_mate_ref[...] = norm_acc[own:, :].astype(bf16)


def ffn(normed, cot, in_parts, back_parts, in_sent, back_sent):
    parts = len(in_parts)
    units, width = in_parts[0].shape
    rows = normed.shape[0]
    chunk = min(CHUNK, units)
    per_part = units // chunk
    once = lambda shape: pl.BlockSpec(shape, lambda i: (0, 0), pipeline_mode=pl.Buffered(1))
    piece = lambda q: pl.BlockSpec((chunk, width), lambda i: (jnp.clip(i - q * per_part, 0, per_part - 1), 0))
    weights = [piece(q) for q in range(parts)]
    sums = [jax.ShapeDtypeStruct((rows // 2, width), kind) for kind in (jnp.float32, jnp.bfloat16)]
    grads, grad_specs = [], []
    for sent in (in_sent, back_sent):
        for members in ([q for q in range(parts) if q not in sent], list(sent)):
            steps = [q * per_part + n for q in members for n in range(per_part)]
            index = lambda i, ups=tuple(steps[1:]): (sum([(i >= up).astype(jnp.int32) for up in ups], jnp.int32(0)), 0)
            grads.append(jax.ShapeDtypeStruct((len(members) * units, width), jnp.bfloat16))
            grad_specs.append(pl.BlockSpec((chunk, width), index))
    return pl.pallas_call(
        functools.partial(ffn_kernel, parts, per_part, in_sent, back_sent),
        grid=(parts * per_part,),
        out_shape=sums * 2 + grads,
        in_specs=[once((rows, width)), once((rows, width))] + weights * 2,
        out_specs=[once((rows // 2, width))] * 4 + grad_specs,
        scratch_shapes=[pltpu.VMEM((chunk, width), jnp.bfloat16)] * 2 + [pltpu.VMEM((rows, width), jnp.float32)] * 2,
        compiler_params=pltpu.CompilerParams(dimension_semantics=("arbitrary",), vmem_limit_bytes=60 << 20),
        cost_estimate=pl.CostEstimate(flops=int(35e9), transcendentals=0, bytes_accessed=16 << 20),
        name="ffn",
    )(normed, cot, *in_parts, *back_parts)


def over_rows(left_side, right_side):
    return lax.dot_general(
        left_side, right_side, (((0,), (0,)), ((), ())), preferred_element_type=jnp.float32
    )


def against(left_side, right_side):
    return lax.dot_general(
        left_side, right_side, (((1,), (1,)), ((), ())), preferred_element_type=jnp.float32
    )


def matmul(left_side, right_side):
    return jnp.dot(left_side, right_side, preferred_element_type=jnp.float32)


def norm_back(grad_normed, unit_rows, inv_scale, gain_row):
    scaled = grad_normed * gain_row
    return inv_scale * (scaled - unit_rows * jnp.mean(scaled * unit_rows, axis=-1, keepdims=True))


def low(values_in):
    return values_in.astype(jnp.bfloat16)


def wide(values_in):
    return values_in.astype(jnp.float32)


def bits_of(size):
    return [1 << n for n in range(size.bit_length() - 1)]


def tie(*values):
    return lax.optimization_barrier(values)


def finish(steps):
    for step in steps:
        last = step
    return last


def send_or_none(steps, value):
    try:
        return steps.send(value)
    except StopIteration:
        return None


class Slice:
    def __init__(self, mesh):
        self.dp, self.group, self.tensor = (mesh.shape[name] for name in ("dp", "group", "tensor"))

    def swap(self, array, axis, mask):
        size = getattr(self, axis)
        return lax.ppermute(array, axis, [(i, i ^ mask) for i in range(size)])

    def pair_swap(self, array):
        return self.swap(array, "group", 1)

    def row_steps(self):
        return [("group", 2 * bit) for bit in bits_of(self.group // 2)]

    def col_steps(self):
        return [("dp", bit) for bit in bits_of(self.dp)]

    def spread(self, block):
        have = {(0, 0): block}
        size = self.dp * self.group
        for col in range(self.dp):
            for row in range(self.group // 2):
                mask = col * self.group + 2 * row
                if mask:
                    have[col, row] = lax.ppermute(block, ("dp", "group"), [(i, i ^ mask) for i in range(size)])
        return have

    def collect_order(self, rows_first):
        steps = self.row_steps() + self.col_steps() if rows_first else self.col_steps() + self.row_steps()
        return list(reversed(steps))

    def sent_first(self, keys, rows_first):
        return self.sent_first_of(keys, self.collect_order(rows_first)[0])

    def collect(self, keys, kept, sent, rows_first):
        order = self.collect_order(rows_first)
        leaves = self.sent_first(keys, rows_first)
        keys = [key for n, key in enumerate(keys) if n not in leaves]
        units = kept.shape[0] // len(keys)
        for n, (axis, mask) in enumerate(order):
            other = yield self.swap(sent, axis, mask)
            total = low(wide(kept) + wide(other))
            if n + 1 < len(order):
                leaves = self.sent_first_of(keys, order[n + 1])
                block = lambda k: total[k * units:(k + 1) * units]
                pick = lambda ks: block(ks[0]) if len(ks) == 1 else jnp.concatenate([block(k) for k in ks], axis=0)
                kept, sent = pick([k for k in range(len(keys)) if k not in leaves]), pick(list(leaves))
                keys = [key for k, key in enumerate(keys) if k not in leaves]
        yield total

    def sent_first_of(self, keys, step):
        axis, mask = step
        return tuple(n for n, (col, row) in enumerate(keys) if (row & mask // 2 if axis == "group" else col & mask))

    def slot(self):
        rows = self.group // 2
        group = lax.axis_index("group")
        return (group % 2) * (self.dp * rows) + lax.axis_index("dp") * rows + group // 2

    def slot_gather(self, block):
        for axis, mask in self.row_steps() + self.col_steps() + [("group", 1)]:
            upper = (lax.axis_index(axis) // mask) % 2 == 1
            other = self.swap(block, axis, mask)
            yield other
            block = jnp.concatenate((jnp.where(upper, other, block), jnp.where(upper, block, other)), axis=2)
        yield block.reshape(block.shape[0], -1, block.shape[3])

    def plane_sum(self, grad, others):
        mine = lax.axis_index("dp")
        for axis, mask in reversed(self.col_steps()):
            half = grad.shape[0] // 2
            bit = (mine // mask) % 2
            keep = lax.dynamic_slice_in_dim(grad, bit * half, half, 0)
            send = lax.dynamic_slice_in_dim(grad, (1 - bit) * half, half, 0)
            other = self.swap(send, axis, mask)
            grad = low(wide(keep) + wide(other))
        for axis, mask in self.row_steps() + [("group", 1)]:
            other = self.swap(grad, axis, mask)
            if axis == "group" and mask == 2:
                other, others = tie(other, others)
            grad = low(wide(grad) + wide(other))
        return grad[0], others

    def small_sum(self, vector, axes):
        for axis in axes:
            for mask in bits_of(getattr(self, axis)):
                vector = vector + self.swap(vector, axis, mask)
        return vector

    def col_exchange(self, blocks):
        mine = lax.axis_index("dp")
        for axis, mask in reversed(self.col_steps()):
            half = blocks.shape[3] // 2
            upper = (mine // mask) % 2 == 1
            low_half, high_half = blocks[..., :half], blocks[..., half:]
            keep = jnp.where(upper, high_half, low_half)
            other = self.swap(jnp.where(upper, low_half, high_half), axis, mask)
            pair = jnp.where(upper, jnp.stack((other, keep), axis=1), jnp.stack((keep, other), axis=1))
            blocks = pair.reshape((pair.shape[0], -1) + pair.shape[3:])
        if self.dp > 2:
            count, bits = blocks.shape[0], self.dp.bit_length() - 1
            split = blocks.reshape((count,) + (2,) * bits + blocks.shape[2:])
            split = split.transpose((0,) + tuple(range(bits, 0, -1)) + (bits + 1, bits + 2))
            blocks = split.reshape(blocks.shape)
        return blocks

    def group_gather(self, block):
        block = block[None]
        for mask in reversed(bits_of(self.group)):
            upper = (lax.axis_index("group") // mask) % 2 == 1
            other = self.swap(block, "group", mask)
            block = jnp.where(upper, jnp.stack((other, block), axis=1), jnp.stack((block, other), axis=1))
            block = block.reshape((-1,) + block.shape[2:])
        return block

    def col_exchange_rows(self, rows):
        return self.col_exchange(rows[None, None])[0]


def on_device(
    sl,
    inputs,
    segments,
    gain_attn,
    w_query,
    w_key,
    w_value,
    w_out,
    bias_table,
    gain_ffn,
    w_in,
    w_back,
    cotangent,
):
    heads_here = bias_table.shape[1]
    width = inputs.shape[1]
    pairs = heads_here // PAIR
    cols = PAIR * 64
    dp_index, group_index = lax.axis_index("dp"), lax.axis_index("group")
    segment_row = segments.reshape(-1)
    lo, hi = block_bounds(segment_row)
    tiles = bias_tiles(bias_table)

    stream = wide(inputs)
    inv_attn = lax.rsqrt(jnp.mean(stream * stream, axis=-1, keepdims=True) + EPSILON)
    unit_attn = stream * inv_attn
    rows = stream.shape[0]
    units_g = w_back.shape[0] // sl.group
    units = units_g // sl.dp
    start = group_index * units_g + dp_index * units
    plane = sl.dp * sl.group
    slot = sl.slot()
    qkv = [jnp.concatenate([w[:, k * cols:(k + 1) * cols] for w in (w_query, w_key, w_value)], axis=1) for k in range(pairs)]
    n_out, n_qkv = w_out.shape[0] // plane, 3 * cols // plane
    own_in = [lax.dynamic_slice_in_dim(w_in, start, units, 1).T]
    own_in.append(lax.dynamic_slice_in_dim(w_out, slot * n_out, n_out, 0))
    own_in = jnp.concatenate(own_in, axis=0)
    own_back = lax.dynamic_slice_in_dim(w_back, start, units, 0)
    own_qkv = jnp.concatenate([lax.dynamic_slice_in_dim(qkv[k], slot * n_qkv, n_qkv, 1).T for k in range(pairs)], axis=0)
    cot_pair = jnp.concatenate((cotangent, sl.pair_swap(cotangent)), axis=0)
    prep = (tiles, padded_weights(w_query, w_key, w_value, heads_here), operands(segment_row), cot_pair, pad_heads(w_value, heads_here, 128))
    by_pair = lambda block, rows: block.reshape(sl.tensor, pairs, rows, width).transpose(1, 0, 2, 3)
    in_z = lax.all_gather(own_in, "tensor", axis=0, tiled=False)
    own_normed, in_z = tie(low(unit_attn * gain_attn), in_z)
    normed = lax.all_gather(own_normed, "tensor", axis=0, tiled=True)
    in_parts = sl.spread(in_z[:, :units].reshape(-1, width))
    out_full = finish(sl.slot_gather(in_z[:, units:][None]))[0]
    n_rows = own_qkv.shape[0]
    own_qkv = jnp.pad(own_qkv, ((0, -n_rows % 128), (0, 0)))
    own_back, normed, prep, in_parts, qkv, out_full, own_qkv = tie(own_back, normed, prep, in_parts, qkv, out_full, own_qkv)
    tiles, padded, ext, cot_pair, w_vx = prep
    back_z = lax.all_gather(own_back, "tensor", axis=0, tiled=True)

    qx, kx, vt = project(normed, padded, ext, heads_here)
    ctx_t, lse = attn_fwd(lo, hi, bias_table, qx, kx, vt, tiles)
    back_z, ctx_t = tie(back_z, ctx_t)
    back_parts = sl.spread(back_z)
    ctx_rows = lax.all_to_all(ctx_t, "tensor", split_axis=1, concat_axis=0, tiled=True)
    ctx_rows, normed, own_qkv = tie(ctx_rows, normed, own_qkv)
    qkv_z = lax.all_gather(own_qkv, "tensor", axis=0, tiled=False)[:, :n_rows]
    vx, kt = project_back(normed, w_vx, w_key)
    hidden = stream + over_rows(ctx_rows, out_full)
    inv_ffn = lax.rsqrt(jnp.mean(hidden * hidden, axis=-1, keepdims=True) + EPSILON)
    unit_ffn = hidden * inv_ffn

    normed_ffn, qkv_z, back_parts, vx, kt = tie(low(unit_ffn * gain_ffn), qkv_z, back_parts, vx, kt)
    qkv_all = lax.all_gather(qkv_z, ("dp", "group"), axis=0, tiled=False)
    normed_pair = jnp.concatenate((normed_ffn, sl.pair_swap(normed_ffn)), axis=0)
    keys = sorted(in_parts)
    results = ffn(
        normed_pair, cot_pair, [in_parts[key] for key in keys], [back_parts[key] for key in keys],
        sl.sent_first(keys, True), sl.sent_first(keys, False),
    )
    out_own, out_mate, normed_own, normed_mate = results[:4]
    in_steps, back_steps = sl.collect(keys, *results[4:6], True), sl.collect(keys, *results[6:8], False)
    normed_own, qkv_all = tie(normed_own, qkv_all)
    grad_normed_ffn = normed_own + wide(sl.pair_swap(normed_mate))
    output = hidden + out_own + wide(sl.pair_swap(out_mate))

    gain_ffn_part = jnp.sum(grad_normed_ffn * unit_ffn, axis=0)
    grad_hidden = wide(cotangent) + norm_back(grad_normed_ffn, unit_ffn, inv_ffn, gain_ffn)
    grad_hidden_low = low(grad_hidden)
    grad_ctx = low(against(out_full, grad_hidden_low))
    grad_hidden_late, grad_ctx = tie(grad_hidden_low, grad_ctx)
    grad_ctx_t = lax.all_to_all(grad_ctx, "tensor", split_axis=0, concat_axis=1, tiled=True)

    grad_w_out = low(matmul(ctx_rows, grad_hidden_late)).reshape(sl.tensor, sl.group, -1, width)

    def out_scatter(grad):
        for mask in bits_of(sl.group):
            grad = grad.reshape((sl.tensor, -1, 2) + grad.shape[2:])
            bit = (group_index // mask) % 2
            keep = lax.dynamic_index_in_dim(grad, bit, 2, keepdims=False)
            other = sl.swap(lax.dynamic_index_in_dim(grad, 1 - bit, 2, keepdims=False), "group", mask)
            other = yield other
            grad = low(wide(keep) + wide(other))
        grad = grad[:, 0]
        for axis, mask in reversed(sl.col_steps()):
            n = grad.shape[1] // 2
            bit = (dp_index // mask) % 2
            keep = lax.dynamic_slice_in_dim(grad, bit * n, n, 1)
            other = sl.swap(lax.dynamic_slice_in_dim(grad, (1 - bit) * n, n, 1), axis, mask)
            other = yield other
            grad = low(wide(keep) + wide(other))
        yield grad

    out_steps = out_scatter(grad_w_out)
    first, grad_ctx_t = tie((next(in_steps), next(back_steps), next(out_steps)), grad_ctx_t)
    second = [steps.send(other) for steps, other in zip((in_steps, back_steps, out_steps), first)]
    tables, grad_parts, grad_rows = [], [], []
    for k in range(pairs):
        lo_k = lo
        if k == pairs - 1:
            own_sums = []
            if k > 0:
                second, grad_parts[-1] = tie(second, grad_parts[-1])
            for steps, last in zip((in_steps, back_steps, out_steps), second):
                for other in iter(lambda: send_or_none(steps, last), None):
                    last = other
                own_sums.append(last)
            own_sums = jnp.concatenate([part.reshape(sl.tensor, -1, width) for part in own_sums], axis=1)
            lo_k, own_sums = tie(lo, own_sums)
            own_rows = own_sums.shape[1]
            summed = lax.psum_scatter(own_sums.reshape(-1, width), "tensor", scatter_dimension=0, tiled=True)
        grads, diag = attn_bwd(k, lo_k, hi, bias_table, qx, kx, vx, kt, grad_ctx_t, ctx_t, lse, tiles)
        grad_parts.append(grads)
        if k > 0:
            grads, diag, grad_rows[k - 1] = tie(grads, diag, grad_rows[k - 1])
        grad_rows.append(lax.all_to_all(grads, "tensor", split_axis=0, concat_axis=1, tiled=True))
        tables.append(table_grad(diag, PAIR))

    summed = sl.col_exchange_rows(summed)
    grad_parts = tie(*grad_parts)
    gain_dot, grad_w_qkv = 0.0, []
    for k in range(pairs):
        grad_w = over_rows(normed, grad_parts[k])
        gain_dot = gain_dot + jnp.sum(grad_w * wide(qkv[k]), axis=1)
        grad_w_qkv.append(low(grad_w))

    columns = pairs * 3 * cols
    small = jnp.concatenate([gain_dot / gain_attn, gain_ffn_part] + [table.T.reshape(-1) for table in tables])
    small_rows = -(-small.shape[0] // columns)
    small = low(jnp.pad(small, (0, small_rows * columns - small.shape[0]))).reshape(1, small_rows, columns)
    grad_w_qkv = jnp.concatenate(grad_w_qkv, axis=1).reshape(sl.dp, -1, columns)
    grad_w_qkv = jnp.concatenate((grad_w_qkv, jnp.tile(small, (sl.dp, 1, 1))), axis=1)
    grad_w_qkv, (grad_rows, summed) = sl.plane_sum(grad_w_qkv, (grad_rows, summed))
    small = grad_w_qkv[-small_rows:].reshape(-1)
    grad_w_qkv = wide(grad_w_qkv[:-small_rows])
    gain_grads = sl.small_sum(wide(small[:2 * width]), ("tensor",))
    table_rows = bias_table.shape[0] // sl.dp
    grad_table = wide(small[2 * width:2 * width + bias_table.size]).reshape(heads_here, -1)
    grad_table = lax.dynamic_slice_in_dim(grad_table, dp_index * table_rows, table_rows, 1).T

    everything = sl.group_gather(summed)
    cuts = [0, units, 2 * units, own_rows]
    pick = lambda n: wide(everything[:, :, cuts[n]:cuts[n + 1]].reshape(-1, width // sl.dp))
    grad_w_in, grad_w_back, grad_w_out = pick(0).T, pick(1), pick(2)
    qkv_all = qkv_all.reshape(sl.dp, sl.group // 2, 2, sl.tensor, pairs, n_qkv, width).transpose(4, 3, 2, 0, 1, 5, 6)
    qkv_full = qkv_all.reshape(pairs, -1, width)
    grad_normed = 0.0
    for k in range(pairs):
        grad_normed = grad_normed + matmul(grad_rows[k], qkv_full[k])
    grad_inputs = grad_hidden + norm_back(grad_normed, unit_attn, inv_attn, gain_attn)
    grad_w_query, grad_w_key, grad_w_value = (
        jnp.concatenate([grad_w_qkv[:, (3 * k + n) * cols:(3 * k + n + 1) * cols] for k in range(pairs)], axis=1) for n in range(3)
    )
    return (
        output,
        grad_inputs,
        gain_grads[:width],
        grad_w_query,
        grad_w_key,
        grad_w_value,
        grad_w_out,
        grad_table,
        gain_grads[width:],
        grad_w_in,
        grad_w_back,
    )


def solution(mesh):
    return jax.shard_map(
        functools.partial(on_device, Slice(mesh)),
        mesh=mesh,
        in_specs=(
            P(("dp", "group", "tensor"), None),
            P(("dp", "group"), None),
            P(),
            P(None, "tensor"),
            P(None, "tensor"),
            P(None, "tensor"),
            P("tensor", None),
            P(None, "tensor"),
            P(),
            P(None, "tensor"),
            P("tensor", None),
            P(("dp", "group", "tensor"), None),
        ),
        out_specs=(
            P(("dp", "group", "tensor"), None),
            P(("dp", "group", "tensor"), None),
            P(),
            P("dp", "tensor"),
            P("dp", "tensor"),
            P("dp", "tensor"),
            P("tensor", "dp"),
            P("dp", "tensor"),
            P(),
            P("dp", "tensor"),
            P("tensor", "dp"),
        ),
        check_vma=False,
    )
```

```python
import functools
import math

import jax
import jax.numpy as jnp
from jax import lax
from jax.experimental import pallas as pl
from jax.experimental.pallas import tpu as pltpu
from jax.sharding import PartitionSpec as P

EPSILON = 1e-06

LOG2E = math.log2(math.e)
MASKED = -1e30
TILE = 256
VROWS = 80
PAIR = 2
TN = (((0,), (1,)), ((), ()))
reach_marks = (12, 16, 23, 32, 46, 64, 91)


def bucket_of(offset):
    distance = jnp.abs(offset)
    far_bucket = jnp.full(offset.shape, 8, jnp.int32)
    for threshold in reach_marks:
        far_bucket = far_bucket + (distance >= threshold).astype(jnp.int32)
    return 16 * (offset > 0).astype(jnp.int32) + jnp.where(distance < 8, distance, far_bucket)


def bias_tiles_kernel(heads, table_ref, tile_ref):
    T = TILE
    for d in range(3):
        t = lax.broadcasted_iota(jnp.int32, (8, 2 * T), 1)
        t = jnp.where(t < T, t, t - 2 * T)
        bucket = bucket_of((d - 1) * T - t)
        for h in range(heads):
            row = jnp.zeros((8, 2 * T), jnp.float32)
            for b in range(32):
                row = jnp.where(bucket == b, table_ref[b, h] * LOG2E, row)
            wide = jnp.broadcast_to(row[0:1], (T, 2 * T))
            rolled = pltpu.roll(wide, 0, 1, stride=1, stride_axis=0)
            tile_ref[h * 3 + d] = rolled[:, :T]


def bias_tiles(bias_table):
    heads = bias_table.shape[1]
    return pl.pallas_call(
        functools.partial(bias_tiles_kernel, heads),
        out_shape=jax.ShapeDtypeStruct((heads * 3, TILE, TILE), jnp.float32),
        in_specs=[pl.BlockSpec(memory_space=pltpu.SMEM)],
        out_specs=pl.BlockSpec(memory_space=pltpu.VMEM),
        name="bias_tiles",
    )(bias_table)


def block_loops(i, lo, hi, far, near):
    lax.fori_loop(lo, i - 1, lambda j, _: far(j, 0) or 0, 0)
    lax.fori_loop(jnp.maximum(lo, i - 1), jnp.minimum(hi, i + 1) + 1, lambda j, _: near(j) or 0, 0)
    lax.fori_loop(i + 2, hi + 1, lambda j, _: far(j, 1) or 0, 0)


def attn_fwd_kernel(heads, first, lo_ref, hi_ref, table_ref, qx_ref, kx_ref, vt_ref, tile_ref, o_ref, lse_ref, m_ref, acc_ref, s_ref):
    T = TILE
    i = pl.program_id(0)
    lo, hi = lo_ref[i], hi_ref[i]
    m_ref[...] = jnp.full(m_ref.shape, MASKED, jnp.float32)
    acc_ref[...] = jnp.zeros(acc_ref.shape, jnp.float32)

    def scores(j, bias_of):
        start = pl.multiple_of(j * T, T)
        for h in range(heads):
            k = kx_ref[pl.ds(start, T), h * 128:(h + 1) * 128]
            s = jnp.dot(k, qx_ref[h * 128:(h + 1) * 128, :], preferred_element_type=jnp.float32)
            s = s + bias_of(h)
            s_ref[j - lo, h] = s
            m_ref[h] = jnp.maximum(m_ref[h], jnp.max(s.reshape(T // 8, 8, T), axis=0))

    def far(j, side):
        scores(j, lambda h: table_ref[16 * side + 15, first + h] * LOG2E)

    def near(j):
        scores(j, lambda h: tile_ref[h * 3 + j - i + 1])

    block_loops(i, lo, hi, far, near)
    tops = [jnp.max(m_ref[h], axis=0, keepdims=True) for h in range(heads)]

    def values(j, _):
        start = pl.multiple_of(j * T, T)
        for h in range(heads):
            p = jnp.exp2(s_ref[j - lo, h] - tops[h]).astype(jnp.bfloat16)
            rows = slice(h * VROWS, (h + 1) * VROWS)
            acc_ref[rows, :] += jnp.dot(vt_ref[rows, pl.ds(start, T)], p, preferred_element_type=jnp.float32)
        return 0

    lax.fori_loop(lo, hi + 1, values, 0)
    for h in range(heads):
        total = acc_ref[h * VROWS + 64:h * VROWS + 65, :]
        o_ref[h * 64:(h + 1) * 64, :] = (acc_ref[h * VROWS:h * VROWS + 64, :] / total).astype(jnp.bfloat16)
        lse_ref[h:h + 1, :] = tops[h] + jnp.log2(total)


def attn_cost(seq_len, heads, micros):
    return pl.CostEstimate(flops=int(micros * 1e9), transcendentals=0, bytes_accessed=seq_len * heads * 2048)


def attn_fwd(lo, hi, bias_table, qx, kx, vt, tiles):
    heads = bias_table.shape[1]
    T = TILE
    S = lo.shape[0] * T
    smem = pl.BlockSpec(memory_space=pltpu.SMEM)
    once = lambda shape, index: pl.BlockSpec(shape, lambda i: index, pipeline_mode=pl.Buffered(1))
    return pl.pallas_call(
        functools.partial(attn_fwd_kernel, heads, 0),
        grid=(S // T,),
        out_shape=(jax.ShapeDtypeStruct((heads * 64, S), jnp.bfloat16), jax.ShapeDtypeStruct((8, S), jnp.float32)),
        in_specs=[smem, smem, smem, pl.BlockSpec((heads * 128, T), lambda i: (0, i)), once((S, heads * 128), (0, 0)),
                  once((heads * VROWS, S), (0, 0)), once((heads * 3, T, T), (0, 0, 0))],
        out_specs=(pl.BlockSpec((heads * 64, T), lambda i: (0, i)), pl.BlockSpec((8, T), lambda i: (0, i))),
        scratch_shapes=[pltpu.VMEM((heads, 8, T), jnp.float32), pltpu.VMEM((heads * VROWS, T), jnp.float32),
                        pltpu.VMEM((S // T, heads, T, T), jnp.float32)],
        compiler_params=pltpu.CompilerParams(dimension_semantics=("arbitrary",), vmem_limit_bytes=24 << 20),
        cost_estimate=attn_cost(S, heads, 25),
        name="attn_fwd",
    )(lo, hi, bias_table, qx, kx, vt, tiles)


def attn_bwd_kernel(heads, first, lo_ref, hi_ref, table_ref, qx_ref, kx_ref, vx_ref, kt_ref, dot_ref, ot_ref, lse_ref, tile_ref,
                    grad_ref, diag_ref, d_ref, dqacc_ref, bacc_ref, far_ref, dk_acc, dv_acc):
    T = TILE
    j = pl.program_id(0)
    last = pl.num_programs(0) - 1
    lo, hi = lo_ref[j], hi_ref[j]
    NT = (((1,), (1,)), ((), ()))

    @pl.when(j == 0)
    def _():
        dqacc_ref[...] = jnp.zeros(dqacc_ref.shape, jnp.float32)
        bacc_ref[...] = jnp.zeros(bacc_ref.shape, jnp.float32)
        far_ref[...] = jnp.zeros(far_ref.shape, jnp.float32)
        for h in range(heads):
            rows = slice(h * 64, (h + 1) * 64)
            d_ref[h:h + 1, :] = jnp.sum(dot_ref[rows, :].astype(jnp.float32) * ot_ref[rows, :].astype(jnp.float32), axis=0, keepdims=True)

    dk_acc[...] = jnp.zeros(dk_acc.shape, jnp.float32)
    dv_acc[...] = jnp.zeros(dv_acc.shape, jnp.float32)

    def tile(i, bias_of, sums):
        cols = pl.ds(pl.multiple_of(i * T, T), T)
        for h in range(heads):
            rows = slice(h * 64, (h + 1) * 64)
            q = qx_ref[h * 128:(h + 1) * 128, cols]
            do = dot_ref[rows, cols]
            s = jnp.dot(kx_ref[:, h * 128:(h + 1) * 128], q, preferred_element_type=jnp.float32)
            p = jnp.exp2(s + bias_of(h, lse_ref[first + h:first + h + 1, cols]))
            dp = jnp.dot(vx_ref[:, h * 128:h * 128 + 64], do, preferred_element_type=jnp.float32)
            ds = p * (dp - d_ref[h:h + 1, cols])
            sums(h, ds)
            pb = p.astype(jnp.bfloat16)
            db = ds.astype(jnp.bfloat16)
            dv_acc[h] += lax.dot_general(pb, do, NT, preferred_element_type=jnp.float32)
            dk_acc[h] += lax.dot_general(db, q[:64], NT, preferred_element_type=jnp.float32)
            dqacc_ref[rows, cols] += jnp.dot(kt_ref[rows, :], db, preferred_element_type=jnp.float32)

    def far(i, later):
        side = 1 - later

        def bias_of(h, lse):
            return table_ref[16 * side + 15, first + h] * LOG2E - lse

        def sums(h, ds):
            far_ref[h * 2 + side] += jnp.sum(ds.reshape(T // 8, 8, T), axis=0)
        tile(i, bias_of, sums)

    def near(i):
        def bias_of(h, lse):
            return tile_ref[h * 3 + j - i + 1] - lse

        def sums(h, ds):
            bacc_ref[h * 3 + j - i + 1] += ds
        tile(i, bias_of, sums)

    block_loops(j, lo, hi, far, near)
    HC = heads * 64
    block = pl.ds(pl.multiple_of(j * T, T), T)
    grad_ref[block, HC:2 * HC] = (jnp.concatenate([dk_acc[h] for h in range(heads)], axis=1) * (1.0 / LOG2E)).astype(jnp.bfloat16)
    grad_ref[block, 2 * HC:] = jnp.concatenate([dv_acc[h] for h in range(heads)], axis=1).astype(jnp.bfloat16)

    @pl.when(j == last)
    def _():
        for n in range(dqacc_ref.shape[1] // T):
            grad_ref[n * T:(n + 1) * T, 0:HC] = dqacc_ref[:, n * T:(n + 1) * T].T.astype(jnp.bfloat16)
        zero = jnp.zeros((8, T), jnp.float32)
        sub = lax.broadcasted_iota(jnp.int32, (8, 2 * T), 0)
        for n in range(heads * 3):
            total = jnp.concatenate((bacc_ref[n, 0:8, :], zero), axis=1)
            for g in range(1, T // 8):
                rows = jnp.concatenate((bacc_ref[n, 8 * g:8 * g + 8, :], zero), axis=1)
                total = total + pltpu.roll(rows, 2 * T - 8 * g, 1)
            for bit in (1, 2, 4):
                total = jnp.where((sub & bit) != 0, pltpu.roll(total, 2 * T - bit, 1), total)
            diag_ref[n:n + 1, :] = jnp.sum(total, axis=0, keepdims=True)
        for n in range(heads * 2):
            diag_ref[heads * 3 + n:heads * 3 + n + 1, 0:T] = jnp.sum(far_ref[n], axis=0, keepdims=True)
            diag_ref[heads * 3 + n:heads * 3 + n + 1, T:] = jnp.zeros((1, T), jnp.float32)


def attn_bwd(pair, lo, hi, bias_table, qx, kx, vx, kt, dot, ot, lse, tiles):
    heads = PAIR
    T = TILE
    S = lo.shape[0] * T
    smem = pl.BlockSpec(memory_space=pltpu.SMEM)
    once = lambda shape, index: pl.BlockSpec(shape, lambda i: index, pipeline_mode=pl.Buffered(1))
    rows = lambda n: pl.BlockSpec((T, n), lambda i: (i, pair))
    HC = heads * 64
    return pl.pallas_call(
        functools.partial(attn_bwd_kernel, heads, pair * heads),
        grid=(S // T,),
        out_shape=(jax.ShapeDtypeStruct((S, 3 * HC), jnp.bfloat16), jax.ShapeDtypeStruct((heads * 5, 2 * T), jnp.float32)),
        in_specs=[smem, smem, smem, once((heads * 128, S), (pair, 0)), rows(heads * 128), rows(heads * 128),
                  pl.BlockSpec((HC, T), lambda i: (pair, i)), once((HC, S), (pair, 0)), once((HC, S), (pair, 0)), once((8, S), (0, 0)),
                  once((heads * 3, T, T), (pair, 0, 0))],
        out_specs=(once((S, 3 * HC), (0, 0)), once((heads * 5, 2 * T), (0, 0))),
        scratch_shapes=[pltpu.VMEM((8, S), jnp.float32), pltpu.VMEM((HC, S), jnp.float32),
                        pltpu.VMEM((heads * 3, T, T), jnp.float32), pltpu.VMEM((heads * 2, 8, T), jnp.float32),
                        pltpu.VMEM((heads, T, 64), jnp.float32), pltpu.VMEM((heads, T, 64), jnp.float32)],
        compiler_params=pltpu.CompilerParams(dimension_semantics=("arbitrary",), vmem_limit_bytes=60 << 20),
        cost_estimate=attn_cost(S, heads, 24),
        name="attn_bwd",
    )(lo, hi, bias_table, qx, kx, vx, kt, dot, ot, lse, tiles)


def table_grad(diag, heads):
    T = TILE
    t = jnp.arange(2 * T, dtype=jnp.int32)
    t = jnp.where(t < T, t, t - 2 * T)
    d = jnp.arange(3, dtype=jnp.int32)
    bucket = bucket_of((d[:, None] - 1) * T - t[None, :])
    onehot = (bucket[:, :, None] == jnp.arange(32, dtype=jnp.int32)).astype(jnp.float32)
    near = jnp.einsum("hdt,dtb->bh", diag[:heads * 3].reshape(heads, 3, 2 * T), onehot, precision=lax.Precision.HIGHEST)
    far = jnp.sum(diag[heads * 3:].reshape(heads, 2, 2 * T), axis=2)
    ids = jnp.arange(32, dtype=jnp.int32)[:, None]
    return near + jnp.where(ids == 15, far[None, :, 0], 0.0) + jnp.where(ids == 31, far[None, :, 1], 0.0)


def block_bounds(segment_row):
    S = segment_row.shape[0]
    blocks = segment_row.reshape(S // TILE, TILE)
    first, final = blocks[:, 0], blocks[:, TILE - 1]
    lo = jnp.sum((segment_row[None, :] < first[:, None]).astype(jnp.int32), axis=1) // TILE
    hi = (jnp.sum((segment_row[None, :] <= final[:, None]).astype(jnp.int32), axis=1) - 1) // TILE
    return lo, hi


def pad_heads(w, heads, width):
    D = w.shape[0]
    return jnp.pad(w.reshape(D, heads, 64), ((0, 0), (0, 0), (0, width - 64))).reshape(D, heads * width)


def operands(segment_row):
    S = segment_row.shape[0]
    row = jnp.arange(128, dtype=jnp.int32)
    same = segment_row[None, :] == (row[:, None] - 64)
    inside = (row >= 64) & (row < 80)
    qext = jnp.where(inside[:, None] & same, 1.0, 0.0)
    kext = jnp.where(inside[None, :] & ~same.T, MASKED, 0.0)
    vext = jnp.where(jnp.arange(VROWS) == 64, 1.0, 0.0)[:, None]
    return qext, kext, vext


def padded_weights(w_query, w_key, w_value, heads):
    return pad_heads(w_query, heads, 128), pad_heads(w_key, heads, 128), pad_heads(w_value, heads, VROWS)


def project(normed, weights, ext, heads):
    (qext, kext, vext), (wq, wk, wv) = ext, weights
    f32 = jnp.float32
    qx = lax.dot_general(wq, normed, TN, preferred_element_type=f32) * LOG2E
    qx = (qx + jnp.tile(qext, (heads, 1))).astype(jnp.bfloat16)
    kx = jnp.dot(normed, wk, preferred_element_type=f32)
    kx = (kx + jnp.tile(kext, (1, heads))).astype(jnp.bfloat16)
    vt = lax.dot_general(wv, normed, TN, preferred_element_type=f32)
    vt = (vt + jnp.tile(vext, (heads, 1))).astype(jnp.bfloat16)
    return qx, kx, vt


def project_back(normed, w_vx, w_key):
    vx = jnp.dot(normed, w_vx, preferred_element_type=jnp.float32).astype(jnp.bfloat16)
    kt = lax.dot_general(w_key, normed, TN, preferred_element_type=jnp.float32).astype(jnp.bfloat16)
    return vx, kt


CHUNK = 256
ROOT = math.sqrt(2 / math.pi)


def ffn_kernel(parts, per_part, in_sent, back_sent, n_ref, c_ref, *refs):
    in_refs, back_refs = refs[:parts], refs[parts:2 * parts]
    out_ref, out_mate_ref, norm_ref, norm_mate_ref = refs[2 * parts:2 * parts + 4]
    gin_refs, gback_refs = refs[2 * parts + 4:2 * parts + 6], refs[2 * parts + 6:2 * parts + 8]
    w_in, w_back, out_acc, norm_acc = refs[2 * parts + 8:]
    step = pl.program_id(0)
    f32, bf16 = jnp.float32, jnp.bfloat16
    NT = (((1,), (1,)), ((), ()))
    TN = (((0,), (0,)), ((), ()))

    @pl.when(step == 0)
    def _():
        out_acc[...] = jnp.zeros(out_acc.shape, f32)
        norm_acc[...] = jnp.zeros(norm_acc.shape, f32)

    for q in range(parts):
        @pl.when(step // per_part == q)
        def _():
            w_in[...] = in_refs[q][...]
            w_back[...] = back_refs[q][...]

    rows = n_ref.shape[0]
    inner = lax.dot_general(n_ref[...], w_in[...], NT, preferred_element_type=f32)
    cube = inner * inner * 0.044715
    th = jnp.tanh(ROOT * inner * (1.0 + cube))
    half = 0.5 * (1.0 + th)
    active = (inner * half).astype(bf16)
    slope = half + (0.5 * ROOT) * inner * (1.0 - th * th) * (1.0 + 3.0 * cube)
    grad = (lax.dot_general(c_ref[...], w_back[...], NT, preferred_element_type=f32) * slope).astype(bf16)
    norm_acc[...] += jnp.dot(grad, w_in[...], preferred_element_type=f32)
    out_acc[...] += jnp.dot(active, w_back[...], preferred_element_type=f32)
    gin = lax.dot_general(grad, n_ref[...], TN, preferred_element_type=f32).astype(bf16)
    gback = lax.dot_general(active, c_ref[...], TN, preferred_element_type=f32).astype(bf16)
    part = step // per_part
    for grad_refs, value, sent in ((gin_refs, gin, in_sent), (gback_refs, gback, back_sent)):
        leaves = functools.reduce(jnp.logical_or, [part == q for q in sent], False)

        @pl.when(leaves)
        def _():
            grad_refs[1][...] = value

        @pl.when(jnp.logical_not(leaves))
        def _():
            grad_refs[0][...] = value

    @pl.when(step == pl.num_programs(0) - 1)
    def _():
        own = out_ref.shape[0]
        out_ref[...] = out_acc[:own, :]
        out_mate_ref[...] = out_acc[own:, :].astype(bf16)
        norm_ref[...] = norm_acc[:own, :]
        norm_mate_ref[...] = norm_acc[own:, :].astype(bf16)


def ffn(normed, cot, in_parts, back_parts, in_sent, back_sent):
    parts = len(in_parts)
    units, width = in_parts[0].shape
    rows = normed.shape[0]
    chunk = min(CHUNK, units)
    per_part = units // chunk
    once = lambda shape: pl.BlockSpec(shape, lambda i: (0, 0), pipeline_mode=pl.Buffered(1))
    piece = lambda q: pl.BlockSpec((chunk, width), lambda i: (jnp.clip(i - q * per_part, 0, per_part - 1), 0))
    weights = [piece(q) for q in range(parts)]
    sums = [jax.ShapeDtypeStruct((rows // 2, width), kind) for kind in (jnp.float32, jnp.bfloat16)]
    grads, grad_specs = [], []
    for sent in (in_sent, back_sent):
        for members in ([q for q in range(parts) if q not in sent], list(sent)):
            steps = [q * per_part + n for q in members for n in range(per_part)]
            index = lambda i, ups=tuple(steps[1:]): (sum([(i >= up).astype(jnp.int32) for up in ups], jnp.int32(0)), 0)
            grads.append(jax.ShapeDtypeStruct((len(members) * units, width), jnp.bfloat16))
            grad_specs.append(pl.BlockSpec((chunk, width), index))
    return pl.pallas_call(
        functools.partial(ffn_kernel, parts, per_part, in_sent, back_sent),
        grid=(parts * per_part,),
        out_shape=sums * 2 + grads,
        in_specs=[once((rows, width)), once((rows, width))] + weights * 2,
        out_specs=[once((rows // 2, width))] * 4 + grad_specs,
        scratch_shapes=[pltpu.VMEM((chunk, width), jnp.bfloat16)] * 2 + [pltpu.VMEM((rows, width), jnp.float32)] * 2,
        compiler_params=pltpu.CompilerParams(dimension_semantics=("arbitrary",), vmem_limit_bytes=60 << 20),
        cost_estimate=pl.CostEstimate(flops=int(35e9), transcendentals=0, bytes_accessed=16 << 20),
        name="ffn",
    )(normed, cot, *in_parts, *back_parts)


def over_rows(left_side, right_side):
    return lax.dot_general(
        left_side, right_side, (((0,), (0,)), ((), ())), preferred_element_type=jnp.float32
    )


def against(left_side, right_side):
    return lax.dot_general(
        left_side, right_side, (((1,), (1,)), ((), ())), preferred_element_type=jnp.float32
    )


def matmul(left_side, right_side):
    return jnp.dot(left_side, right_side, preferred_element_type=jnp.float32)


def norm_back(grad_normed, unit_rows, inv_scale, gain_row):
    scaled = grad_normed * gain_row
    return inv_scale * (scaled - unit_rows * jnp.mean(scaled * unit_rows, axis=-1, keepdims=True))


def low(values_in):
    return values_in.astype(jnp.bfloat16)


def wide(values_in):
    return values_in.astype(jnp.float32)


def bits_of(size):
    return [1 << n for n in range(size.bit_length() - 1)]


def tie(*values):
    return lax.optimization_barrier(values)


def finish(steps):
    for step in steps:
        last = step
    return last


def send_or_none(steps, value):
    try:
        return steps.send(value)
    except StopIteration:
        return None


class Slice:
    def __init__(self, mesh):
        self.dp, self.group, self.tensor = (mesh.shape[name] for name in ("dp", "group", "tensor"))

    def swap(self, array, axis, mask):
        size = getattr(self, axis)
        return lax.ppermute(array, axis, [(i, i ^ mask) for i in range(size)])

    def pair_swap(self, array):
        return self.swap(array, "group", 1)

    def row_steps(self):
        return [("group", 2 * bit) for bit in bits_of(self.group // 2)]

    def col_steps(self):
        return [("dp", bit) for bit in bits_of(self.dp)]

    def spread(self, block):
        have = {(0, 0): block}
        size = self.dp * self.group
        for col in range(self.dp):
            for row in range(self.group // 2):
                mask = col * self.group + 2 * row
                if mask:
                    have[col, row] = lax.ppermute(block, ("dp", "group"), [(i, i ^ mask) for i in range(size)])
        return have

    def collect_order(self, rows_first):
        steps = self.row_steps() + self.col_steps() if rows_first else self.col_steps() + self.row_steps()
        return list(reversed(steps))

    def sent_first(self, keys, rows_first):
        return self.sent_first_of(keys, self.collect_order(rows_first)[0])

    def collect(self, keys, kept, sent, rows_first):
        order = self.collect_order(rows_first)
        leaves = self.sent_first(keys, rows_first)
        keys = [key for n, key in enumerate(keys) if n not in leaves]
        units = kept.shape[0] // len(keys)
        for n, (axis, mask) in enumerate(order):
            other = yield self.swap(sent, axis, mask)
            total = low(wide(kept) + wide(other))
            if n + 1 < len(order):
                leaves = self.sent_first_of(keys, order[n + 1])
                block = lambda k: total[k * units:(k + 1) * units]
                pick = lambda ks: block(ks[0]) if len(ks) == 1 else jnp.concatenate([block(k) for k in ks], axis=0)
                kept, sent = pick([k for k in range(len(keys)) if k not in leaves]), pick(list(leaves))
                keys = [key for k, key in enumerate(keys) if k not in leaves]
        yield total

    def sent_first_of(self, keys, step):
        axis, mask = step
        return tuple(n for n, (col, row) in enumerate(keys) if (row & mask // 2 if axis == "group" else col & mask))

    def slot(self):
        rows = self.group // 2
        group = lax.axis_index("group")
        return (group % 2) * (self.dp * rows) + lax.axis_index("dp") * rows + group // 2

    def slot_gather(self, block):
        for axis, mask in self.row_steps() + self.col_steps() + [("group", 1)]:
            upper = (lax.axis_index(axis) // mask) % 2 == 1
            other = self.swap(block, axis, mask)
            yield other
            block = jnp.concatenate((jnp.where(upper, other, block), jnp.where(upper, block, other)), axis=2)
        yield block.reshape(block.shape[0], -1, block.shape[3])

    def plane_sum(self, grad, others):
        mine = lax.axis_index("dp")
        for axis, mask in reversed(self.col_steps()):
            half = grad.shape[0] // 2
            bit = (mine // mask) % 2
            keep = lax.dynamic_slice_in_dim(grad, bit * half, half, 0)
            send = lax.dynamic_slice_in_dim(grad, (1 - bit) * half, half, 0)
            other = self.swap(send, axis, mask)
            grad = low(wide(keep) + wide(other))
        for axis, mask in self.row_steps() + [("group", 1)]:
            other = self.swap(grad, axis, mask)
            if axis == "group" and mask == 2:
                other, others = tie(other, others)
            grad = low(wide(grad) + wide(other))
        return grad[0], others

    def small_sum(self, vector, axes):
        for axis in axes:
            for mask in bits_of(getattr(self, axis)):
                vector = vector + self.swap(vector, axis, mask)
        return vector

    def col_exchange(self, blocks):
        mine = lax.axis_index("dp")
        for axis, mask in reversed(self.col_steps()):
            half = blocks.shape[3] // 2
            upper = (mine // mask) % 2 == 1
            low_half, high_half = blocks[..., :half], blocks[..., half:]
            keep = jnp.where(upper, high_half, low_half)
            other = self.swap(jnp.where(upper, low_half, high_half), axis, mask)
            pair = jnp.where(upper, jnp.stack((other, keep), axis=1), jnp.stack((keep, other), axis=1))
            blocks = pair.reshape((pair.shape[0], -1) + pair.shape[3:])
        if self.dp > 2:
            count, bits = blocks.shape[0], self.dp.bit_length() - 1
            split = blocks.reshape((count,) + (2,) * bits + blocks.shape[2:])
            split = split.transpose((0,) + tuple(range(bits, 0, -1)) + (bits + 1, bits + 2))
            blocks = split.reshape(blocks.shape)
        return blocks

    def group_gather(self, block):
        block = block[None]
        for mask in reversed(bits_of(self.group)):
            upper = (lax.axis_index("group") // mask) % 2 == 1
            other = self.swap(block, "group", mask)
            block = jnp.where(upper, jnp.stack((other, block), axis=1), jnp.stack((block, other), axis=1))
            block = block.reshape((-1,) + block.shape[2:])
        return block

    def col_exchange_rows(self, rows):
        return self.col_exchange(rows[None, None])[0]


def on_device(
    sl,
    inputs,
    segments,
    gain_attn,
    w_query,
    w_key,
    w_value,
    w_out,
    bias_table,
    gain_ffn,
    w_in,
    w_back,
    cotangent,
):
    heads_here = bias_table.shape[1]
    width = inputs.shape[1]
    pairs = heads_here // PAIR
    cols = PAIR * 64
    dp_index, group_index = lax.axis_index("dp"), lax.axis_index("group")
    segment_row = segments.reshape(-1)
    lo, hi = block_bounds(segment_row)
    tiles = bias_tiles(bias_table)

    stream = wide(inputs)
    inv_attn = lax.rsqrt(jnp.mean(stream * stream, axis=-1, keepdims=True) + EPSILON)
    unit_attn = stream * inv_attn
    rows = stream.shape[0]
    units_g = w_back.shape[0] // sl.group
    units = units_g // sl.dp
    start = group_index * units_g + dp_index * units
    plane = sl.dp * sl.group
    slot = sl.slot()
    qkv = [jnp.concatenate([w[:, k * cols:(k + 1) * cols] for w in (w_query, w_key, w_value)], axis=1) for k in range(pairs)]
    n_out, n_qkv = w_out.shape[0] // plane, 3 * cols // plane
    own_in = [lax.dynamic_slice_in_dim(w_in, start, units, 1).T]
    own_in.append(lax.dynamic_slice_in_dim(w_out, slot * n_out, n_out, 0))
    own_in = jnp.concatenate(own_in, axis=0)
    own_back = lax.dynamic_slice_in_dim(w_back, start, units, 0)
    own_qkv = jnp.concatenate([lax.dynamic_slice_in_dim(qkv[k], slot * n_qkv, n_qkv, 1).T for k in range(pairs)], axis=0)
    cot_pair = jnp.concatenate((cotangent, sl.pair_swap(cotangent)), axis=0)
    prep = (tiles, padded_weights(w_query, w_key, w_value, heads_here), operands(segment_row), cot_pair, pad_heads(w_value, heads_here, 128))
    by_pair = lambda block, rows: block.reshape(sl.tensor, pairs, rows, width).transpose(1, 0, 2, 3)
    in_z = lax.all_gather(own_in, "tensor", axis=0, tiled=False)
    own_normed, in_z = tie(low(unit_attn * gain_attn), in_z)
    normed = lax.all_gather(own_normed, "tensor", axis=0, tiled=True)
    in_parts = sl.spread(in_z[:, :units].reshape(-1, width))
    out_full = finish(sl.slot_gather(in_z[:, units:][None]))[0]
    n_rows = own_qkv.shape[0]
    own_qkv = jnp.pad(own_qkv, ((0, -n_rows % 128), (0, 0)))
    own_back, normed, prep, in_parts, qkv, out_full, own_qkv = tie(own_back, normed, prep, in_parts, qkv, out_full, own_qkv)
    tiles, padded, ext, cot_pair, w_vx = prep
    back_z = lax.all_gather(own_back, "tensor", axis=0, tiled=True)

    qx, kx, vt = project(normed, padded, ext, heads_here)
    ctx_t, lse = attn_fwd(lo, hi, bias_table, qx, kx, vt, tiles)
    back_z, ctx_t, own_qkv = tie(back_z, ctx_t, own_qkv)
    qkv_z = lax.all_gather(own_qkv, "tensor", axis=0, tiled=False)[:, :n_rows]
    back_parts = sl.spread(back_z)
    ctx_rows = lax.all_to_all(ctx_t, "tensor", split_axis=1, concat_axis=0, tiled=True)
    hidden = stream + over_rows(ctx_rows, out_full)
    inv_ffn = lax.rsqrt(jnp.mean(hidden * hidden, axis=-1, keepdims=True) + EPSILON)
    unit_ffn = hidden * inv_ffn

    normed_ffn, qkv_z, back_parts = tie(low(unit_ffn * gain_ffn), qkv_z, back_parts)
    qkv_all = lax.all_gather(qkv_z, ("dp", "group"), axis=0, tiled=False)
    normed_pair = jnp.concatenate((normed_ffn, sl.pair_swap(normed_ffn)), axis=0)
    keys = sorted(in_parts)
    results = ffn(
        normed_pair, cot_pair, [in_parts[key] for key in keys], [back_parts[key] for key in keys],
        sl.sent_first(keys, True), sl.sent_first(keys, False),
    )
    out_own, out_mate, normed_own, normed_mate = results[:4]
    in_steps, back_steps = sl.collect(keys, *results[4:6], True), sl.collect(keys, *results[6:8], False)
    normed_own, qkv_all = tie(normed_own, qkv_all)
    grad_normed_ffn = normed_own + wide(sl.pair_swap(normed_mate))
    output = hidden + out_own + wide(sl.pair_swap(out_mate))

    gain_ffn_part = jnp.sum(grad_normed_ffn * unit_ffn, axis=0)
    grad_hidden = wide(cotangent) + norm_back(grad_normed_ffn, unit_ffn, inv_ffn, gain_ffn)
    grad_hidden_low = low(grad_hidden)
    grad_ctx = low(against(out_full, grad_hidden_low))
    grad_hidden_late, grad_ctx, normed = tie(grad_hidden_low, grad_ctx, normed)
    vx, kt = project_back(normed, w_vx, w_key)
    grad_ctx_t = lax.all_to_all(grad_ctx, "tensor", split_axis=0, concat_axis=1, tiled=True)

    grad_w_out = low(matmul(ctx_rows, grad_hidden_late)).reshape(sl.tensor, sl.group, -1, width)

    def out_scatter(grad):
        for mask in bits_of(sl.group):
            grad = grad.reshape((sl.tensor, -1, 2) + grad.shape[2:])
            bit = (group_index // mask) % 2
            keep = lax.dynamic_index_in_dim(grad, bit, 2, keepdims=False)
            other = sl.swap(lax.dynamic_index_in_dim(grad, 1 - bit, 2, keepdims=False), "group", mask)
            other = yield other
            grad = low(wide(keep) + wide(other))
        grad = grad[:, 0]
        for axis, mask in reversed(sl.col_steps()):
            n = grad.shape[1] // 2
            bit = (dp_index // mask) % 2
            keep = lax.dynamic_slice_in_dim(grad, bit * n, n, 1)
            other = sl.swap(lax.dynamic_slice_in_dim(grad, (1 - bit) * n, n, 1), axis, mask)
            other = yield other
            grad = low(wide(keep) + wide(other))
        yield grad

    out_steps = out_scatter(grad_w_out)
    first, grad_ctx_t, vx, kt = tie((next(in_steps), next(back_steps), next(out_steps)), grad_ctx_t, vx, kt)
    second = [steps.send(other) for steps, other in zip((in_steps, back_steps, out_steps), first)]
    tables, grad_parts, grad_rows = [], [], []
    for k in range(pairs):
        lo_k = lo
        if k == pairs - 1:
            own_sums = []
            if k > 0:
                second, grad_parts[-1] = tie(second, grad_parts[-1])
            for steps, last in zip((in_steps, back_steps, out_steps), second):
                for other in iter(lambda: send_or_none(steps, last), None):
                    last = other
                own_sums.append(last)
            own_sums = jnp.concatenate([part.reshape(sl.tensor, -1, width) for part in own_sums], axis=1)
            lo_k, own_sums = tie(lo, own_sums)
            own_rows = own_sums.shape[1]
            summed = lax.psum_scatter(own_sums.reshape(-1, width), "tensor", scatter_dimension=0, tiled=True)
        grads, diag = attn_bwd(k, lo_k, hi, bias_table, qx, kx, vx, kt, grad_ctx_t, ctx_t, lse, tiles)
        grad_parts.append(grads)
        if k > 0:
            grads, diag, grad_rows[k - 1] = tie(grads, diag, grad_rows[k - 1])
        grad_rows.append(lax.all_to_all(grads, "tensor", split_axis=0, concat_axis=1, tiled=True))
        tables.append(table_grad(diag, PAIR))

    summed = sl.col_exchange_rows(summed)
    grad_parts = tie(*grad_parts)
    gain_dot, grad_w_qkv = 0.0, []
    for k in range(pairs):
        grad_w = over_rows(normed, grad_parts[k])
        gain_dot = gain_dot + jnp.sum(grad_w * wide(qkv[k]), axis=1)
        grad_w_qkv.append(low(grad_w))

    columns = pairs * 3 * cols
    small = jnp.concatenate([gain_dot / gain_attn, gain_ffn_part] + [table.T.reshape(-1) for table in tables])
    small_rows = -(-small.shape[0] // columns)
    small = low(jnp.pad(small, (0, small_rows * columns - small.shape[0]))).reshape(1, small_rows, columns)
    grad_w_qkv = jnp.concatenate(grad_w_qkv, axis=1).reshape(sl.dp, -1, columns)
    grad_w_qkv = jnp.concatenate((grad_w_qkv, jnp.tile(small, (sl.dp, 1, 1))), axis=1)
    grad_w_qkv, (grad_rows, summed) = sl.plane_sum(grad_w_qkv, (grad_rows, summed))
    small = grad_w_qkv[-small_rows:].reshape(-1)
    grad_w_qkv = wide(grad_w_qkv[:-small_rows])
    gain_grads = sl.small_sum(wide(small[:2 * width]), ("tensor",))
    table_rows = bias_table.shape[0] // sl.dp
    grad_table = wide(small[2 * width:2 * width + bias_table.size]).reshape(heads_here, -1)
    grad_table = lax.dynamic_slice_in_dim(grad_table, dp_index * table_rows, table_rows, 1).T

    everything = sl.group_gather(summed)
    cuts = [0, units, 2 * units, own_rows]
    pick = lambda n: wide(everything[:, :, cuts[n]:cuts[n + 1]].reshape(-1, width // sl.dp))
    grad_w_in, grad_w_back, grad_w_out = pick(0).T, pick(1), pick(2)
    qkv_all = qkv_all.reshape(sl.dp, sl.group // 2, 2, sl.tensor, pairs, n_qkv, width).transpose(4, 3, 2, 0, 1, 5, 6)
    qkv_full = qkv_all.reshape(pairs, -1, width)
    grad_normed = 0.0
    for k in range(pairs):
        grad_normed = grad_normed + matmul(grad_rows[k], qkv_full[k])
    grad_inputs = grad_hidden + norm_back(grad_normed, unit_attn, inv_attn, gain_attn)
    grad_w_query, grad_w_key, grad_w_value = (
        jnp.concatenate([grad_w_qkv[:, (3 * k + n) * cols:(3 * k + n + 1) * cols] for k in range(pairs)], axis=1) for n in range(3)
    )
    return (
        output,
        grad_inputs,
        gain_grads[:width],
        grad_w_query,
        grad_w_key,
        grad_w_value,
        grad_w_out,
        grad_table,
        gain_grads[width:],
        grad_w_in,
        grad_w_back,
    )


def solution(mesh):
    return jax.shard_map(
        functools.partial(on_device, Slice(mesh)),
        mesh=mesh,
        in_specs=(
            P(("dp", "group", "tensor"), None),
            P(("dp", "group"), None),
            P(),
            P(None, "tensor"),
            P(None, "tensor"),
            P(None, "tensor"),
            P("tensor", None),
            P(None, "tensor"),
            P(),
            P(None, "tensor"),
            P("tensor", None),
            P(("dp", "group", "tensor"), None),
        ),
        out_specs=(
            P(("dp", "group", "tensor"), None),
            P(("dp", "group", "tensor"), None),
            P(),
            P("dp", "tensor"),
            P("dp", "tensor"),
            P("dp", "tensor"),
            P("tensor", "dp"),
            P("dp", "tensor"),
            P(),
            P("dp", "tensor"),
            P("tensor", "dp"),
        ),
        check_vma=False,
    )
```

```python
import functools
import math

import jax
import jax.numpy as jnp
from jax import lax
from jax.experimental import pallas as pl
from jax.experimental.pallas import tpu as pltpu
from jax.sharding import PartitionSpec as P

EPSILON = 1e-06

LOG2E = math.log2(math.e)
MASKED = -1e30
TILE = 256
VROWS = 80
PAIR = 2
TN = (((0,), (1,)), ((), ()))
reach_marks = (12, 16, 23, 32, 46, 64, 91)


def bucket_of(offset):
    distance = jnp.abs(offset)
    far_bucket = jnp.full(offset.shape, 8, jnp.int32)
    for threshold in reach_marks:
        far_bucket = far_bucket + (distance >= threshold).astype(jnp.int32)
    return 16 * (offset > 0).astype(jnp.int32) + jnp.where(distance < 8, distance, far_bucket)


def bias_tiles_kernel(heads, table_ref, tile_ref):
    T = TILE
    for d in range(3):
        t = lax.broadcasted_iota(jnp.int32, (8, 2 * T), 1)
        t = jnp.where(t < T, t, t - 2 * T)
        bucket = bucket_of((d - 1) * T - t)
        for h in range(heads):
            row = jnp.zeros((8, 2 * T), jnp.float32)
            for b in range(32):
                row = jnp.where(bucket == b, table_ref[b, h] * LOG2E, row)
            wide = jnp.broadcast_to(row[0:1], (T, 2 * T))
            rolled = pltpu.roll(wide, 0, 1, stride=1, stride_axis=0)
            tile_ref[h * 3 + d] = rolled[:, :T]


def bias_tiles(bias_table):
    heads = bias_table.shape[1]
    return pl.pallas_call(
        functools.partial(bias_tiles_kernel, heads),
        out_shape=jax.ShapeDtypeStruct((heads * 3, TILE, TILE), jnp.float32),
        in_specs=[pl.BlockSpec(memory_space=pltpu.SMEM)],
        out_specs=pl.BlockSpec(memory_space=pltpu.VMEM),
        name="bias_tiles",
    )(bias_table)


def block_loops(i, lo, hi, far, near):
    lax.fori_loop(lo, i - 1, lambda j, _: far(j, 0) or 0, 0)
    lax.fori_loop(jnp.maximum(lo, i - 1), jnp.minimum(hi, i + 1) + 1, lambda j, _: near(j) or 0, 0)
    lax.fori_loop(i + 2, hi + 1, lambda j, _: far(j, 1) or 0, 0)


def attn_fwd_kernel(heads, first, lo_ref, hi_ref, table_ref, qx_ref, kx_ref, vt_ref, tile_ref, o_ref, lse_ref, m_ref, acc_ref, s_ref):
    T = TILE
    i = pl.program_id(0)
    lo, hi = lo_ref[i], hi_ref[i]
    m_ref[...] = jnp.full(m_ref.shape, MASKED, jnp.float32)
    acc_ref[...] = jnp.zeros(acc_ref.shape, jnp.float32)

    def scores(j, bias_of):
        start = pl.multiple_of(j * T, T)
        for h in range(heads):
            k = kx_ref[pl.ds(start, T), h * 128:(h + 1) * 128]
            s = jnp.dot(k, qx_ref[h * 128:(h + 1) * 128, :], preferred_element_type=jnp.float32)
            s = s + bias_of(h)
            s_ref[j - lo, h] = s
            m_ref[h] = jnp.maximum(m_ref[h], jnp.max(s.reshape(T // 8, 8, T), axis=0))

    def far(j, side):
        scores(j, lambda h: table_ref[16 * side + 15, first + h] * LOG2E)

    def near(j):
        scores(j, lambda h: tile_ref[h * 3 + j - i + 1])

    block_loops(i, lo, hi, far, near)
    tops = [jnp.max(m_ref[h], axis=0, keepdims=True) for h in range(heads)]

    def values(j, _):
        start = pl.multiple_of(j * T, T)
        for h in range(heads):
            p = jnp.exp2(s_ref[j - lo, h] - tops[h]).astype(jnp.bfloat16)
            rows = slice(h * VROWS, (h + 1) * VROWS)
            acc_ref[rows, :] += jnp.dot(vt_ref[rows, pl.ds(start, T)], p, preferred_element_type=jnp.float32)
        return 0

    lax.fori_loop(lo, hi + 1, values, 0)
    for h in range(heads):
        total = acc_ref[h * VROWS + 64:h * VROWS + 65, :]
        o_ref[h * 64:(h + 1) * 64, :] = (acc_ref[h * VROWS:h * VROWS + 64, :] / total).astype(jnp.bfloat16)
        lse_ref[h:h + 1, :] = tops[h] + jnp.log2(total)


def attn_cost(seq_len, heads, micros):
    return pl.CostEstimate(flops=int(micros * 1e9), transcendentals=0, bytes_accessed=seq_len * heads * 2048)


def attn_fwd(lo, hi, bias_table, qx, kx, vt, tiles):
    heads = bias_table.shape[1]
    T = TILE
    S = lo.shape[0] * T
    smem = pl.BlockSpec(memory_space=pltpu.SMEM)
    once = lambda shape, index: pl.BlockSpec(shape, lambda i: index, pipeline_mode=pl.Buffered(1))
    return pl.pallas_call(
        functools.partial(attn_fwd_kernel, heads, 0),
        grid=(S // T,),
        out_shape=(jax.ShapeDtypeStruct((heads * 64, S), jnp.bfloat16), jax.ShapeDtypeStruct((8, S), jnp.float32)),
        in_specs=[smem, smem, smem, pl.BlockSpec((heads * 128, T), lambda i: (0, i)), once((S, heads * 128), (0, 0)),
                  once((heads * VROWS, S), (0, 0)), once((heads * 3, T, T), (0, 0, 0))],
        out_specs=(pl.BlockSpec((heads * 64, T), lambda i: (0, i)), pl.BlockSpec((8, T), lambda i: (0, i))),
        scratch_shapes=[pltpu.VMEM((heads, 8, T), jnp.float32), pltpu.VMEM((heads * VROWS, T), jnp.float32),
                        pltpu.VMEM((S // T, heads, T, T), jnp.float32)],
        compiler_params=pltpu.CompilerParams(dimension_semantics=("arbitrary",), vmem_limit_bytes=24 << 20),
        cost_estimate=attn_cost(S, heads, 25),
        name="attn_fwd",
    )(lo, hi, bias_table, qx, kx, vt, tiles)


def attn_bwd_kernel(heads, first, lo_ref, hi_ref, table_ref, qx_ref, kx_ref, vx_ref, kt_ref, dot_ref, ot_ref, lse_ref, tile_ref,
                    grad_ref, diag_ref, d_ref, dqacc_ref, bacc_ref, far_ref, dk_acc, dv_acc):
    T = TILE
    j = pl.program_id(0)
    last = pl.num_programs(0) - 1
    lo, hi = lo_ref[j], hi_ref[j]
    NT = (((1,), (1,)), ((), ()))

    @pl.when(j == 0)
    def _():
        dqacc_ref[...] = jnp.zeros(dqacc_ref.shape, jnp.float32)
        bacc_ref[...] = jnp.zeros(bacc_ref.shape, jnp.float32)
        far_ref[...] = jnp.zeros(far_ref.shape, jnp.float32)
        for h in range(heads):
            rows = slice(h * 64, (h + 1) * 64)
            d_ref[h:h + 1, :] = jnp.sum(dot_ref[rows, :].astype(jnp.float32) * ot_ref[rows, :].astype(jnp.float32), axis=0, keepdims=True)

    dk_acc[...] = jnp.zeros(dk_acc.shape, jnp.float32)
    dv_acc[...] = jnp.zeros(dv_acc.shape, jnp.float32)

    def tile(i, bias_of, sums):
        cols = pl.ds(pl.multiple_of(i * T, T), T)
        for h in range(heads):
            rows = slice(h * 64, (h + 1) * 64)
            q = qx_ref[h * 128:(h + 1) * 128, cols]
            do = dot_ref[rows, cols]
            s = jnp.dot(kx_ref[:, h * 128:(h + 1) * 128], q, preferred_element_type=jnp.float32)
            p = jnp.exp2(s + bias_of(h, lse_ref[first + h:first + h + 1, cols]))
            dp = jnp.dot(vx_ref[:, h * 128:h * 128 + 64], do, preferred_element_type=jnp.float32)
            ds = p * (dp - d_ref[h:h + 1, cols])
            sums(h, ds)
            pb = p.astype(jnp.bfloat16)
            db = ds.astype(jnp.bfloat16)
            dv_acc[h] += lax.dot_general(pb, do, NT, preferred_element_type=jnp.float32)
            dk_acc[h] += lax.dot_general(db, q[:64], NT, preferred_element_type=jnp.float32)
            dqacc_ref[rows, cols] += jnp.dot(kt_ref[rows, :], db, preferred_element_type=jnp.float32)

    def far(i, later):
        side = 1 - later

        def bias_of(h, lse):
            return table_ref[16 * side + 15, first + h] * LOG2E - lse

        def sums(h, ds):
            far_ref[h * 2 + side] += jnp.sum(ds.reshape(T // 8, 8, T), axis=0)
        tile(i, bias_of, sums)

    def near(i):
        def bias_of(h, lse):
            return tile_ref[h * 3 + j - i + 1] - lse

        def sums(h, ds):
            bacc_ref[h * 3 + j - i + 1] += ds
        tile(i, bias_of, sums)

    block_loops(j, lo, hi, far, near)
    HC = heads * 64
    block = pl.ds(pl.multiple_of(j * T, T), T)
    grad_ref[block, HC:2 * HC] = (jnp.concatenate([dk_acc[h] for h in range(heads)], axis=1) * (1.0 / LOG2E)).astype(jnp.bfloat16)
    grad_ref[block, 2 * HC:] = jnp.concatenate([dv_acc[h] for h in range(heads)], axis=1).astype(jnp.bfloat16)

    @pl.when(j == last)
    def _():
        for n in range(dqacc_ref.shape[1] // T):
            grad_ref[n * T:(n + 1) * T, 0:HC] = dqacc_ref[:, n * T:(n + 1) * T].T.astype(jnp.bfloat16)
        zero = jnp.zeros((8, T), jnp.float32)
        sub = lax.broadcasted_iota(jnp.int32, (8, 2 * T), 0)
        for n in range(heads * 3):
            total = jnp.concatenate((bacc_ref[n, 0:8, :], zero), axis=1)
            for g in range(1, T // 8):
                rows = jnp.concatenate((bacc_ref[n, 8 * g:8 * g + 8, :], zero), axis=1)
                total = total + pltpu.roll(rows, 2 * T - 8 * g, 1)
            for bit in (1, 2, 4):
                total = jnp.where((sub & bit) != 0, pltpu.roll(total, 2 * T - bit, 1), total)
            diag_ref[n:n + 1, :] = jnp.sum(total, axis=0, keepdims=True)
        for n in range(heads * 2):
            diag_ref[heads * 3 + n:heads * 3 + n + 1, 0:T] = jnp.sum(far_ref[n], axis=0, keepdims=True)
            diag_ref[heads * 3 + n:heads * 3 + n + 1, T:] = jnp.zeros((1, T), jnp.float32)


def attn_bwd(pair, lo, hi, bias_table, qx, kx, vx, kt, dot, ot, lse, tiles):
    heads = PAIR
    T = TILE
    S = lo.shape[0] * T
    smem = pl.BlockSpec(memory_space=pltpu.SMEM)
    once = lambda shape, index: pl.BlockSpec(shape, lambda i: index, pipeline_mode=pl.Buffered(1))
    rows = lambda n: pl.BlockSpec((T, n), lambda i: (i, pair))
    HC = heads * 64
    return pl.pallas_call(
        functools.partial(attn_bwd_kernel, heads, pair * heads),
        grid=(S // T,),
        out_shape=(jax.ShapeDtypeStruct((S, 3 * HC), jnp.bfloat16), jax.ShapeDtypeStruct((heads * 5, 2 * T), jnp.float32)),
        in_specs=[smem, smem, smem, once((heads * 128, S), (pair, 0)), rows(heads * 128), rows(heads * 128),
                  pl.BlockSpec((HC, T), lambda i: (pair, i)), once((HC, S), (pair, 0)), once((HC, S), (pair, 0)), once((8, S), (0, 0)),
                  once((heads * 3, T, T), (pair, 0, 0))],
        out_specs=(once((S, 3 * HC), (0, 0)), once((heads * 5, 2 * T), (0, 0))),
        scratch_shapes=[pltpu.VMEM((8, S), jnp.float32), pltpu.VMEM((HC, S), jnp.float32),
                        pltpu.VMEM((heads * 3, T, T), jnp.float32), pltpu.VMEM((heads * 2, 8, T), jnp.float32),
                        pltpu.VMEM((heads, T, 64), jnp.float32), pltpu.VMEM((heads, T, 64), jnp.float32)],
        compiler_params=pltpu.CompilerParams(dimension_semantics=("arbitrary",), vmem_limit_bytes=60 << 20),
        cost_estimate=attn_cost(S, heads, 24),
        name="attn_bwd",
    )(lo, hi, bias_table, qx, kx, vx, kt, dot, ot, lse, tiles)


def table_grad(diag, heads):
    T = TILE
    t = jnp.arange(2 * T, dtype=jnp.int32)
    t = jnp.where(t < T, t, t - 2 * T)
    d = jnp.arange(3, dtype=jnp.int32)
    bucket = bucket_of((d[:, None] - 1) * T - t[None, :])
    onehot = (bucket[:, :, None] == jnp.arange(32, dtype=jnp.int32)).astype(jnp.float32)
    near = jnp.einsum("hdt,dtb->bh", diag[:heads * 3].reshape(heads, 3, 2 * T), onehot, precision=lax.Precision.HIGHEST)
    far = jnp.sum(diag[heads * 3:].reshape(heads, 2, 2 * T), axis=2)
    ids = jnp.arange(32, dtype=jnp.int32)[:, None]
    return near + jnp.where(ids == 15, far[None, :, 0], 0.0) + jnp.where(ids == 31, far[None, :, 1], 0.0)


def block_bounds(segment_row):
    S = segment_row.shape[0]
    blocks = segment_row.reshape(S // TILE, TILE)
    first, final = blocks[:, 0], blocks[:, TILE - 1]
    lo = jnp.sum((segment_row[None, :] < first[:, None]).astype(jnp.int32), axis=1) // TILE
    hi = (jnp.sum((segment_row[None, :] <= final[:, None]).astype(jnp.int32), axis=1) - 1) // TILE
    return lo, hi


def pad_heads(w, heads, width):
    D = w.shape[0]
    return jnp.pad(w.reshape(D, heads, 64), ((0, 0), (0, 0), (0, width - 64))).reshape(D, heads * width)


def operands(segment_row):
    S = segment_row.shape[0]
    row = jnp.arange(128, dtype=jnp.int32)
    same = segment_row[None, :] == (row[:, None] - 64)
    inside = (row >= 64) & (row < 80)
    qext = jnp.where(inside[:, None] & same, 1.0, 0.0)
    kext = jnp.where(inside[None, :] & ~same.T, MASKED, 0.0)
    vext = jnp.where(jnp.arange(VROWS) == 64, 1.0, 0.0)[:, None]
    return qext, kext, vext


def padded_weights(w_query, w_key, w_value, heads):
    return pad_heads(w_query, heads, 128), pad_heads(w_key, heads, 128), pad_heads(w_value, heads, VROWS)


def project(normed, weights, ext, heads):
    (qext, kext, vext), (wq, wk, wv) = ext, weights
    f32 = jnp.float32
    qx = lax.dot_general(wq, normed, TN, preferred_element_type=f32) * LOG2E
    qx = (qx + jnp.tile(qext, (heads, 1))).astype(jnp.bfloat16)
    kx = jnp.dot(normed, wk, preferred_element_type=f32)
    kx = (kx + jnp.tile(kext, (1, heads))).astype(jnp.bfloat16)
    vt = lax.dot_general(wv, normed, TN, preferred_element_type=f32)
    vt = (vt + jnp.tile(vext, (heads, 1))).astype(jnp.bfloat16)
    return qx, kx, vt


def project_back(normed, w_vx, w_key):
    vx = jnp.dot(normed, w_vx, preferred_element_type=jnp.float32).astype(jnp.bfloat16)
    kt = lax.dot_general(w_key, normed, TN, preferred_element_type=jnp.float32).astype(jnp.bfloat16)
    return vx, kt


CHUNK = 256
ROOT = math.sqrt(2 / math.pi)


def ffn_kernel(parts, per_part, in_sent, back_sent, n_ref, c_ref, *refs):
    in_refs, back_refs = refs[:parts], refs[parts:2 * parts]
    out_ref, out_mate_ref, norm_ref, norm_mate_ref = refs[2 * parts:2 * parts + 4]
    gin_refs, gback_refs = refs[2 * parts + 4:2 * parts + 6], refs[2 * parts + 6:2 * parts + 8]
    w_in, w_back, out_acc, norm_acc = refs[2 * parts + 8:]
    step = pl.program_id(0)
    f32, bf16 = jnp.float32, jnp.bfloat16
    NT = (((1,), (1,)), ((), ()))
    TN = (((0,), (0,)), ((), ()))

    @pl.when(step == 0)
    def _():
        out_acc[...] = jnp.zeros(out_acc.shape, f32)
        norm_acc[...] = jnp.zeros(norm_acc.shape, f32)

    for q in range(parts):
        @pl.when(step // per_part == q)
        def _():
            w_in[...] = in_refs[q][...]
            w_back[...] = back_refs[q][...]

    rows = n_ref.shape[0]
    inner = lax.dot_general(n_ref[...], w_in[...], NT, preferred_element_type=f32)
    cube = inner * inner * 0.044715
    th = jnp.tanh(ROOT * inner * (1.0 + cube))
    half = 0.5 * (1.0 + th)
    active = (inner * half).astype(bf16)
    slope = half + (0.5 * ROOT) * inner * (1.0 - th * th) * (1.0 + 3.0 * cube)
    grad = (lax.dot_general(c_ref[...], w_back[...], NT, preferred_element_type=f32) * slope).astype(bf16)
    norm_acc[...] += jnp.dot(grad, w_in[...], preferred_element_type=f32)
    out_acc[...] += jnp.dot(active, w_back[...], preferred_element_type=f32)
    gin = lax.dot_general(grad, n_ref[...], TN, preferred_element_type=f32).astype(bf16)
    gback = lax.dot_general(active, c_ref[...], TN, preferred_element_type=f32).astype(bf16)
    part = step // per_part
    for grad_refs, value, sent in ((gin_refs, gin, in_sent), (gback_refs, gback, back_sent)):
        leaves = functools.reduce(jnp.logical_or, [part == q for q in sent], False)

        @pl.when(leaves)
        def _():
            grad_refs[1][...] = value

        @pl.when(jnp.logical_not(leaves))
        def _():
            grad_refs[0][...] = value

    @pl.when(step == pl.num_programs(0) - 1)
    def _():
        own = out_ref.shape[0]
        out_ref[...] = out_acc[:own, :]
        out_mate_ref[...] = out_acc[own:, :].astype(bf16)
        norm_ref[...] = norm_acc[:own, :]
        norm_mate_ref[...] = norm_acc[own:, :].astype(bf16)


def ffn(normed, cot, in_parts, back_parts, in_sent, back_sent):
    parts = len(in_parts)
    units, width = in_parts[0].shape
    rows = normed.shape[0]
    chunk = min(CHUNK, units)
    per_part = units // chunk
    once = lambda shape: pl.BlockSpec(shape, lambda i: (0, 0), pipeline_mode=pl.Buffered(1))
    piece = lambda q: pl.BlockSpec((chunk, width), lambda i: (jnp.clip(i - q * per_part, 0, per_part - 1), 0))
    weights = [piece(q) for q in range(parts)]
    sums = [jax.ShapeDtypeStruct((rows // 2, width), kind) for kind in (jnp.float32, jnp.bfloat16)]
    grads, grad_specs = [], []
    for sent in (in_sent, back_sent):
        for members in ([q for q in range(parts) if q not in sent], list(sent)):
            steps = [q * per_part + n for q in members for n in range(per_part)]
            index = lambda i, ups=tuple(steps[1:]): (sum([(i >= up).astype(jnp.int32) for up in ups], jnp.int32(0)), 0)
            grads.append(jax.ShapeDtypeStruct((len(members) * units, width), jnp.bfloat16))
            grad_specs.append(pl.BlockSpec((chunk, width), index))
    return pl.pallas_call(
        functools.partial(ffn_kernel, parts, per_part, in_sent, back_sent),
        grid=(parts * per_part,),
        out_shape=sums * 2 + grads,
        in_specs=[once((rows, width)), once((rows, width))] + weights * 2,
        out_specs=[once((rows // 2, width))] * 4 + grad_specs,
        scratch_shapes=[pltpu.VMEM((chunk, width), jnp.bfloat16)] * 2 + [pltpu.VMEM((rows, width), jnp.float32)] * 2,
        compiler_params=pltpu.CompilerParams(dimension_semantics=("arbitrary",), vmem_limit_bytes=60 << 20),
        cost_estimate=pl.CostEstimate(flops=int(35e9), transcendentals=0, bytes_accessed=16 << 20),
        name="ffn",
    )(normed, cot, *in_parts, *back_parts)


def over_rows(left_side, right_side):
    return lax.dot_general(
        left_side, right_side, (((0,), (0,)), ((), ())), preferred_element_type=jnp.float32
    )


def against(left_side, right_side):
    return lax.dot_general(
        left_side, right_side, (((1,), (1,)), ((), ())), preferred_element_type=jnp.float32
    )


def matmul(left_side, right_side):
    return jnp.dot(left_side, right_side, preferred_element_type=jnp.float32)


def norm_back(grad_normed, unit_rows, inv_scale, gain_row):
    scaled = grad_normed * gain_row
    return inv_scale * (scaled - unit_rows * jnp.mean(scaled * unit_rows, axis=-1, keepdims=True))


def low(values_in):
    return values_in.astype(jnp.bfloat16)


def wide(values_in):
    return values_in.astype(jnp.float32)


def bits_of(size):
    return [1 << n for n in range(size.bit_length() - 1)]


def tie(*values):
    return lax.optimization_barrier(values)


def finish(steps):
    for step in steps:
        last = step
    return last


def send_or_none(steps, value):
    try:
        return steps.send(value)
    except StopIteration:
        return None


class Slice:
    def __init__(self, mesh):
        self.dp, self.group, self.tensor = (mesh.shape[name] for name in ("dp", "group", "tensor"))

    def swap(self, array, axis, mask):
        size = getattr(self, axis)
        return lax.ppermute(array, axis, [(i, i ^ mask) for i in range(size)])

    def pair_swap(self, array):
        return self.swap(array, "group", 1)

    def row_steps(self):
        return [("group", 2 * bit) for bit in bits_of(self.group // 2)]

    def col_steps(self):
        return [("dp", bit) for bit in bits_of(self.dp)]

    def spread(self, block):
        have = {(0, 0): block}
        size = self.dp * self.group
        for col in range(self.dp):
            for row in range(self.group // 2):
                mask = col * self.group + 2 * row
                if mask:
                    have[col, row] = lax.ppermute(block, ("dp", "group"), [(i, i ^ mask) for i in range(size)])
        return have

    def collect_order(self, rows_first):
        steps = self.row_steps() + self.col_steps() if rows_first else self.col_steps() + self.row_steps()
        return list(reversed(steps))

    def sent_first(self, keys, rows_first):
        return self.sent_first_of(keys, self.collect_order(rows_first)[0])

    def collect(self, keys, kept, sent, rows_first):
        order = self.collect_order(rows_first)
        leaves = self.sent_first(keys, rows_first)
        keys = [key for n, key in enumerate(keys) if n not in leaves]
        units = kept.shape[0] // len(keys)
        for n, (axis, mask) in enumerate(order):
            other = yield self.swap(sent, axis, mask)
            total = low(wide(kept) + wide(other))
            if n + 1 < len(order):
                leaves = self.sent_first_of(keys, order[n + 1])
                block = lambda k: total[k * units:(k + 1) * units]
                pick = lambda ks: block(ks[0]) if len(ks) == 1 else jnp.concatenate([block(k) for k in ks], axis=0)
                kept, sent = pick([k for k in range(len(keys)) if k not in leaves]), pick(list(leaves))
                keys = [key for k, key in enumerate(keys) if k not in leaves]
        yield total

    def sent_first_of(self, keys, step):
        axis, mask = step
        return tuple(n for n, (col, row) in enumerate(keys) if (row & mask // 2 if axis == "group" else col & mask))

    def slot(self):
        rows = self.group // 2
        group = lax.axis_index("group")
        return (group % 2) * (self.dp * rows) + lax.axis_index("dp") * rows + group // 2

    def slot_gather(self, block):
        for axis, mask in self.row_steps() + self.col_steps() + [("group", 1)]:
            upper = (lax.axis_index(axis) // mask) % 2 == 1
            other = self.swap(block, axis, mask)
            yield other
            block = jnp.concatenate((jnp.where(upper, other, block), jnp.where(upper, block, other)), axis=2)
        yield block.reshape(block.shape[0], -1, block.shape[3])

    def plane_sum(self, grad, others):
        mine = lax.axis_index("dp")
        for axis, mask in reversed(self.col_steps()):
            half = grad.shape[0] // 2
            bit = (mine // mask) % 2
            keep = lax.dynamic_slice_in_dim(grad, bit * half, half, 0)
            send = lax.dynamic_slice_in_dim(grad, (1 - bit) * half, half, 0)
            other = self.swap(send, axis, mask)
            grad = low(wide(keep) + wide(other))
        for axis, mask in self.row_steps() + [("group", 1)]:
            other = self.swap(grad, axis, mask)
            if axis == "group" and mask == 2:
                other, others = tie(other, others)
            grad = low(wide(grad) + wide(other))
        return grad[0], others

    def tensor_parts(self, vector):
        return [vector] + [self.swap(vector, "tensor", mask) for mask in range(1, self.tensor)]

    def tensor_total(self, parts):
        while len(parts) > 1:
            parts = [one + two for one, two in zip(parts[::2], parts[1::2])]
        return parts[0]

    def col_exchange(self, blocks):
        mine = lax.axis_index("dp")
        for axis, mask in reversed(self.col_steps()):
            half = blocks.shape[3] // 2
            upper = (mine // mask) % 2 == 1
            low_half, high_half = blocks[..., :half], blocks[..., half:]
            keep = jnp.where(upper, high_half, low_half)
            other = self.swap(jnp.where(upper, low_half, high_half), axis, mask)
            pair = jnp.where(upper, jnp.stack((other, keep), axis=1), jnp.stack((keep, other), axis=1))
            blocks = pair.reshape((pair.shape[0], -1) + pair.shape[3:])
        if self.dp > 2:
            count, bits = blocks.shape[0], self.dp.bit_length() - 1
            split = blocks.reshape((count,) + (2,) * bits + blocks.shape[2:])
            split = split.transpose((0,) + tuple(range(bits, 0, -1)) + (bits + 1, bits + 2))
            blocks = split.reshape(blocks.shape)
        return blocks

    def group_gather(self, block):
        block = block[None]
        for mask in reversed(bits_of(self.group)):
            upper = (lax.axis_index("group") // mask) % 2 == 1
            other = self.swap(block, "group", mask)
            block = jnp.where(upper, jnp.stack((other, block), axis=1), jnp.stack((block, other), axis=1))
            block = block.reshape((-1,) + block.shape[2:])
        return block

    def col_exchange_rows(self, rows):
        return self.col_exchange(rows[None, None])[0]


def on_device(
    sl,
    inputs,
    segments,
    gain_attn,
    w_query,
    w_key,
    w_value,
    w_out,
    bias_table,
    gain_ffn,
    w_in,
    w_back,
    cotangent,
):
    heads_here = bias_table.shape[1]
    width = inputs.shape[1]
    pairs = heads_here // PAIR
    cols = PAIR * 64
    dp_index, group_index = lax.axis_index("dp"), lax.axis_index("group")
    segment_row = segments.reshape(-1)
    lo, hi = block_bounds(segment_row)
    tiles = bias_tiles(bias_table)

    stream = wide(inputs)
    inv_attn = lax.rsqrt(jnp.mean(stream * stream, axis=-1, keepdims=True) + EPSILON)
    unit_attn = stream * inv_attn
    rows = stream.shape[0]
    units_g = w_back.shape[0] // sl.group
    units = units_g // sl.dp
    start = group_index * units_g + dp_index * units
    plane = sl.dp * sl.group
    slot = sl.slot()
    qkv = [jnp.concatenate([w[:, k * cols:(k + 1) * cols] for w in (w_query, w_key, w_value)], axis=1) for k in range(pairs)]
    n_out, n_qkv = w_out.shape[0] // plane, 3 * cols // plane
    own_in = [lax.dynamic_slice_in_dim(w_in, start, units, 1).T]
    own_in.append(lax.dynamic_slice_in_dim(w_out, slot * n_out, n_out, 0))
    own_in = jnp.concatenate(own_in, axis=0)
    own_back = lax.dynamic_slice_in_dim(w_back, start, units, 0)
    own_qkv = jnp.concatenate([lax.dynamic_slice_in_dim(qkv[k], slot * n_qkv, n_qkv, 1).T for k in range(pairs)], axis=0)
    cot_pair = jnp.concatenate((cotangent, sl.pair_swap(cotangent)), axis=0)
    prep = (tiles, padded_weights(w_query, w_key, w_value, heads_here), operands(segment_row), cot_pair, pad_heads(w_value, heads_here, 128))
    by_pair = lambda block, rows: block.reshape(sl.tensor, pairs, rows, width).transpose(1, 0, 2, 3)
    in_z = lax.all_gather(own_in, "tensor", axis=0, tiled=False)
    own_normed, in_z = tie(low(unit_attn * gain_attn), in_z)
    normed = lax.all_gather(own_normed, "tensor", axis=0, tiled=True)
    in_parts = sl.spread(in_z[:, :units].reshape(-1, width))
    out_full = finish(sl.slot_gather(in_z[:, units:][None]))[0]
    n_rows = own_qkv.shape[0]
    own_qkv = jnp.pad(own_qkv, ((0, -n_rows % 128), (0, 0)))
    own_back, normed, prep, in_parts, qkv, out_full, own_qkv = tie(own_back, normed, prep, in_parts, qkv, out_full, own_qkv)
    tiles, padded, ext, cot_pair, w_vx = prep
    back_z = lax.all_gather(own_back, "tensor", axis=0, tiled=True)

    qx, kx, vt = project(normed, padded, ext, heads_here)
    ctx_t, lse = attn_fwd(lo, hi, bias_table, qx, kx, vt, tiles)
    back_z, ctx_t, own_qkv = tie(back_z, ctx_t, own_qkv)
    qkv_z = lax.all_gather(own_qkv, "tensor", axis=0, tiled=False)[:, :n_rows]
    back_parts = sl.spread(back_z)
    ctx_rows = lax.all_to_all(ctx_t, "tensor", split_axis=1, concat_axis=0, tiled=True)
    hidden = stream + over_rows(ctx_rows, out_full)
    inv_ffn = lax.rsqrt(jnp.mean(hidden * hidden, axis=-1, keepdims=True) + EPSILON)
    unit_ffn = hidden * inv_ffn

    normed_ffn, qkv_z, back_parts = tie(low(unit_ffn * gain_ffn), qkv_z, back_parts)
    qkv_all = lax.all_gather(qkv_z, ("dp", "group"), axis=0, tiled=False)
    normed_pair = jnp.concatenate((normed_ffn, sl.pair_swap(normed_ffn)), axis=0)
    keys = sorted(in_parts)
    results = ffn(
        normed_pair, cot_pair, [in_parts[key] for key in keys], [back_parts[key] for key in keys],
        sl.sent_first(keys, True), sl.sent_first(keys, False),
    )
    out_own, out_mate, normed_own, normed_mate = results[:4]
    in_steps, back_steps = sl.collect(keys, *results[4:6], True), sl.collect(keys, *results[6:8], False)
    normed_own, qkv_all = tie(normed_own, qkv_all)
    grad_normed_ffn = normed_own + wide(sl.pair_swap(normed_mate))
    output = hidden + out_own + wide(sl.pair_swap(out_mate))

    gain_ffn_part = jnp.sum(grad_normed_ffn * unit_ffn, axis=0)
    grad_hidden = wide(cotangent) + norm_back(grad_normed_ffn, unit_ffn, inv_ffn, gain_ffn)
    grad_hidden_low = low(grad_hidden)
    grad_ctx = low(against(out_full, grad_hidden_low))
    grad_hidden_late, grad_ctx, normed = tie(grad_hidden_low, grad_ctx, normed)
    vx, kt = project_back(normed, w_vx, w_key)
    grad_ctx_t = lax.all_to_all(grad_ctx, "tensor", split_axis=0, concat_axis=1, tiled=True)

    grad_w_out = low(matmul(ctx_rows, grad_hidden_late)).reshape(sl.tensor, sl.group, -1, width)

    def out_scatter(grad):
        for mask in bits_of(sl.group):
            grad = grad.reshape((sl.tensor, -1, 2) + grad.shape[2:])
            bit = (group_index // mask) % 2
            keep = lax.dynamic_index_in_dim(grad, bit, 2, keepdims=False)
            other = sl.swap(lax.dynamic_index_in_dim(grad, 1 - bit, 2, keepdims=False), "group", mask)
            other = yield other
            grad = low(wide(keep) + wide(other))
        grad = grad[:, 0]
        for axis, mask in reversed(sl.col_steps()):
            n = grad.shape[1] // 2
            bit = (dp_index // mask) % 2
            keep = lax.dynamic_slice_in_dim(grad, bit * n, n, 1)
            other = sl.swap(lax.dynamic_slice_in_dim(grad, (1 - bit) * n, n, 1), axis, mask)
            other = yield other
            grad = low(wide(keep) + wide(other))
        yield grad

    out_steps = out_scatter(grad_w_out)
    first, grad_ctx_t, vx, kt = tie((next(in_steps), next(back_steps), next(out_steps)), grad_ctx_t, vx, kt)
    second = [steps.send(other) for steps, other in zip((in_steps, back_steps, out_steps), first)]
    tables, grad_parts, grad_rows = [], [], []
    for k in range(pairs):
        lo_k = lo
        if k == pairs - 1:
            own_sums = []
            if k > 0:
                second, grad_parts[-1] = tie(second, grad_parts[-1])
            for steps, last in zip((in_steps, back_steps, out_steps), second):
                for other in iter(lambda: send_or_none(steps, last), None):
                    last = other
                own_sums.append(last)
            own_sums = jnp.concatenate([part.reshape(sl.tensor, -1, width) for part in own_sums], axis=1)
            lo_k, own_sums = tie(lo, own_sums)
            own_rows = own_sums.shape[1]
            summed = lax.psum_scatter(own_sums.reshape(-1, width), "tensor", scatter_dimension=0, tiled=True)
        grads, diag = attn_bwd(k, lo_k, hi, bias_table, qx, kx, vx, kt, grad_ctx_t, ctx_t, lse, tiles)
        grad_parts.append(grads)
        if k > 0:
            grads, diag, grad_rows[k - 1] = tie(grads, diag, grad_rows[k - 1])
        grad_rows.append(lax.all_to_all(grads, "tensor", split_axis=0, concat_axis=1, tiled=True))
        tables.append(table_grad(diag, PAIR))

    summed = sl.col_exchange_rows(summed)
    grad_parts = tie(*grad_parts)
    gain_dot, grad_w_qkv = 0.0, []
    for k in range(pairs):
        grad_w = over_rows(normed, grad_parts[k])
        gain_dot = gain_dot + jnp.sum(grad_w * wide(qkv[k]), axis=1)
        grad_w_qkv.append(low(grad_w))

    columns = pairs * 3 * cols
    small = jnp.concatenate([gain_dot / gain_attn, gain_ffn_part] + [table.T.reshape(-1) for table in tables])
    small_rows = -(-small.shape[0] // columns)
    small = low(jnp.pad(small, (0, small_rows * columns - small.shape[0]))).reshape(1, small_rows, columns)
    grad_w_qkv = jnp.concatenate(grad_w_qkv, axis=1).reshape(sl.dp, -1, columns)
    grad_w_qkv = jnp.concatenate((grad_w_qkv, jnp.tile(small, (sl.dp, 1, 1))), axis=1)
    grad_w_qkv, (grad_rows, summed) = sl.plane_sum(grad_w_qkv, (grad_rows, summed))
    small = grad_w_qkv[-small_rows:].reshape(-1)
    grad_w_qkv = wide(grad_w_qkv[:-small_rows])
    gain_parts = sl.tensor_parts(wide(small[:2 * width]))
    table_rows = bias_table.shape[0] // sl.dp
    grad_table = wide(small[2 * width:2 * width + bias_table.size]).reshape(heads_here, -1)
    grad_table = lax.dynamic_slice_in_dim(grad_table, dp_index * table_rows, table_rows, 1).T

    everything = sl.group_gather(summed)
    cuts = [0, units, 2 * units, own_rows]
    pick = lambda n: wide(everything[:, :, cuts[n]:cuts[n + 1]].reshape(-1, width // sl.dp))
    grad_w_in, grad_w_back, grad_w_out = pick(0).T, pick(1), pick(2)
    qkv_all = qkv_all.reshape(sl.dp, sl.group // 2, 2, sl.tensor, pairs, n_qkv, width).transpose(4, 3, 2, 0, 1, 5, 6)
    qkv_full = qkv_all.reshape(pairs, -1, width)
    grad_normed = 0.0
    for k in range(pairs):
        grad_normed = grad_normed + matmul(grad_rows[k], qkv_full[k])
    grad_inputs = grad_hidden + norm_back(grad_normed, unit_attn, inv_attn, gain_attn)
    grad_w_query, grad_w_key, grad_w_value = (
        jnp.concatenate([grad_w_qkv[:, (3 * k + n) * cols:(3 * k + n + 1) * cols] for k in range(pairs)], axis=1) for n in range(3)
    )
    weight_grads = (grad_w_query, grad_w_key, grad_w_value, grad_w_out, grad_w_in, grad_w_back)
    gain_parts, weight_grads = tie(gain_parts, weight_grads)
    grad_w_query, grad_w_key, grad_w_value, grad_w_out, grad_w_in, grad_w_back = weight_grads
    gain_grads = sl.tensor_total(gain_parts)
    return (
        output,
        grad_inputs,
        gain_grads[:width],
        grad_w_query,
        grad_w_key,
        grad_w_value,
        grad_w_out,
        grad_table,
        gain_grads[width:],
        grad_w_in,
        grad_w_back,
    )


def solution(mesh):
    return jax.shard_map(
        functools.partial(on_device, Slice(mesh)),
        mesh=mesh,
        in_specs=(
            P(("dp", "group", "tensor"), None),
            P(("dp", "group"), None),
            P(),
            P(None, "tensor"),
            P(None, "tensor"),
            P(None, "tensor"),
            P("tensor", None),
            P(None, "tensor"),
            P(),
            P(None, "tensor"),
            P("tensor", None),
            P(("dp", "group", "tensor"), None),
        ),
        out_specs=(
            P(("dp", "group", "tensor"), None),
            P(("dp", "group", "tensor"), None),
            P(),
            P("dp", "tensor"),
            P("dp", "tensor"),
            P("dp", "tensor"),
            P("tensor", "dp"),
            P("dp", "tensor"),
            P(),
            P("dp", "tensor"),
            P("tensor", "dp"),
        ),
        check_vma=False,
    )
```

```python
import functools
import math

import jax
import jax.numpy as jnp
from jax import lax
from jax.experimental import pallas as pl
from jax.experimental.pallas import tpu as pltpu
from jax.sharding import PartitionSpec as P

EPSILON = 1e-06

LOG2E = math.log2(math.e)
MASKED = -1e30
TILE = 256
VROWS = 80
PAIR = 2
TN = (((0,), (1,)), ((), ()))
reach_marks = (12, 16, 23, 32, 46, 64, 91)


def bucket_of(offset):
    distance = jnp.abs(offset)
    far_bucket = jnp.full(offset.shape, 8, jnp.int32)
    for threshold in reach_marks:
        far_bucket = far_bucket + (distance >= threshold).astype(jnp.int32)
    return 16 * (offset > 0).astype(jnp.int32) + jnp.where(distance < 8, distance, far_bucket)


def bias_tiles_kernel(heads, table_ref, tile_ref):
    T = TILE
    for d in range(3):
        t = lax.broadcasted_iota(jnp.int32, (8, 2 * T), 1)
        t = jnp.where(t < T, t, t - 2 * T)
        bucket = bucket_of((d - 1) * T - t)
        for h in range(heads):
            row = jnp.zeros((8, 2 * T), jnp.float32)
            for b in range(32):
                row = jnp.where(bucket == b, table_ref[b, h] * LOG2E, row)
            wide = jnp.broadcast_to(row[0:1], (T, 2 * T))
            rolled = pltpu.roll(wide, 0, 1, stride=1, stride_axis=0)
            tile_ref[h * 3 + d] = rolled[:, :T]


def bias_tiles(bias_table):
    heads = bias_table.shape[1]
    return pl.pallas_call(
        functools.partial(bias_tiles_kernel, heads),
        out_shape=jax.ShapeDtypeStruct((heads * 3, TILE, TILE), jnp.float32),
        in_specs=[pl.BlockSpec(memory_space=pltpu.SMEM)],
        out_specs=pl.BlockSpec(memory_space=pltpu.VMEM),
        name="bias_tiles",
    )(bias_table)


def block_loops(i, lo, hi, far, near):
    lax.fori_loop(lo, i - 1, lambda j, _: far(j, 0) or 0, 0)
    lax.fori_loop(jnp.maximum(lo, i - 1), jnp.minimum(hi, i + 1) + 1, lambda j, _: near(j) or 0, 0)
    lax.fori_loop(i + 2, hi + 1, lambda j, _: far(j, 1) or 0, 0)


def attn_fwd_kernel(heads, first, lo_ref, hi_ref, table_ref, qx_ref, kx_ref, vt_ref, tile_ref, o_ref, lse_ref, m_ref, acc_ref, s_ref):
    T = TILE
    i = pl.program_id(0)
    lo, hi = lo_ref[i], hi_ref[i]
    m_ref[...] = jnp.full(m_ref.shape, MASKED, jnp.float32)
    acc_ref[...] = jnp.zeros(acc_ref.shape, jnp.float32)

    def scores(j, bias_of):
        start = pl.multiple_of(j * T, T)
        for h in range(heads):
            k = kx_ref[pl.ds(start, T), h * 128:(h + 1) * 128]
            s = jnp.dot(k, qx_ref[h * 128:(h + 1) * 128, :], preferred_element_type=jnp.float32)
            s = s + bias_of(h)
            s_ref[j - lo, h] = s
            m_ref[h] = jnp.maximum(m_ref[h], jnp.max(s.reshape(T // 8, 8, T), axis=0))

    def far(j, side):
        scores(j, lambda h: table_ref[16 * side + 15, first + h] * LOG2E)

    def near(j):
        scores(j, lambda h: tile_ref[h * 3 + j - i + 1])

    block_loops(i, lo, hi, far, near)
    tops = [jnp.max(m_ref[h], axis=0, keepdims=True) for h in range(heads)]

    def values(j, _):
        start = pl.multiple_of(j * T, T)
        for h in range(heads):
            p = jnp.exp2(s_ref[j - lo, h] - tops[h]).astype(jnp.bfloat16)
            rows = slice(h * VROWS, (h + 1) * VROWS)
            acc_ref[rows, :] += jnp.dot(vt_ref[rows, pl.ds(start, T)], p, preferred_element_type=jnp.float32)
        return 0

    lax.fori_loop(lo, hi + 1, values, 0)
    for h in range(heads):
        total = acc_ref[h * VROWS + 64:h * VROWS + 65, :]
        o_ref[h * 64:(h + 1) * 64, :] = (acc_ref[h * VROWS:h * VROWS + 64, :] / total).astype(jnp.bfloat16)
        lse_ref[h:h + 1, :] = tops[h] + jnp.log2(total)


def attn_cost(seq_len, heads, micros):
    return pl.CostEstimate(flops=int(micros * 1e9), transcendentals=0, bytes_accessed=seq_len * heads * 2048)


def attn_fwd(lo, hi, bias_table, qx, kx, vt, tiles):
    heads = bias_table.shape[1]
    T = TILE
    S = lo.shape[0] * T
    smem = pl.BlockSpec(memory_space=pltpu.SMEM)
    once = lambda shape, index: pl.BlockSpec(shape, lambda i: index, pipeline_mode=pl.Buffered(1))
    return pl.pallas_call(
        functools.partial(attn_fwd_kernel, heads, 0),
        grid=(S // T,),
        out_shape=(jax.ShapeDtypeStruct((heads * 64, S), jnp.bfloat16), jax.ShapeDtypeStruct((8, S), jnp.float32)),
        in_specs=[smem, smem, smem, pl.BlockSpec((heads * 128, T), lambda i: (0, i)), once((S, heads * 128), (0, 0)),
                  once((heads * VROWS, S), (0, 0)), once((heads * 3, T, T), (0, 0, 0))],
        out_specs=(pl.BlockSpec((heads * 64, T), lambda i: (0, i)), pl.BlockSpec((8, T), lambda i: (0, i))),
        scratch_shapes=[pltpu.VMEM((heads, 8, T), jnp.float32), pltpu.VMEM((heads * VROWS, T), jnp.float32),
                        pltpu.VMEM((S // T, heads, T, T), jnp.float32)],
        compiler_params=pltpu.CompilerParams(dimension_semantics=("arbitrary",), vmem_limit_bytes=24 << 20),
        cost_estimate=attn_cost(S, heads, 25),
        name="attn_fwd",
    )(lo, hi, bias_table, qx, kx, vt, tiles)


def attn_bwd_kernel(heads, first, lo_ref, hi_ref, table_ref, qx_ref, kx_ref, vx_ref, kt_ref, dot_ref, ot_ref, lse_ref, tile_ref,
                    grad_ref, diag_ref, d_ref, dqacc_ref, bacc_ref, far_ref, dk_acc, dv_acc):
    T = TILE
    j = pl.program_id(0)
    last = pl.num_programs(0) - 1
    lo, hi = lo_ref[j], hi_ref[j]
    NT = (((1,), (1,)), ((), ()))

    @pl.when(j == 0)
    def _():
        dqacc_ref[...] = jnp.zeros(dqacc_ref.shape, jnp.float32)
        bacc_ref[...] = jnp.zeros(bacc_ref.shape, jnp.float32)
        far_ref[...] = jnp.zeros(far_ref.shape, jnp.float32)
        for h in range(heads):
            rows = slice(h * 64, (h + 1) * 64)
            d_ref[h:h + 1, :] = jnp.sum(dot_ref[rows, :].astype(jnp.float32) * ot_ref[rows, :].astype(jnp.float32), axis=0, keepdims=True)

    dk_acc[...] = jnp.zeros(dk_acc.shape, jnp.float32)
    dv_acc[...] = jnp.zeros(dv_acc.shape, jnp.float32)

    def tile(i, bias_of, sums):
        cols = pl.ds(pl.multiple_of(i * T, T), T)
        for h in range(heads):
            rows = slice(h * 64, (h + 1) * 64)
            q = qx_ref[h * 128:(h + 1) * 128, cols]
            do = dot_ref[rows, cols]
            s = jnp.dot(kx_ref[:, h * 128:(h + 1) * 128], q, preferred_element_type=jnp.float32)
            p = jnp.exp2(s + bias_of(h, lse_ref[first + h:first + h + 1, cols]))
            dp = jnp.dot(vx_ref[:, h * 128:h * 128 + 64], do, preferred_element_type=jnp.float32)
            ds = p * (dp - d_ref[h:h + 1, cols])
            sums(h, ds)
            pb = p.astype(jnp.bfloat16)
            db = ds.astype(jnp.bfloat16)
            dv_acc[h] += lax.dot_general(pb, do, NT, preferred_element_type=jnp.float32)
            dk_acc[h] += lax.dot_general(db, q[:64], NT, preferred_element_type=jnp.float32)
            dqacc_ref[rows, cols] += jnp.dot(kt_ref[rows, :], db, preferred_element_type=jnp.float32)

    def far(i, later):
        side = 1 - later

        def bias_of(h, lse):
            return table_ref[16 * side + 15, first + h] * LOG2E - lse

        def sums(h, ds):
            far_ref[h * 2 + side] += jnp.sum(ds.reshape(T // 8, 8, T), axis=0)
        tile(i, bias_of, sums)

    def near(i):
        def bias_of(h, lse):
            return tile_ref[h * 3 + j - i + 1] - lse

        def sums(h, ds):
            bacc_ref[h * 3 + j - i + 1] += ds
        tile(i, bias_of, sums)

    block_loops(j, lo, hi, far, near)
    HC = heads * 64
    block = pl.ds(pl.multiple_of(j * T, T), T)
    grad_ref[block, HC:2 * HC] = (jnp.concatenate([dk_acc[h] for h in range(heads)], axis=1) * (1.0 / LOG2E)).astype(jnp.bfloat16)
    grad_ref[block, 2 * HC:] = jnp.concatenate([dv_acc[h] for h in range(heads)], axis=1).astype(jnp.bfloat16)

    @pl.when(j == last)
    def _():
        for n in range(dqacc_ref.shape[1] // T):
            grad_ref[n * T:(n + 1) * T, 0:HC] = dqacc_ref[:, n * T:(n + 1) * T].T.astype(jnp.bfloat16)
        zero = jnp.zeros((8, T), jnp.float32)
        sub = lax.broadcasted_iota(jnp.int32, (8, 2 * T), 0)
        for n in range(heads * 3):
            total = jnp.concatenate((bacc_ref[n, 0:8, :], zero), axis=1)
            for g in range(1, T // 8):
                rows = jnp.concatenate((bacc_ref[n, 8 * g:8 * g + 8, :], zero), axis=1)
                total = total + pltpu.roll(rows, 2 * T - 8 * g, 1)
            for bit in (1, 2, 4):
                total = jnp.where((sub & bit) != 0, pltpu.roll(total, 2 * T - bit, 1), total)
            diag_ref[n:n + 1, :] = jnp.sum(total, axis=0, keepdims=True)
        for n in range(heads * 2):
            diag_ref[heads * 3 + n:heads * 3 + n + 1, 0:T] = jnp.sum(far_ref[n], axis=0, keepdims=True)
            diag_ref[heads * 3 + n:heads * 3 + n + 1, T:] = jnp.zeros((1, T), jnp.float32)


def attn_bwd(pair, lo, hi, bias_table, qx, kx, vx, kt, dot, ot, lse, tiles):
    heads = PAIR
    T = TILE
    S = lo.shape[0] * T
    smem = pl.BlockSpec(memory_space=pltpu.SMEM)
    once = lambda shape, index: pl.BlockSpec(shape, lambda i: index, pipeline_mode=pl.Buffered(1))
    rows = lambda n: pl.BlockSpec((T, n), lambda i: (i, pair))
    HC = heads * 64
    return pl.pallas_call(
        functools.partial(attn_bwd_kernel, heads, pair * heads),
        grid=(S // T,),
        out_shape=(jax.ShapeDtypeStruct((S, 3 * HC), jnp.bfloat16), jax.ShapeDtypeStruct((heads * 5, 2 * T), jnp.float32)),
        in_specs=[smem, smem, smem, once((heads * 128, S), (pair, 0)), rows(heads * 128), rows(heads * 128),
                  pl.BlockSpec((HC, T), lambda i: (pair, i)), once((HC, S), (pair, 0)), once((HC, S), (pair, 0)), once((8, S), (0, 0)),
                  once((heads * 3, T, T), (pair, 0, 0))],
        out_specs=(once((S, 3 * HC), (0, 0)), once((heads * 5, 2 * T), (0, 0))),
        scratch_shapes=[pltpu.VMEM((8, S), jnp.float32), pltpu.VMEM((HC, S), jnp.float32),
                        pltpu.VMEM((heads * 3, T, T), jnp.float32), pltpu.VMEM((heads * 2, 8, T), jnp.float32),
                        pltpu.VMEM((heads, T, 64), jnp.float32), pltpu.VMEM((heads, T, 64), jnp.float32)],
        compiler_params=pltpu.CompilerParams(dimension_semantics=("arbitrary",), vmem_limit_bytes=60 << 20),
        cost_estimate=attn_cost(S, heads, 24),
        name="attn_bwd",
    )(lo, hi, bias_table, qx, kx, vx, kt, dot, ot, lse, tiles)


def table_grad(diag, heads):
    T = TILE
    t = jnp.arange(2 * T, dtype=jnp.int32)
    t = jnp.where(t < T, t, t - 2 * T)
    d = jnp.arange(3, dtype=jnp.int32)
    bucket = bucket_of((d[:, None] - 1) * T - t[None, :])
    onehot = (bucket[:, :, None] == jnp.arange(32, dtype=jnp.int32)).astype(jnp.float32)
    near = jnp.einsum("hdt,dtb->bh", diag[:heads * 3].reshape(heads, 3, 2 * T), onehot, precision=lax.Precision.HIGHEST)
    far = jnp.sum(diag[heads * 3:].reshape(heads, 2, 2 * T), axis=2)
    ids = jnp.arange(32, dtype=jnp.int32)[:, None]
    return near + jnp.where(ids == 15, far[None, :, 0], 0.0) + jnp.where(ids == 31, far[None, :, 1], 0.0)


def block_bounds(segment_row):
    S = segment_row.shape[0]
    blocks = segment_row.reshape(S // TILE, TILE)
    first, final = blocks[:, 0], blocks[:, TILE - 1]
    lo = jnp.sum((segment_row[None, :] < first[:, None]).astype(jnp.int32), axis=1) // TILE
    hi = (jnp.sum((segment_row[None, :] <= final[:, None]).astype(jnp.int32), axis=1) - 1) // TILE
    return lo, hi


def pad_heads(w, heads, width):
    D = w.shape[0]
    return jnp.pad(w.reshape(D, heads, 64), ((0, 0), (0, 0), (0, width - 64))).reshape(D, heads * width)


def operands(segment_row):
    S = segment_row.shape[0]
    row = jnp.arange(128, dtype=jnp.int32)
    same = segment_row[None, :] == (row[:, None] - 64)
    inside = (row >= 64) & (row < 80)
    qext = jnp.where(inside[:, None] & same, 1.0, 0.0)
    kext = jnp.where(inside[None, :] & ~same.T, MASKED, 0.0)
    vext = jnp.where(jnp.arange(VROWS) == 64, 1.0, 0.0)[:, None]
    return qext, kext, vext


def padded_weights(w_query, w_key, w_value, heads):
    return pad_heads(w_query, heads, 128), pad_heads(w_key, heads, 128), pad_heads(w_value, heads, VROWS)


def project(normed, weights, ext, heads):
    (qext, kext, vext), (wq, wk, wv) = ext, weights
    f32 = jnp.float32
    qx = lax.dot_general(wq, normed, TN, preferred_element_type=f32) * LOG2E
    qx = (qx + jnp.tile(qext, (heads, 1))).astype(jnp.bfloat16)
    kx = jnp.dot(normed, wk, preferred_element_type=f32)
    kx = (kx + jnp.tile(kext, (1, heads))).astype(jnp.bfloat16)
    vt = lax.dot_general(wv, normed, TN, preferred_element_type=f32)
    vt = (vt + jnp.tile(vext, (heads, 1))).astype(jnp.bfloat16)
    return qx, kx, vt


def project_back(normed, w_vx, w_key):
    vx = jnp.dot(normed, w_vx, preferred_element_type=jnp.float32).astype(jnp.bfloat16)
    kt = lax.dot_general(w_key, normed, TN, preferred_element_type=jnp.float32).astype(jnp.bfloat16)
    return vx, kt


CHUNK = 256
ROOT = math.sqrt(2 / math.pi)


def ffn_kernel(parts, per_part, in_sent, back_sent, n_ref, c_ref, *refs):
    in_refs, back_refs = refs[:parts], refs[parts:2 * parts]
    out_ref, out_mate_ref, norm_ref, norm_mate_ref = refs[2 * parts:2 * parts + 4]
    gin_refs, gback_refs = refs[2 * parts + 4:2 * parts + 6], refs[2 * parts + 6:2 * parts + 8]
    w_in, w_back, out_acc, norm_acc = refs[2 * parts + 8:]
    step = pl.program_id(0)
    f32, bf16 = jnp.float32, jnp.bfloat16
    NT = (((1,), (1,)), ((), ()))
    TN = (((0,), (0,)), ((), ()))

    @pl.when(step == 0)
    def _():
        out_acc[...] = jnp.zeros(out_acc.shape, f32)
        norm_acc[...] = jnp.zeros(norm_acc.shape, f32)

    for q in range(parts):
        @pl.when(step // per_part == q)
        def _():
            w_in[...] = in_refs[q][...]
            w_back[...] = back_refs[q][...]

    rows = n_ref.shape[0]
    inner = lax.dot_general(n_ref[...], w_in[...], NT, preferred_element_type=f32)
    cube = inner * inner * 0.044715
    th = jnp.tanh(ROOT * inner * (1.0 + cube))
    half = 0.5 * (1.0 + th)
    active = (inner * half).astype(bf16)
    slope = half + (0.5 * ROOT) * inner * (1.0 - th * th) * (1.0 + 3.0 * cube)
    grad = (lax.dot_general(c_ref[...], w_back[...], NT, preferred_element_type=f32) * slope).astype(bf16)
    norm_acc[...] += jnp.dot(grad, w_in[...], preferred_element_type=f32)
    out_acc[...] += jnp.dot(active, w_back[...], preferred_element_type=f32)
    gin = lax.dot_general(grad, n_ref[...], TN, preferred_element_type=f32).astype(bf16)
    gback = lax.dot_general(active, c_ref[...], TN, preferred_element_type=f32).astype(bf16)
    part = step // per_part
    for grad_refs, value, sent in ((gin_refs, gin, in_sent), (gback_refs, gback, back_sent)):
        leaves = functools.reduce(jnp.logical_or, [part == q for q in sent], False)

        @pl.when(leaves)
        def _():
            grad_refs[1][...] = value

        @pl.when(jnp.logical_not(leaves))
        def _():
            grad_refs[0][...] = value

    @pl.when(step == pl.num_programs(0) - 1)
    def _():
        own = out_ref.shape[0]
        out_ref[...] = out_acc[:own, :]
        out_mate_ref[...] = out_acc[own:, :].astype(bf16)
        norm_ref[...] = norm_acc[:own, :]
        norm_mate_ref[...] = norm_acc[own:, :].astype(bf16)


def ffn(normed, cot, in_parts, back_parts, in_sent, back_sent):
    parts = len(in_parts)
    units, width = in_parts[0].shape
    rows = normed.shape[0]
    chunk = min(CHUNK, units)
    per_part = units // chunk
    once = lambda shape: pl.BlockSpec(shape, lambda i: (0, 0), pipeline_mode=pl.Buffered(1))
    piece = lambda q: pl.BlockSpec((chunk, width), lambda i: (jnp.clip(i - q * per_part, 0, per_part - 1), 0))
    weights = [piece(q) for q in range(parts)]
    sums = [jax.ShapeDtypeStruct((rows // 2, width), kind) for kind in (jnp.float32, jnp.bfloat16)]
    grads, grad_specs = [], []
    for sent in (in_sent, back_sent):
        for members in ([q for q in range(parts) if q not in sent], list(sent)):
            steps = [q * per_part + n for q in members for n in range(per_part)]
            index = lambda i, ups=tuple(steps[1:]): (sum([(i >= up).astype(jnp.int32) for up in ups], jnp.int32(0)), 0)
            grads.append(jax.ShapeDtypeStruct((len(members) * units, width), jnp.bfloat16))
            grad_specs.append(pl.BlockSpec((chunk, width), index))
    return pl.pallas_call(
        functools.partial(ffn_kernel, parts, per_part, in_sent, back_sent),
        grid=(parts * per_part,),
        out_shape=sums * 2 + grads,
        in_specs=[once((rows, width)), once((rows, width))] + weights * 2,
        out_specs=[once((rows // 2, width))] * 4 + grad_specs,
        scratch_shapes=[pltpu.VMEM((chunk, width), jnp.bfloat16)] * 2 + [pltpu.VMEM((rows, width), jnp.float32)] * 2,
        compiler_params=pltpu.CompilerParams(dimension_semantics=("arbitrary",), vmem_limit_bytes=60 << 20),
        cost_estimate=pl.CostEstimate(flops=int(35e9), transcendentals=0, bytes_accessed=16 << 20),
        name="ffn",
    )(normed, cot, *in_parts, *back_parts)


def over_rows(left_side, right_side):
    return lax.dot_general(
        left_side, right_side, (((0,), (0,)), ((), ())), preferred_element_type=jnp.float32
    )


def against(left_side, right_side):
    return lax.dot_general(
        left_side, right_side, (((1,), (1,)), ((), ())), preferred_element_type=jnp.float32
    )


def matmul(left_side, right_side):
    return jnp.dot(left_side, right_side, preferred_element_type=jnp.float32)


def norm_back(grad_normed, unit_rows, inv_scale, gain_row):
    scaled = grad_normed * gain_row
    return inv_scale * (scaled - unit_rows * jnp.mean(scaled * unit_rows, axis=-1, keepdims=True))


def low(values_in):
    return values_in.astype(jnp.bfloat16)


def wide(values_in):
    return values_in.astype(jnp.float32)


def bits_of(size):
    return [1 << n for n in range(size.bit_length() - 1)]


def tie(*values):
    return lax.optimization_barrier(values)


def finish(steps):
    for step in steps:
        last = step
    return last


def send_or_none(steps, value):
    try:
        return steps.send(value)
    except StopIteration:
        return None


class Slice:
    def __init__(self, mesh):
        self.dp, self.group, self.tensor = (mesh.shape[name] for name in ("dp", "group", "tensor"))

    def swap(self, array, axis, mask):
        size = getattr(self, axis)
        return lax.ppermute(array, axis, [(i, i ^ mask) for i in range(size)])

    def pair_swap(self, array):
        return self.swap(array, "group", 1)

    def row_steps(self):
        return [("group", 2 * bit) for bit in bits_of(self.group // 2)]

    def col_steps(self):
        return [("dp", bit) for bit in bits_of(self.dp)]

    def spread(self, block):
        have = {(0, 0): block}
        size = self.dp * self.group
        for col in range(self.dp):
            for row in range(self.group // 2):
                mask = col * self.group + 2 * row
                if mask:
                    have[col, row] = lax.ppermute(block, ("dp", "group"), [(i, i ^ mask) for i in range(size)])
        return have

    def collect_order(self, rows_first):
        steps = self.row_steps() + self.col_steps() if rows_first else self.col_steps() + self.row_steps()
        return list(reversed(steps))

    def sent_first(self, keys, rows_first):
        return self.sent_first_of(keys, self.collect_order(rows_first)[0])

    def collect(self, keys, kept, sent, rows_first):
        order = self.collect_order(rows_first)
        leaves = self.sent_first(keys, rows_first)
        keys = [key for n, key in enumerate(keys) if n not in leaves]
        units = kept.shape[0] // len(keys)
        for n, (axis, mask) in enumerate(order):
            other = yield self.swap(sent, axis, mask)
            total = low(wide(kept) + wide(other))
            if n + 1 < len(order):
                leaves = self.sent_first_of(keys, order[n + 1])
                block = lambda k: total[k * units:(k + 1) * units]
                pick = lambda ks: block(ks[0]) if len(ks) == 1 else jnp.concatenate([block(k) for k in ks], axis=0)
                kept, sent = pick([k for k in range(len(keys)) if k not in leaves]), pick(list(leaves))
                keys = [key for k, key in enumerate(keys) if k not in leaves]
        yield total

    def sent_first_of(self, keys, step):
        axis, mask = step
        return tuple(n for n, (col, row) in enumerate(keys) if (row & mask // 2 if axis == "group" else col & mask))

    def slot(self):
        rows = self.group // 2
        group = lax.axis_index("group")
        return (group % 2) * (self.dp * rows) + lax.axis_index("dp") * rows + group // 2

    def slot_gather(self, block):
        for axis, mask in self.row_steps() + self.col_steps() + [("group", 1)]:
            upper = (lax.axis_index(axis) // mask) % 2 == 1
            other = self.swap(block, axis, mask)
            yield other
            block = jnp.concatenate((jnp.where(upper, other, block), jnp.where(upper, block, other)), axis=2)
        yield block.reshape(block.shape[0], -1, block.shape[3])

    def plane_sum(self, grad, others):
        mine = lax.axis_index("dp")
        for axis, mask in reversed(self.col_steps()):
            half = grad.shape[0] // 2
            bit = (mine // mask) % 2
            keep = lax.dynamic_slice_in_dim(grad, bit * half, half, 0)
            send = lax.dynamic_slice_in_dim(grad, (1 - bit) * half, half, 0)
            other = self.swap(send, axis, mask)
            grad = low(wide(keep) + wide(other))
        for axis, mask in self.row_steps() + [("group", 1)]:
            other = self.swap(grad, axis, mask)
            if axis == "group" and mask == 2:
                other, others = tie(other, others)
            grad = low(wide(grad) + wide(other))
        return grad[0], others

    def tensor_parts(self, vector):
        return [vector] + [self.swap(vector, "tensor", mask) for mask in range(1, self.tensor)]

    def tensor_total(self, parts):
        while len(parts) > 1:
            parts = [one + two for one, two in zip(parts[::2], parts[1::2])]
        return parts[0]

    def col_exchange(self, blocks):
        mine = lax.axis_index("dp")
        for axis, mask in reversed(self.col_steps()):
            half = blocks.shape[3] // 2
            upper = (mine // mask) % 2 == 1
            low_half, high_half = blocks[..., :half], blocks[..., half:]
            keep = jnp.where(upper, high_half, low_half)
            other = self.swap(jnp.where(upper, low_half, high_half), axis, mask)
            pair = jnp.where(upper, jnp.stack((other, keep), axis=1), jnp.stack((keep, other), axis=1))
            blocks = pair.reshape((pair.shape[0], -1) + pair.shape[3:])
        if self.dp > 2:
            count, bits = blocks.shape[0], self.dp.bit_length() - 1
            split = blocks.reshape((count,) + (2,) * bits + blocks.shape[2:])
            split = split.transpose((0,) + tuple(range(bits, 0, -1)) + (bits + 1, bits + 2))
            blocks = split.reshape(blocks.shape)
        return blocks

    def group_gather(self, block):
        block = block[None]
        for mask in reversed(bits_of(self.group)):
            upper = (lax.axis_index("group") // mask) % 2 == 1
            other = self.swap(block, "group", mask)
            block = jnp.where(upper, jnp.stack((other, block), axis=1), jnp.stack((block, other), axis=1))
            block = block.reshape((-1,) + block.shape[2:])
        return block

    def col_exchange_rows(self, rows):
        return self.col_exchange(rows[None, None])[0]


def on_device(
    sl,
    inputs,
    segments,
    gain_attn,
    w_query,
    w_key,
    w_value,
    w_out,
    bias_table,
    gain_ffn,
    w_in,
    w_back,
    cotangent,
):
    heads_here = bias_table.shape[1]
    width = inputs.shape[1]
    pairs = heads_here // PAIR
    cols = PAIR * 64
    dp_index, group_index = lax.axis_index("dp"), lax.axis_index("group")
    segment_row = segments.reshape(-1)
    lo, hi = block_bounds(segment_row)
    tiles = bias_tiles(bias_table)

    stream = wide(inputs)
    inv_attn = lax.rsqrt(jnp.mean(stream * stream, axis=-1, keepdims=True) + EPSILON)
    unit_attn = stream * inv_attn
    rows = stream.shape[0]
    units_g = w_back.shape[0] // sl.group
    units = units_g // sl.dp
    start = group_index * units_g + dp_index * units
    plane = sl.dp * sl.group
    slot = sl.slot()
    qkv = [jnp.concatenate([w[:, k * cols:(k + 1) * cols] for w in (w_query, w_key, w_value)], axis=1) for k in range(pairs)]
    n_out, n_qkv = w_out.shape[0] // plane, 3 * cols // plane
    own_in = [lax.dynamic_slice_in_dim(w_in, start, units, 1).T]
    own_in.append(lax.dynamic_slice_in_dim(w_out, slot * n_out, n_out, 0))
    own_in = jnp.concatenate(own_in, axis=0)
    own_back = lax.dynamic_slice_in_dim(w_back, start, units, 0)
    own_qkv = jnp.concatenate([lax.dynamic_slice_in_dim(qkv[k], slot * n_qkv, n_qkv, 1).T for k in range(pairs)], axis=0)
    cot_pair = jnp.concatenate((cotangent, sl.pair_swap(cotangent)), axis=0)
    prep = (tiles, padded_weights(w_query, w_key, w_value, heads_here), operands(segment_row), cot_pair, pad_heads(w_value, heads_here, 128))
    by_pair = lambda block, rows: block.reshape(sl.tensor, pairs, rows, width).transpose(1, 0, 2, 3)
    in_z = lax.all_gather(own_in, "tensor", axis=0, tiled=False)
    own_normed, in_z = tie(low(unit_attn * gain_attn), in_z)
    normed = lax.all_gather(own_normed, "tensor", axis=0, tiled=True)
    in_parts = sl.spread(in_z[:, :units].reshape(-1, width))
    out_full = finish(sl.slot_gather(in_z[:, units:][None]))[0]
    n_rows = own_qkv.shape[0]
    own_qkv = jnp.pad(own_qkv, ((0, -n_rows % 128), (0, 0)))
    own_back, normed, prep, in_parts, qkv, out_full, own_qkv = tie(own_back, normed, prep, in_parts, qkv, out_full, own_qkv)
    tiles, padded, ext, cot_pair, w_vx = prep
    back_z = lax.all_gather(own_back, "tensor", axis=0, tiled=True)

    qx, kx, vt = project(normed, padded, ext, heads_here)
    ctx_t, lse = attn_fwd(lo, hi, bias_table, qx, kx, vt, tiles)
    back_z, ctx_t, own_qkv = tie(back_z, ctx_t, own_qkv)
    qkv_z = lax.all_gather(own_qkv, "tensor", axis=0, tiled=False)[:, :n_rows]
    back_parts = sl.spread(back_z)
    ctx_rows = lax.all_to_all(ctx_t, "tensor", split_axis=1, concat_axis=0, tiled=True)
    hidden = stream + over_rows(ctx_rows, out_full)
    inv_ffn = lax.rsqrt(jnp.mean(hidden * hidden, axis=-1, keepdims=True) + EPSILON)
    unit_ffn = hidden * inv_ffn

    normed_ffn, qkv_z, back_parts = tie(low(unit_ffn * gain_ffn), qkv_z, back_parts)
    qkv_all = lax.all_gather(qkv_z, ("dp", "group"), axis=0, tiled=False)
    normed_pair = jnp.concatenate((normed_ffn, sl.pair_swap(normed_ffn)), axis=0)
    keys = sorted(in_parts)
    results = ffn(
        normed_pair, cot_pair, [in_parts[key] for key in keys], [back_parts[key] for key in keys],
        sl.sent_first(keys, True), sl.sent_first(keys, False),
    )
    out_own, out_mate, normed_own, normed_mate = results[:4]
    in_steps, back_steps = sl.collect(keys, *results[4:6], True), sl.collect(keys, *results[6:8], False)
    normed_own, qkv_all = tie(normed_own, qkv_all)
    grad_normed_ffn = normed_own + wide(sl.pair_swap(normed_mate))
    output = hidden + out_own + wide(sl.pair_swap(out_mate))

    gain_ffn_part = jnp.sum(grad_normed_ffn * unit_ffn, axis=0)
    grad_hidden = wide(cotangent) + norm_back(grad_normed_ffn, unit_ffn, inv_ffn, gain_ffn)
    grad_hidden_low = low(grad_hidden)
    grad_ctx = low(against(out_full, grad_hidden_low))
    grad_hidden_late, grad_ctx, normed = tie(grad_hidden_low, grad_ctx, normed)
    vx, kt = project_back(normed, w_vx, w_key)
    grad_ctx_t = lax.all_to_all(grad_ctx, "tensor", split_axis=0, concat_axis=1, tiled=True)

    grad_w_out = low(matmul(ctx_rows, grad_hidden_late)).reshape(sl.tensor, sl.group, -1, width)

    def out_scatter(grad):
        grad = grad.reshape((sl.tensor, -1, 2) + grad.shape[2:])
        bit = group_index % 2
        keep = lax.dynamic_index_in_dim(grad, bit, 2, keepdims=False)
        other = yield sl.pair_swap(lax.dynamic_index_in_dim(grad, 1 - bit, 2, keepdims=False))
        grad = low(wide(keep) + wide(other))
        grad = grad.reshape(sl.tensor, sl.group // 2 * sl.dp, -1, width)
        size = sl.dp * sl.group
        block = lambda col, row: lax.dynamic_index_in_dim(grad, ((group_index // 2) ^ row) * sl.dp + (dp_index ^ col), 1, keepdims=False)
        keys = [(col, row) for col in range(sl.dp) for row in range(sl.group // 2)]
        masks = {key: key[0] * sl.group + 2 * key[1] for key in keys}
        others = yield [
            lax.ppermute(block(*key), ("dp", "group"), [(i, i ^ masks[key]) for i in range(size)]) for key in keys[1:]
        ]
        yield low(sum((wide(part) for part in others), wide(block(0, 0))))

    out_steps = out_scatter(grad_w_out)
    first, grad_ctx_t, vx, kt = tie((next(in_steps), next(back_steps), next(out_steps)), grad_ctx_t, vx, kt)
    second = [steps.send(other) for steps, other in zip((in_steps, back_steps, out_steps), first)]
    tables, grad_parts, grad_rows = [], [], []
    for k in range(pairs):
        lo_k = lo
        if k == pairs - 1:
            own_sums = []
            if k > 0:
                second, grad_parts[-1] = tie(second, grad_parts[-1])
            for steps, last in zip((in_steps, back_steps, out_steps), second):
                for other in iter(lambda: send_or_none(steps, last), None):
                    last = other
                own_sums.append(last)
            own_sums = jnp.concatenate([part.reshape(sl.tensor, -1, width) for part in own_sums], axis=1)
            lo_k, own_sums = tie(lo, own_sums)
            own_rows = own_sums.shape[1]
            summed = lax.psum_scatter(own_sums.reshape(-1, width), "tensor", scatter_dimension=0, tiled=True)
        grads, diag = attn_bwd(k, lo_k, hi, bias_table, qx, kx, vx, kt, grad_ctx_t, ctx_t, lse, tiles)
        grad_parts.append(grads)
        if k > 0:
            grads, diag, grad_rows[k - 1] = tie(grads, diag, grad_rows[k - 1])
        grad_rows.append(lax.all_to_all(grads, "tensor", split_axis=0, concat_axis=1, tiled=True))
        tables.append(table_grad(diag, PAIR))

    summed = sl.col_exchange_rows(summed)
    grad_parts = tie(*grad_parts)
    gain_dot, grad_w_qkv = 0.0, []
    for k in range(pairs):
        grad_w = over_rows(normed, grad_parts[k])
        gain_dot = gain_dot + jnp.sum(grad_w * wide(qkv[k]), axis=1)
        grad_w_qkv.append(low(grad_w))

    columns = pairs * 3 * cols
    small = jnp.concatenate([gain_dot / gain_attn, gain_ffn_part] + [table.T.reshape(-1) for table in tables])
    small_rows = -(-small.shape[0] // columns)
    small = low(jnp.pad(small, (0, small_rows * columns - small.shape[0]))).reshape(1, small_rows, columns)
    grad_w_qkv = jnp.concatenate(grad_w_qkv, axis=1).reshape(sl.dp, -1, columns)
    grad_w_qkv = jnp.concatenate((grad_w_qkv, jnp.tile(small, (sl.dp, 1, 1))), axis=1)
    grad_w_qkv, (grad_rows, summed) = sl.plane_sum(grad_w_qkv, (grad_rows, summed))
    small = grad_w_qkv[-small_rows:].reshape(-1)
    grad_w_qkv = wide(grad_w_qkv[:-small_rows])
    gain_parts = sl.tensor_parts(wide(small[:2 * width]))
    table_rows = bias_table.shape[0] // sl.dp
    grad_table = wide(small[2 * width:2 * width + bias_table.size]).reshape(heads_here, -1)
    grad_table = lax.dynamic_slice_in_dim(grad_table, dp_index * table_rows, table_rows, 1).T

    everything = sl.group_gather(summed)
    cuts = [0, units, 2 * units, own_rows]
    pick = lambda n: wide(everything[:, :, cuts[n]:cuts[n + 1]].reshape(-1, width // sl.dp))
    grad_w_in, grad_w_back, grad_w_out = pick(0).T, pick(1), pick(2)
    qkv_all = qkv_all.reshape(sl.dp, sl.group // 2, 2, sl.tensor, pairs, n_qkv, width).transpose(4, 3, 2, 0, 1, 5, 6)
    qkv_full = qkv_all.reshape(pairs, -1, width)
    grad_normed = 0.0
    for k in range(pairs):
        grad_normed = grad_normed + matmul(grad_rows[k], qkv_full[k])
    grad_inputs = grad_hidden + norm_back(grad_normed, unit_attn, inv_attn, gain_attn)
    grad_w_query, grad_w_key, grad_w_value = (
        jnp.concatenate([grad_w_qkv[:, (3 * k + n) * cols:(3 * k + n + 1) * cols] for k in range(pairs)], axis=1) for n in range(3)
    )
    weight_grads = (grad_w_query, grad_w_key, grad_w_value, grad_w_out, grad_w_in, grad_w_back)
    gain_parts, weight_grads = tie(gain_parts, weight_grads)
    grad_w_query, grad_w_key, grad_w_value, grad_w_out, grad_w_in, grad_w_back = weight_grads
    gain_grads = sl.tensor_total(gain_parts)
    return (
        output,
        grad_inputs,
        gain_grads[:width],
        grad_w_query,
        grad_w_key,
        grad_w_value,
        grad_w_out,
        grad_table,
        gain_grads[width:],
        grad_w_in,
        grad_w_back,
    )


def solution(mesh):
    return jax.shard_map(
        functools.partial(on_device, Slice(mesh)),
        mesh=mesh,
        in_specs=(
            P(("dp", "group", "tensor"), None),
            P(("dp", "group"), None),
            P(),
            P(None, "tensor"),
            P(None, "tensor"),
            P(None, "tensor"),
            P("tensor", None),
            P(None, "tensor"),
            P(),
            P(None, "tensor"),
            P("tensor", None),
            P(("dp", "group", "tensor"), None),
        ),
        out_specs=(
            P(("dp", "group", "tensor"), None),
            P(("dp", "group", "tensor"), None),
            P(),
            P("dp", "tensor"),
            P("dp", "tensor"),
            P("dp", "tensor"),
            P("tensor", "dp"),
            P("dp", "tensor"),
            P(),
            P("dp", "tensor"),
            P("tensor", "dp"),
        ),
        check_vma=False,
    )
```
